32 devices in a mesh: groups: 2 (over y), space: 4 (over z), dp: 2 (over x), rep: 2 (over core).
Axes of the slice: x: 2, y: 2, z: 4, core: 2. Of those that a mesh axis runs over, the one named last changes fastest.
Arguments:
- volumes: bfloat16 [8, 16, 24, 24, 128], P(('groups', 'dp', 'rep'), 'space'), parts along dimension 0, may hold values from -6 to 6
- targets: float32 [8, 4], P(('groups', 'dp', 'rep')), parts along dimension 0, may hold values from -4 to 4
- first_kernel: bfloat16 [3456, 128], replicated, may hold values from -0.109375 to 0.109375
- second_kernel: bfloat16 [3456, 256], P(None, 'space'), may hold values from -0.109375 to 0.109375
- head_weights: float32 [256, 4], replicated, may hold values from -0.375 to 0.375
Outputs:
- grad_first: float32 [6912, 128], P('groups'), parts along dimension 0
- grad_second: float32 [6912, 256], P('groups', 'space'), parts along dimension 0
- grad_head: float32 [512, 4], P(('groups', 'space')), parts along dimension 0
The draws below stay inside these ranges and needn't reach their ends.
There are 2 independent parts, one for each index of `groups`. The reference program is written for one: setup_inputs(seed, part) draws one part's arguments, and reference() takes and returns one part's arrays. A program takes and returns all parts, laid end to end along the dimension named above; an argument that names none is the same for every part. Nothing has to cross between parts.
All inputs are finite; a program needn't handle non-finite values.
Results may differ from the reference program's by a relative error of at most 0.0038.
Values may be sent and summed in bfloat16 or wider, within the bound.
No kernel may reach another device: no remote copies, remote signals or barrier semaphores. Data moves between devices by JAX's collectives and lax.ppermute only.
A program may use at most 128 MiB of HBM per device.

```python
import jax
import jax.numpy as jnp
from jax import lax

C1 = 128
C2 = 256
HW = 24
OUTS = 4
DEPTH = 16
VOLS = 4


def level_of(stream_key, extent, cuts, least, high):
    factor_of = 1.0
    for position, shards_of in cuts:
        draws = jax.random.uniform(jax.random.fold_in(jax.random.fold_in(stream_key, 6), position), (shards_of,), jnp.float32, least / len(cuts), high / len(cuts))
        factor_of = factor_of * jnp.repeat(jnp.exp(draws), extent[position] // shards_of).reshape((-1,) + (1,) * (len(extent) - 1 - position))
    return factor_of


def scatter_about(rng, shape, deviation, limit, split=(), held_as=jnp.bfloat16):
    entries = jax.random.normal(rng, shape, jnp.float32) * deviation
    if len(split) > 0:
        entries = level_of(rng, shape, split, -0.22, 0.18) * entries
    return jnp.clip(entries, min=-limit, max=limit).astype(held_as)


def setup_inputs(seed: int = 0, part: int = 0) -> dict:
    arg_keys = jax.random.split(jax.random.key(seed), 6)
    part_splits = jax.random.split(jax.random.fold_in(arg_keys[5], part), 6)
    volumes = scatter_about(part_splits[0], (VOLS, DEPTH, HW, HW, C1), 1.0, 6.0, ((0, 4), (1, 4)))
    targets = scatter_about(part_splits[1], (VOLS, OUTS), 1.0, 4.0, ((0, 4),), jnp.float32)
    first_kernel = scatter_about(arg_keys[2], (27 * C1, C1), (27 * C1) ** -0.5, 0.109375)
    second_kernel = scatter_about(arg_keys[3], (27 * C1, C2), (27 * C1) ** -0.5, 0.109375, ((1, 4),))
    head_weights = scatter_about(arg_keys[4], (C2, OUTS), C2 ** -0.5, 0.375, (), jnp.float32)
    return {"volumes": volumes, "targets": targets, "first_kernel": first_kernel, "second_kernel": second_kernel, "head_weights": head_weights}


leak_slope = 0.3
log_two = 0.6931471805599453

def activate(value):
    return leak_slope * value + (1.0 - leak_slope) * (jax.nn.softplus(value) - log_two)

def activate_slope(value):
    return leak_slope + (1.0 - leak_slope) * jax.nn.sigmoid(value)

def convolve(grid, kernel):
    result = lax.conv_general_dilated(grid[None], kernel, (1, 1, 1), [(1, 1), (1, 1), (1, 1)], dimension_numbers=('NDHWC', 'DHWIO', 'NDHWC'), precision=lax.Precision.HIGHEST)
    return result[0]

def pooling(grid):
    depth, rows, cols, chans = grid.shape
    return grid.reshape(depth // 2, 2, rows // 2, 2, cols // 2, 2, chans).mean(axis=(1, 3, 5))

def expand(grid):
    depth, rows, cols, chans = grid.shape
    spread = jnp.broadcast_to(grid[:, None, :, None, :, None, :], (depth, 2, rows, 2, cols, 2, chans))
    return spread.reshape(depth * 2, rows * 2, cols * 2, chans) / 8.0

def kernel_grad(grid, grad):
    depth, rows, cols, chans = grid.shape
    padded = jnp.pad(grid, ((1, 1), (1, 1), (1, 1), (0, 0)))
    flat_grad = grad.reshape(-1, grad.shape[-1])
    blocks = []
    for tap_depth in range(3):
        for tap_row in range(3):
            for tap_col in range(3):
                window = padded[tap_depth:tap_depth + depth, tap_row:tap_row + rows, tap_col:tap_col + cols, :]
                blocks.append(jnp.dot(window.reshape(-1, chans).T, flat_grad, precision=lax.Precision.HIGHEST))
    return jnp.concatenate(blocks, axis=0)

def reference(volumes, targets, first_kernel, second_kernel, head_weights):
    channels = first_kernel.shape[0] // 27
    kernel_one = first_kernel.astype(jnp.float32).reshape(3, 3, 3, channels, first_kernel.shape[1])
    kernel_two = second_kernel.astype(jnp.float32).reshape(3, 3, 3, channels, second_kernel.shape[1])
    flipped = jnp.swapaxes(kernel_two[::-1, ::-1, ::-1], 3, 4)

    def one_volume(totals, inputs):
        grid_in, target_row = inputs
        wide_in = grid_in.astype(jnp.float32)
        before_one = convolve(wide_in, kernel_one)
        pooled = pooling(activate(before_one)).astype(jnp.bfloat16)
        pooled_wide = lax.optimization_barrier(pooled).astype(jnp.float32)
        before_two = convolve(pooled_wide, kernel_two)
        feature = lax.optimization_barrier(jnp.mean(activate(before_two), axis=(0, 1, 2)))
        predicted = jnp.dot(feature, head_weights, precision=lax.Precision.HIGHEST)
        error = predicted - target_row
        head_part = feature[:, None] * error[None, :]
        feature_grad = jnp.dot(head_weights, error, precision=lax.Precision.HIGHEST)
        grad_two = (feature_grad * activate_slope(before_two)).astype(jnp.bfloat16)
        grad_two_wide = lax.optimization_barrier(grad_two).astype(jnp.float32)
        second_part = kernel_grad(pooled_wide, grad_two_wide)
        pooled_grad = convolve(grad_two_wide, flipped)
        grad_one = (expand(pooled_grad) * activate_slope(before_one)).astype(jnp.bfloat16)
        grad_one_wide = lax.optimization_barrier(grad_one).astype(jnp.float32)
        first_part = kernel_grad(wide_in, grad_one_wide)
        return ((totals[0] + first_part, totals[1] + second_part, totals[2] + head_part), None)
    start = (jnp.zeros(first_kernel.shape, jnp.float32), jnp.zeros(second_kernel.shape, jnp.float32), jnp.zeros(head_weights.shape, jnp.float32))
    totals, unused = lax.scan(one_volume, start, (volumes, targets))
    return (totals[0], totals[1], totals[2])
```

```python
import jax
import jax.numpy as jnp
from jax import lax
from jax.sharding import PartitionSpec as P

leak_slope = 0.3
log_two = 0.6931471805599453
direct_most = 4


def swap(x, axis, bits):
    return lax.ppermute(x, axis, [(i, i ^ bits) for i in range(lax.axis_size(axis))])


def direct(axis):
    return lax.axis_size(axis) <= direct_most


def gathered(x, axis):
    if not direct(axis):
        return lax.all_gather(x, axis)
    size, place = lax.axis_size(axis), lax.axis_index(axis)
    parts = [x] + [swap(x, axis, bits) for bits in range(1, size)]
    out = jnp.zeros((size,) + x.shape, x.dtype)
    for bits, part in enumerate(parts):
        out = lax.dynamic_update_index_in_dim(out, part, place ^ bits, 0)
    return out


def scattered_sum(x, axis, wire):
    size, place = lax.axis_size(axis), lax.axis_index(axis)
    blocks = x.reshape((size, x.shape[0] // size) + x.shape[1:])
    if not direct(axis):
        return lax.psum_scatter(blocks, axis)
    total = lax.dynamic_index_in_dim(blocks, place, 0, False)
    for bits in range(1, size):
        sent = lax.dynamic_index_in_dim(blocks, place ^ bits, 0, False).astype(wire)
        total = total + swap(sent, axis, bits).astype(jnp.float32)
    return total


def total_first(x):
    columns = x.shape[1]
    x = scattered_sum(x, "rep", jnp.float32)
    x = scattered_sum(x, "dp", jnp.bfloat16)
    if direct("space"):
        x = scattered_sum(x, "space", jnp.bfloat16).astype(jnp.bfloat16)
        x = gathered(x, "space").reshape(-1, columns)
    else:
        x = lax.psum(x, "space").astype(jnp.bfloat16)
    x = gathered(x, "dp").reshape(-1, columns)
    x = gathered(x, "rep").reshape(-1, columns)
    return x.astype(jnp.float32)


def total_second(x):
    columns = x.shape[1]
    x = scattered_sum(x, "rep", jnp.float32)
    if direct("dp"):
        x = gathered(x.astype(jnp.bfloat16), "dp").astype(jnp.float32).sum(0)
    else:
        x = lax.psum(x, "dp")
    return gathered(x, "rep").reshape(-1, columns)


def whole_kernel(part):
    rows, share = part.shape
    copies = [axis for axis in ("dp", "rep")]
    pieces, place = (1, 0)
    for axis in copies:
        place = place * lax.axis_size(axis) + lax.axis_index(axis)
        pieces = pieces * lax.axis_size(axis)
    length = rows // pieces
    piece = lax.dynamic_slice_in_dim(part, place * length, length, 0)
    packed = jnp.concatenate([piece[: length // 2], piece[length // 2 :]], axis=1)
    packs = gathered(packed, "space")
    upper = jnp.moveaxis(packs[:, :, :share], 0, 1).reshape(length // 2, -1)
    lower = jnp.moveaxis(packs[:, :, share:], 0, 1).reshape(length // 2, -1)
    wide = jnp.concatenate([upper, lower], axis=0)
    wide = gathered(wide, "dp")
    wide = jnp.moveaxis(gathered(wide, "rep"), 0, 1)
    return wide.reshape(rows, -1)


def extended_2(x, sides, width):
    for axis, dim in sides:
        devices, length = (lax.axis_size(axis), x.shape[dim])
        up = [(i, (i + 1) % devices) for i in range(devices - 1)]
        down = [(j, i) for i, j in up]
        last = lax.slice_in_dim(x, length - width, length, axis=dim)
        leading = lax.slice_in_dim(x, 0, width, axis=dim)
        before = lax.ppermute(last, axis, up)
        after = lax.ppermute(leading, axis, down)
        x = jnp.concatenate([before, x, after], axis=dim)
    return x


def activate(value):
    return leak_slope * value + (1.0 - leak_slope) * (jax.nn.softplus(value) - log_two)


def activate_slope(value):
    return leak_slope + (1.0 - leak_slope) * jax.nn.sigmoid(value)


def convolve(extended, kernel):
    result = lax.conv_general_dilated(
        extended[None],
        kernel,
        (1, 1, 1),
        [(0, 0), (1, 1), (1, 1)],
        dimension_numbers=("NDHWC", "DHWIO", "NDHWC"),
        preferred_element_type=jnp.float32,
    )
    return result[0]


def pooling(grid):
    depth, rows, cols, chans = grid.shape
    return grid.reshape(depth // 2, 2, rows // 2, 2, cols // 2, 2, chans).mean(axis=(1, 3, 5))


def expand(grid):
    depth, rows, cols, chans = grid.shape
    spread = jnp.broadcast_to(
        grid[:, None, :, None, :, None, :], (depth, 2, rows, 2, cols, 2, chans)
    )
    return spread.reshape(depth * 2, rows * 2, cols * 2, chans) / 8.0


def kernel_grad(extended, grad):
    widened = jnp.pad(extended, ((0, 0), (1, 1), (1, 1), (0, 0)))
    result = lax.conv_general_dilated(
        widened[..., None],
        grad[:, :, :, None, :],
        (1, 1, 1),
        "VALID",
        dimension_numbers=("DHWNC", "DHWIO", "NDHWC"),
        preferred_element_type=jnp.float32,
    )
    return jnp.transpose(result, (1, 2, 3, 0, 4)).reshape(-1, grad.shape[-1])


def shards(volumes, targets, first_kernel, second_kernel, head_weights):
    grid_in = volumes[0]
    target_row = targets[0]
    channels = grid_in.shape[-1]
    kernel_one = first_kernel.reshape(3, 3, 3, channels, first_kernel.shape[1])
    extended = extended_2(grid_in, (("space", 0),), 1)
    share = second_kernel.shape[1]
    place = lax.axis_index("space")
    kernel_two = whole_kernel(second_kernel).reshape(3, 3, 3, channels, -1)
    before_one = convolve(extended, kernel_one)
    pooled = pooling(activate(before_one)).astype(jnp.bfloat16)
    whole = gathered(pooled, "space").reshape((-1,) + pooled.shape[1:])
    padded_whole = jnp.pad(whole, ((1, 1), (0, 0), (0, 0), (0, 0)))
    before_two = convolve(padded_whole, kernel_two)
    feature = jnp.mean(activate(before_two), axis=(0, 1, 2))
    predicted = jnp.dot(feature, head_weights, precision=lax.Precision.HIGHEST)
    error = predicted - target_row
    feature_part = lax.dynamic_slice_in_dim(feature, place * share, share, 0)
    head_grad = feature_part[:, None] * error[None, :]
    feature_grad = jnp.dot(head_weights, error, precision=lax.Precision.HIGHEST)
    grad_two = (feature_grad * activate_slope(before_two)).astype(jnp.bfloat16)
    padded_grad = jnp.pad(grad_two, ((1, 1), (0, 0), (0, 0), (0, 0)))
    flipped = jnp.swapaxes(kernel_two[::-1, ::-1, ::-1], 3, 4)
    planes = pooled.shape[0]
    window = lax.dynamic_slice_in_dim(padded_grad, place * planes, planes + 2, 0)
    pooled_grad = convolve(window, flipped)
    grad_one = (expand(pooled_grad) * activate_slope(before_one)).astype(jnp.bfloat16)
    first_total = total_first(kernel_grad(extended, grad_one))
    grad_part = lax.dynamic_slice_in_dim(grad_two, place * share, share, 3)
    second_part = kernel_grad(padded_whole, grad_part)
    rows = second_part.shape[0]
    packed = jnp.concatenate([second_part[: rows // 2], second_part[rows // 2 :]], axis=1)
    packed = total_second(packed)
    second_total = jnp.concatenate([packed[:, :share], packed[:, share:]], axis=0)
    head_total = gathered(gathered(head_grad, "rep").sum(0), "dp").sum(0)
    return (first_total, second_total, head_total)


def solution(mesh):
    in_specs = (
        P(("groups", "dp", "rep"), "space", None, None, None),
        P(("groups", "dp", "rep"), None),
        P(),
        P(None, "space"),
        P(),
    )
    out_specs = (P("groups", None), P("groups", "space"), P(("groups", "space"), None))
    return jax.shard_map(shards, mesh=mesh, in_specs=in_specs, out_specs=out_specs, check_vma=False)
```

```python
import jax
import jax.numpy as jnp
from jax import lax
from jax.experimental import pallas as pl
from jax.experimental.pallas import tpu as pltpu
from jax.sharding import PartitionSpec as P

leak_slope = 0.3
log_two = 0.6931471805599453
direct_most = 4
f32, bf16 = jnp.float32, jnp.bfloat16
front = 8
heavy = 10**9


def call(body, outs, scratch, *args, smem=(), work=0):
    specs = [pl.BlockSpec(memory_space=pltpu.SMEM if k in smem else pltpu.VMEM) for k in range(len(args))]
    return pl.pallas_call(
        body,
        out_shape=outs,
        in_specs=specs,
        out_specs=jax.tree.map(lambda o: pl.BlockSpec(memory_space=pltpu.VMEM), outs),
        scratch_shapes=scratch,
        compiler_params=pltpu.CompilerParams(vmem_limit_bytes=56 * 2**20),
        cost_estimate=pl.CostEstimate(flops=work, bytes_accessed=0, transcendentals=0),
    )(*args)


def slope_and_activation(value):
    shrunk = jnp.exp(-jnp.abs(value))
    inverse = 1.0 / (1.0 + shrunk)
    slope = leak_slope + (1.0 - leak_slope) * jnp.where(value >= 0, inverse, shrunk * inverse)
    soft = jnp.maximum(value, 0.0) + jnp.log(1.0 + shrunk)
    return slope, leak_slope * value + (1.0 - leak_slope) * (soft - log_two)


def shifted(rows_ref, length, step):
    return rows_ref[front + step : front + step + length, :]


def lay_plane(plane, rows_ref, wide):
    rows, cols, chans = plane.shape
    for h in range(rows):
        rows_ref[front + h * wide : front + h * wide + cols, :] = plane[h].astype(f32)


def wide_plane(source, rows_ref, target, top, wide):
    rows, chans = source.shape[0], source.shape[2]
    lay_plane(source, rows_ref, wide)
    for e in range(3):
        target[top : top + rows * wide, e * chans : (e + 1) * chans] = shifted(
            rows_ref, rows * wide, e - 1
        ).astype(bf16)


def first_forward(vol, before, after, kernel, pooled, slope, u, rows_ref, pairs, acc, half, dense):
    depth, rows, cols, chans = vol.shape
    wide = 32
    cells = rows * wide
    outs = kernel.shape[1]
    span = 3 * chans
    rows_ref[...] = jnp.zeros_like(rows_ref)
    edge = jnp.zeros((u.shape[0], wide, span), bf16)
    u[:, 0:wide, :] = edge
    u[:, wide + cells :, :] = edge
    for p in range(depth + 2):
        if p == 0:
            source = before[0]
        elif p == depth + 1:
            source = after[0]
        else:
            source = vol[p - 1]
        wide_plane(source, rows_ref, u.at[p], wide, wide)

    def tap(a, b):
        return kernel[(9 * a + 3 * b) * chans : (9 * a + 3 * b) * chans + span, :]

    for b in range(3):
        pairs[b, 0:span, 0:outs] = tap(1, b)
        pairs[b, 0:span, outs:] = tap(0, b)
        pairs[b, span:, 0:outs] = tap(2, b)
        pairs[b, span:, outs:] = tap(1, b)
    first_taps = jnp.concatenate([tap(0, b) for b in range(3)], axis=0)
    last_taps = jnp.concatenate([tap(2, b) for b in range(3)], axis=0)

    def one_pair(t, carry):
        def window(q, b):
            return u[2 * t + q, b * wide : b * wide + cells, :]

        left = jnp.concatenate([window(0, b) for b in range(3)], axis=1)
        acc[:, 0:outs] = jnp.dot(left, first_taps, preferred_element_type=f32)
        right = jnp.concatenate([window(3, b) for b in range(3)], axis=1)
        acc[:, outs:] = jnp.dot(right, last_taps, preferred_element_type=f32)
        for b in range(3):
            both = jnp.concatenate([window(1, b), window(2, b)], axis=1)
            acc[...] += jnp.dot(both, pairs[b], preferred_element_type=f32)
        for h in range(rows // 2):
            part = acc[h * 2 * wide : (h + 1) * 2 * wide, :]
            slopes, values = slope_and_activation(part)
            slope[2 * t, h * 2 * wide : (h + 1) * 2 * wide, :] = slopes[:, 0:outs]
            slope[2 * t + 1, h * 2 * wide : (h + 1) * 2 * wide, :] = slopes[:, outs:]
            values = values[:, 0:outs] + values[:, outs:]
            half[h * wide : (h + 1) * wide, :] = values[0:wide] + values[wide:]
        for h in range(rows // 2):
            even = half[pl.ds(h * wide, cols // 2, stride=2), :]
            odd = half[pl.ds(h * wide + 1, cols // 2, stride=2), :]
            dense[t, h * (cols // 2) : (h + 1) * (cols // 2), :] = (even + odd) * 0.125
        return carry

    lax.fori_loop(0, depth // 2, one_pair, 0)
    pooled[...] = dense[...].astype(bf16)


def run_first_forward(vol, before, after, kernel):
    depth, rows, cols, chans = vol.shape
    wide, outs = 32, kernel.shape[1]
    cells = rows * wide
    return call(
        first_forward,
        (
            jax.ShapeDtypeStruct((depth // 2, rows * cols // 4, outs), bf16),
            jax.ShapeDtypeStruct((depth, cells, outs), f32),
        ),
        [
            pltpu.VMEM((depth + 2, cells + 2 * wide, 3 * chans), bf16),
            pltpu.VMEM((cells + 2 * front, chans), f32),
            pltpu.VMEM((3, 6 * chans, 2 * outs), bf16),
            pltpu.VMEM((cells, 2 * outs), f32),
            pltpu.VMEM((cells // 2, outs), f32),
            pltpu.VMEM((depth // 2, rows * cols // 4, outs), f32),
        ],
        vol, before, after, kernel, work=heavy * 8,
    )


def first_backward(vol, before, after, spread, slope, which, keep, send, u, rows_ref, g, acc, twice):
    depth, rows, cols, chans = vol.shape
    wide = 32
    cells = rows * wide
    outs = slope.shape[2]
    rows_ref[...] = jnp.zeros_like(rows_ref)
    for p in range(depth + 2):
        if p == 0:
            source = before[0]
        elif p == depth + 1:
            source = after[0]
        else:
            source = vol[p - 1]
        wide_plane(source, rows_ref, u.at[p], 0, wide)
    edge = jnp.zeros((depth, wide, outs), bf16)
    g[:, 0:wide, :] = edge
    g[:, wide + cells :, :] = edge
    for d in range(depth):
        if d % 2 == 0:
            values = spread[d // 2] * 0.125
            twice[pl.ds(0, cells // 4, stride=2), :] = values
            twice[pl.ds(1, cells // 4, stride=2), :] = values
        for h in range(rows):
            some = twice[(h // 2) * wide : (h // 2 + 1) * wide, :] * slope[d, h * wide : (h + 1) * wide, :]
            g[d, (h + 1) * wide : (h + 2) * wide, :] = some.astype(bf16)
    started = set()
    for p in range(depth + 2):
        taps = [a for a in range(3) if 0 <= p - a < depth]
        rhs = jnp.concatenate(
            [g[p - a, (2 - b) * wide : (2 - b) * wide + cells, :] for a in taps for b in range(3)], axis=1
        )
        part = lax.dot_general(u[p], rhs, (((0,), (0,)), ((), ())), preferred_element_type=f32)
        for place, a in enumerate(taps):
            block = part[:, place * 3 * outs : (place + 1) * 3 * outs]
            lanes = slice(a * 3 * outs, (a + 1) * 3 * outs)
            if a in started:
                acc[:, lanes] += block
            else:
                acc[:, lanes] = block
                started.add(a)
    pieces = keep.shape[0]
    size = chans // (2 * pieces)

    def write(first, second):
        for a in range(3):
            for b in range(3):
                for e in range(3):
                    t = 9 * a + 3 * b + e
                    lanes = slice((3 * a + b) * outs, (3 * a + b + 1) * outs)
                    for target, top in ((first, e * chans), (second, e * chans + chans // 2)):
                        block = acc[top : top + chans // 2, lanes]
                        target[:, t * size : (t + 1) * size, :] = block.reshape(pieces, size, outs)

    @pl.when(which[0] == 0)
    def _():
        write(keep, send)

    @pl.when(which[0] != 0)
    def _():
        write(send, keep)


def run_first_backward(vol, before, after, spread, slope, which, pieces):
    depth, rows, cols, chans = vol.shape
    wide, outs = 32, slope.shape[2]
    cells = rows * wide
    return call(
        first_backward,
        (jax.ShapeDtypeStruct((pieces // 2, 27 * chans // pieces, outs), f32),) * 2,
        [
            pltpu.VMEM((depth + 2, cells, 3 * chans), bf16),
            pltpu.VMEM((cells + 2 * front, chans), f32),
            pltpu.VMEM((depth, cells + 2 * wide, outs), bf16),
            pltpu.VMEM((3 * chans, 9 * outs), f32),
            pltpu.VMEM((cells // 2, outs), f32),
        ],
        vol, before, after, spread, slope, which, work=heavy * 7, smem=(5,),
    )


def lay_pooled(parts, places, flat, rows_ref, target, top, side, wide):
    chans = target.shape[2] // 3
    cells = side * wide
    for part, place in zip(parts, places):
        for d in range(part.shape[0]):
            flat[...] = part[d].astype(f32)
            for h in range(side):
                rows_ref[front + h * wide : front + h * wide + side, :] = flat[h * side : (h + 1) * side, :]
            for e in range(3):
                target[place + d, top : top + cells, e * chans : (e + 1) * chans] = shifted(
                    rows_ref, cells, e - 1
                ).astype(bf16)


def second_layer(
    where, p0, p1, p2, p3, w0, w1, w2, w3, w4, head, wanted,
    pooled_grad, own, result, p, flat, rows_ref, w, acc, slopes, shift_ref, g,
):
    parts, pieces = (p0, p1, p2, p3), (w1, w2, w3, w4)
    planes, area, chans = p0.shape
    side, wide = 12, 16
    cells = side * wide
    depth = planes * len(parts)
    outs = w.shape[0]
    rows_ref[...] = jnp.zeros_like(rows_ref)
    p[0] = jnp.zeros(p.shape[1:], bf16)
    p[depth + 1] = jnp.zeros(p.shape[1:], bf16)
    edge = jnp.zeros((depth + 2, wide, 3 * chans), bf16)
    p[:, 0:wide, :] = edge
    p[:, wide + cells :, :] = edge
    lay_pooled(parts, [1 + planes * where[k] for k in range(4)], flat, rows_ref, p, wide, side, wide)
    share = w0.shape[0]
    quarter = share // 4
    w[0:share, :] = w0[...]
    for k in range(1, 4):
        for j in range(4):
            at = pl.multiple_of(k * share + where[4 + j] * quarter, quarter)
            w[pl.ds(at, quarter), :] = pieces[j][(k - 1) * quarter : k * quarter, :]
    column = lax.broadcasted_iota(jnp.int32, (cells, outs), 0) % wide
    inside = column < side
    step = depth // 2
    slopes[0] = jnp.zeros((cells, outs), f32)
    slopes[depth + 1] = jnp.zeros((cells, outs), f32)

    def half(t, total):
        for a in range(3):
            lhs = jnp.concatenate(
                [
                    p[pl.ds(t * step + a, step), b * wide : b * wide + cells, :].reshape(step * cells, 3 * chans)
                    for b in range(3)
                ],
                axis=1,
            )
            part = lax.dot_general(
                lhs, w[:, 9 * a * chans : 9 * (a + 1) * chans], (((1,), (1,)), ((), ())), preferred_element_type=f32
            )
            if a == 0:
                acc[...] = part
            else:
                acc[...] += part
        for d in range(step):
            slope, value = slope_and_activation(acc[d * cells : (d + 1) * cells, :])
            slopes[t * step + d + 1] = jnp.where(inside, slope, 0.0)
            value = jnp.where(inside, value, 0.0)
            total = total + value.reshape(cells // 8, 8, outs).sum(axis=0)
        return total

    total = lax.fori_loop(0, 2, half, jnp.zeros((8, outs), f32))
    feature = total.sum(axis=0, keepdims=True) / float(depth * area)
    predicted = jnp.sum(feature * head[...], axis=1, keepdims=True)
    error = predicted - wanted[:, 0:1]
    result[...] = error * feature
    scale = jnp.sum(head[...] * error, axis=0, keepdims=True)
    for d in range(depth):
        own[d] = (slopes[d + 1, :, 0:share] * scale[:, 0:share]).astype(bf16)
    shift_ref[...] = jnp.zeros_like(shift_ref)
    rim = jnp.zeros((planes + 2, wide, outs), bf16)
    for e in range(3):
        g[e, :, 0:wide, :] = rim
        g[e, :, wide + cells :, :] = rim
    for k in range(planes + 2):
        shift_ref[front : front + cells, :] = (slopes[where[0] * planes + k] * scale).astype(bf16).astype(f32)
        for e in range(3):
            g[e, k, wide : wide + cells, :] = shifted(shift_ref, cells, 1 - e).astype(bf16)
    out = jnp.zeros((planes * cells, chans), f32)
    for a in range(3):
        for b in range(3):
            for e in range(3):
                lhs = g[e, 2 - a : 2 - a + planes, (2 - b) * wide : (2 - b) * wide + cells, :].reshape(planes * cells, outs)
                t = 9 * a + 3 * b + e
                out = out + jnp.dot(lhs, w[:, t * chans : (t + 1) * chans], preferred_element_type=f32)
    keep = lax.broadcasted_iota(jnp.int32, (planes * cells, chans), 0) % wide < side
    pooled_grad[...] = jnp.where(keep, out, 0.0).reshape(planes, cells, chans)


def run_second_layer(where, parts, part_kernel, pieces, head, wanted):
    planes, area, chans = parts[0].shape
    side, wide = 12, 16
    cells = side * wide
    depth = planes * 4
    share, taps = part_kernel.shape
    outs = 4 * share
    return call(
        second_layer,
        (
            jax.ShapeDtypeStruct((planes, cells, chans), f32),
            jax.ShapeDtypeStruct((depth, cells, share), bf16),
            jax.ShapeDtypeStruct((8, outs), f32),
        ),
        [
            pltpu.VMEM((depth + 2, cells + 2 * wide, 3 * chans), bf16),
            pltpu.VMEM((area, chans), f32),
            pltpu.VMEM((cells + 2 * front, chans), f32),
            pltpu.VMEM((outs, taps), bf16),
            pltpu.VMEM((depth // 2 * cells, outs), f32),
            pltpu.VMEM((depth + 2, cells, outs), f32),
            pltpu.VMEM((cells + 2 * front, outs), f32),
            pltpu.VMEM((3, planes + 2, cells + 2 * wide, outs), bf16),
        ],
        where, *parts, part_kernel, *pieces, head, wanted, smem=(0,), work=heavy * 8,
    )


def second_backward(where, p0, p1, p2, p3, own, result, grad, p, flat, rows_ref, g):
    parts = (p0, p1, p2, p3)
    planes, area, chans = p0.shape
    side, wide = 12, 16
    cells = side * wide
    depth = planes * len(parts)
    share = own.shape[2]
    rows_ref[...] = jnp.zeros_like(rows_ref)
    p[0] = jnp.zeros(p.shape[1:], bf16)
    p[depth + 1] = jnp.zeros(p.shape[1:], bf16)
    lay_pooled(parts, [1 + planes * where[k] for k in range(4)], flat, rows_ref, p, 0, side, wide)
    none = jnp.zeros((depth, wide, share), bf16)
    for b in range(3):
        lanes = slice(b * share, (b + 1) * share)
        if b == 0:
            g[:, 0 : cells - wide, lanes] = own[:, wide:cells, :]
            g[:, cells - wide :, lanes] = none
        elif b == 1:
            g[:, :, lanes] = own[...]
        else:
            g[:, wide:, lanes] = own[:, 0 : cells - wide, :]
            g[:, 0:wide, lanes] = none
    rhs = g[...].reshape(depth * cells, 3 * share)
    for a in range(3):
        lhs = p[a : a + depth].reshape(depth * cells, 3 * chans)
        part = lax.dot_general(rhs, lhs, (((0,), (0,)), ((), ())), preferred_element_type=f32)
        for b in range(3):
            for e in range(3):
                t = 9 * a + 3 * b + e
                block = part[b * share : (b + 1) * share, e * chans : (e + 1) * chans]
                grad[t * share : (t + 1) * share, :] = block
    grad[27 * share : 27 * share + 8, :] = result[:, 0:chans]
    grad[27 * share + 8 :, :] = jnp.zeros((8, chans), f32)


def run_second_backward(where, parts, own, result):
    planes, area, chans = parts[0].shape
    depth, cells, share = own.shape
    return call(
        second_backward,
        jax.ShapeDtypeStruct((27 * share + 16, chans), f32),
        [
            pltpu.VMEM((depth + 2, cells, 3 * chans), bf16),
            pltpu.VMEM((area, chans), f32),
            pltpu.VMEM((cells + 2 * front, chans), f32),
            pltpu.VMEM((depth, cells, 3 * share), bf16),
        ],
        where, *parts, own, result, smem=(0,), work=heavy * 4,
    )


def spread_first(blocks, out):
    pieces, rows, outs = blocks.shape
    size = 8
    for k in range(pieces):
        out[:, k * size : (k + 1) * size, :] = blocks[k].astype(f32).reshape(rows // size, size, outs)


def run_spread_first(blocks):
    pieces, rows, outs = blocks.shape
    steps, size = 9, rows // 27
    out = pl.pallas_call(
        spread_first,
        grid=(steps,),
        out_shape=jax.ShapeDtypeStruct((27, pieces * size, outs), f32),
        in_specs=[pl.BlockSpec((pieces, rows // steps, outs), lambda i: (0, i, 0))],
        out_specs=pl.BlockSpec((27 // steps, pieces * size, outs), lambda i: (i, 0, 0)),
    )(blocks)
    return out.reshape(-1, outs)


def spread_second(packed, out, head):
    chans = packed.shape[1]
    share = out.shape[0]
    for t in range(27):
        out[:, t * chans : (t + 1) * chans] = packed[t * share : (t + 1) * share, :]
    head[...] = packed[27 * share : 27 * share + 8, :]


def run_spread_second(packed, share):
    rows, chans = packed.shape
    return call(
        spread_second,
        (jax.ShapeDtypeStruct((share, 27 * chans), f32), jax.ShapeDtypeStruct((8, chans), f32)),
        [],
        packed,
    )


def turn(x, axis, step):
    size = lax.axis_size(axis)
    return lax.ppermute(x, axis, [(i, (i + step) % size) for i in range(size)])


def direct(axis):
    return lax.axis_size(axis) <= direct_most


def gathered(x, axis):
    if not direct(axis):
        return lax.all_gather(x, axis)
    size, place = lax.axis_size(axis), lax.axis_index(axis)
    parts = [x] + [turn(x, axis, step) for step in range(1, size)]
    out = jnp.zeros((size,) + x.shape, x.dtype)
    for step, part in enumerate(parts):
        out = lax.dynamic_update_index_in_dim(out, part, (place - step) % size, 0)
    return out


def scattered_sum(x, axis, wire):
    size, place = lax.axis_size(axis), lax.axis_index(axis)
    blocks = x.reshape((size, x.shape[0] // size) + x.shape[1:])
    if not direct(axis):
        return lax.psum_scatter(blocks, axis)
    total = lax.dynamic_index_in_dim(blocks, place, 0, False)
    for step in range(1, size):
        sent = lax.dynamic_index_in_dim(blocks, (place + step) % size, 0, False).astype(wire)
        total = total + turn(sent, axis, step).astype(jnp.float32)
    return total


def total_first(x):
    columns = x.shape[1]
    x = scattered_sum(x, "rep", jnp.float32)
    x = scattered_sum(x, "dp", jnp.bfloat16)
    if direct("space"):
        x = scattered_sum(x, "space", jnp.bfloat16).astype(jnp.bfloat16)
        x = gathered(x, "space").reshape(-1, columns)
    else:
        x = lax.psum(x, "space").astype(jnp.bfloat16)
    x = gathered(x, "dp").reshape(-1, columns)
    x = gathered(x, "rep").reshape(-1, columns)
    return x.astype(jnp.float32)


def total_second(x):
    columns = x.shape[1]
    x = scattered_sum(x, "rep", jnp.float32)
    if direct("dp"):
        x = gathered(x.astype(jnp.bfloat16), "dp").astype(jnp.float32).sum(0)
    else:
        x = lax.psum(x, "dp")
    return gathered(x, "rep").reshape(-1, columns)


def whole_kernel(part):
    rows, share = part.shape
    copies = [axis for axis in ("dp", "rep")]
    pieces, place = (1, 0)
    for axis in copies:
        place = place * lax.axis_size(axis) + lax.axis_index(axis)
        pieces = pieces * lax.axis_size(axis)
    length = rows // pieces
    piece = lax.dynamic_slice_in_dim(part, place * length, length, 0)
    packed = jnp.concatenate([piece[: length // 2], piece[length // 2 :]], axis=1)
    packs = gathered(packed, "space")
    upper = jnp.moveaxis(packs[:, :, :share], 0, 1).reshape(length // 2, -1)
    lower = jnp.moveaxis(packs[:, :, share:], 0, 1).reshape(length // 2, -1)
    wide = jnp.concatenate([upper, lower], axis=0)
    wide = gathered(wide, "dp")
    wide = jnp.moveaxis(gathered(wide, "rep"), 0, 1)
    return wide.reshape(rows, -1)


def extended_2(x, sides, width):
    for axis, dim in sides:
        devices, length = (lax.axis_size(axis), x.shape[dim])
        up = [(i, (i + 1) % devices) for i in range(devices - 1)]
        down = [(j, i) for i, j in up]
        last = lax.slice_in_dim(x, length - width, length, axis=dim)
        leading = lax.slice_in_dim(x, 0, width, axis=dim)
        before = lax.ppermute(last, axis, up)
        after = lax.ppermute(leading, axis, down)
        x = jnp.concatenate([before, x, after], axis=dim)
    return x


def activate(value):
    return leak_slope * value + (1.0 - leak_slope) * (jax.nn.softplus(value) - log_two)


def activate_slope(value):
    return leak_slope + (1.0 - leak_slope) * jax.nn.sigmoid(value)


def convolve(extended, kernel):
    result = lax.conv_general_dilated(
        extended[None],
        kernel,
        (1, 1, 1),
        [(0, 0), (1, 1), (1, 1)],
        dimension_numbers=("NDHWC", "DHWIO", "NDHWC"),
        preferred_element_type=jnp.float32,
    )
    return result[0]


def pooling(grid):
    depth, rows, cols, chans = grid.shape
    return grid.reshape(depth // 2, 2, rows // 2, 2, cols // 2, 2, chans).mean(axis=(1, 3, 5))


def expand(grid):
    depth, rows, cols, chans = grid.shape
    spread = jnp.broadcast_to(
        grid[:, None, :, None, :, None, :], (depth, 2, rows, 2, cols, 2, chans)
    )
    return spread.reshape(depth * 2, rows * 2, cols * 2, chans) / 8.0


def kernel_grad(extended, grad):
    widened = jnp.pad(extended, ((0, 0), (1, 1), (1, 1), (0, 0)))
    result = lax.conv_general_dilated(
        widened[..., None],
        grad[:, :, :, None, :],
        (1, 1, 1),
        "VALID",
        dimension_numbers=("DHWNC", "DHWIO", "NDHWC"),
        preferred_element_type=jnp.float32,
    )
    return jnp.transpose(result, (1, 2, 3, 0, 4)).reshape(-1, grad.shape[-1])


def general_shards(volumes, targets, first_kernel, second_kernel, head_weights):
    grid_in = volumes[0]
    target_row = targets[0]
    channels = grid_in.shape[-1]
    kernel_one = first_kernel.reshape(3, 3, 3, channels, first_kernel.shape[1])
    extended = extended_2(grid_in, (("space", 0),), 1)
    share = second_kernel.shape[1]
    place = lax.axis_index("space")
    kernel_two = whole_kernel(second_kernel).reshape(3, 3, 3, channels, -1)
    before_one = convolve(extended, kernel_one)
    pooled = pooling(activate(before_one)).astype(jnp.bfloat16)
    whole = gathered(pooled, "space").reshape((-1,) + pooled.shape[1:])
    padded_whole = jnp.pad(whole, ((1, 1), (0, 0), (0, 0), (0, 0)))
    before_two = convolve(padded_whole, kernel_two)
    feature = jnp.mean(activate(before_two), axis=(0, 1, 2))
    predicted = jnp.dot(feature, head_weights, precision=lax.Precision.HIGHEST)
    error = predicted - target_row
    feature_part = lax.dynamic_slice_in_dim(feature, place * share, share, 0)
    head_grad = feature_part[:, None] * error[None, :]
    feature_grad = jnp.dot(head_weights, error, precision=lax.Precision.HIGHEST)
    grad_two = (feature_grad * activate_slope(before_two)).astype(jnp.bfloat16)
    padded_grad = jnp.pad(grad_two, ((1, 1), (0, 0), (0, 0), (0, 0)))
    flipped = jnp.swapaxes(kernel_two[::-1, ::-1, ::-1], 3, 4)
    planes = pooled.shape[0]
    window = lax.dynamic_slice_in_dim(padded_grad, place * planes, planes + 2, 0)
    pooled_grad = convolve(window, flipped)
    grad_one = (expand(pooled_grad) * activate_slope(before_one)).astype(jnp.bfloat16)
    first_total = total_first(kernel_grad(extended, grad_one))
    grad_part = lax.dynamic_slice_in_dim(grad_two, place * share, share, 3)
    second_part = kernel_grad(padded_whole, grad_part)
    rows = second_part.shape[0]
    packed = jnp.concatenate([second_part[: rows // 2], second_part[rows // 2 :]], axis=1)
    packed = total_second(packed)
    second_total = jnp.concatenate([packed[:, :share], packed[:, share:]], axis=0)
    head_total = gathered(gathered(head_grad, "rep").sum(0), "dp").sum(0)
    return (first_total, second_total, head_total)


def neighbours(grid):
    devices = lax.axis_size("space")
    up = [(i, i + 1) for i in range(devices - 1)]
    down = [(j, i) for i, j in up]
    before = lax.ppermute(grid[-1:], "space", up)
    after = lax.ppermute(grid[:1], "space", down)
    return before, after


def shards(volumes, targets, first_kernel, second_kernel, head_weights):
    sizes = tuple(lax.axis_size(axis) for axis in ("space", "dp", "rep"))
    if sizes != (4, 2, 2):
        return general_shards(volumes, targets, first_kernel, second_kernel, head_weights)
    grid = volumes[0]
    share = second_kernel.shape[1]
    outs = head_weights.shape[1]
    place = lax.axis_index("space")
    rep = lax.axis_index("rep")
    copy = 2 * lax.axis_index("dp") + rep
    where = jnp.stack([(place - k) % 4 for k in range(4)] + [copy ^ k for k in range(4)])
    before, after = neighbours(grid)
    turned = second_kernel.T
    piece = lax.dynamic_slice_in_dim(turned, copy * (share // 4), share // 4, 0)
    others = jnp.concatenate([turn(piece, "space", k) for k in range(1, 4)], axis=0)
    across = turn(others, "dp", 1)
    pieces = [others, turn(others, "rep", 1), across, turn(across, "rep", 1)]
    pooled, slope = run_first_forward(grid, before, after, first_kernel)
    parts = [pooled] + [turn(pooled, "space", k) for k in range(1, 4)]
    blocks = head_weights.T.reshape(outs, 4, share)
    head = jnp.concatenate([lax.dynamic_index_in_dim(blocks, (place - k) % 4, 1, False) for k in range(4)], axis=1)
    head = jnp.pad(head, ((0, 8 - outs), (0, 0)))
    wanted = jnp.pad(jnp.broadcast_to(targets[0][:, None], (outs, 128)), ((0, 8 - outs), (0, 0)))
    pooled_grad, own, result = run_second_layer(where, parts, turned, pieces, head, wanted)
    keep, send = run_first_backward(grid, before, after, pooled_grad, slope, rep[None], 16)
    x = keep + turn(send, "rep", 1)
    x, own = lax.optimization_barrier((x, own))
    second_part = run_second_backward(where, parts, own, result)
    x = x.reshape(-1, x.shape[2])
    x = scattered_sum(x, "dp", bf16)
    x, second_part = lax.optimization_barrier((x, second_part))
    x = scattered_sum(x, "space", bf16).astype(bf16)
    for axis in ("space", "dp", "rep"):
        x = gathered(x, axis).reshape(-1, x.shape[1])
    first_total = run_spread_first(x.reshape((16, -1) + x.shape[1:]))
    second_total, head_total = run_spread_second(total_second(second_part), share)
    return (first_total, second_total.T, head_total[:outs, :share].T)


def solution(mesh):
    in_specs = (
        P(("groups", "dp", "rep"), "space", None, None, None),
        P(("groups", "dp", "rep"), None),
        P(),
        P(None, "space"),
        P(),
    )
    out_specs = (P("groups", None), P("groups", "space"), P(("groups", "space"), None))
    return jax.shard_map(shards, mesh=mesh, in_specs=in_specs, out_specs=out_specs, check_vma=False)
```

```python
import jax
import jax.numpy as jnp
from jax import lax
from jax.experimental import pallas as pl
from jax.experimental.pallas import tpu as pltpu
from jax.sharding import PartitionSpec as P

leak_slope = 0.3
log_two = 0.6931471805599453
direct_most = 4
f32, bf16 = jnp.float32, jnp.bfloat16
front = 8
heavy = 10**9


def call(body, outs, scratch, *args, smem=(), away=(), work=0, room=16, far_outs=()):
    spaces = [pltpu.SMEM if k in smem else pltpu.HBM if k in away else pltpu.VMEM for k in range(len(args))]
    specs = [pl.BlockSpec(memory_space=space) for space in spaces]
    one = not isinstance(outs, tuple)
    out_specs = [
        pl.BlockSpec(memory_space=pltpu.HBM if k in far_outs else pltpu.VMEM) for k in range(1 if one else len(outs))
    ]
    out_specs = out_specs[0] if one else tuple(out_specs)
    return pl.pallas_call(
        body,
        out_shape=outs,
        in_specs=specs,
        out_specs=out_specs,
        scratch_shapes=scratch,
        compiler_params=pltpu.CompilerParams(vmem_limit_bytes=room * 2**20),
        cost_estimate=pl.CostEstimate(flops=work, bytes_accessed=0, transcendentals=0),
    )(*args)


def slope_and_activation(value):
    shrunk = jnp.exp(-jnp.abs(value))
    inverse = 1.0 / (1.0 + shrunk)
    slope = leak_slope + (1.0 - leak_slope) * jnp.where(value >= 0, inverse, shrunk * inverse)
    soft = jnp.maximum(value, 0.0) + jnp.log(1.0 + shrunk)
    return slope, leak_slope * value + (1.0 - leak_slope) * (soft - log_two)


def shifted(rows_ref, length, step):
    return rows_ref[front + step : front + step + length, :]


def lay_plane(plane, rows_ref, wide):
    rows, cols, chans = plane.shape
    for h in range(rows):
        rows_ref[front + h * wide : front + h * wide + cols, :] = plane[h].astype(f32)


def wide_plane(source, rows_ref, target, top, wide):
    rows, chans = source.shape[0], source.shape[2]
    lay_plane(source, rows_ref, wide)
    for e in range(3):
        target[top : top + rows * wide, e * chans : (e + 1) * chans] = shifted(
            rows_ref, rows * wide, e - 1
        ).astype(bf16)


def first_forward(vol, before, after, kernel, pooled, slope, u, rows_ref, pairs, acc, half, dense):
    depth, rows, cols, chans = vol.shape
    wide = 32
    cells = rows * wide
    outs = kernel.shape[1]
    span = 3 * chans
    rows_ref[...] = jnp.zeros_like(rows_ref)
    edge = jnp.zeros((u.shape[0], wide, span), bf16)
    u[:, 0:wide, :] = edge
    u[:, wide + cells :, :] = edge
    for p in range(depth + 2):
        if p == 0:
            source = before[0]
        elif p == depth + 1:
            source = after[0]
        else:
            source = vol[p - 1]
        wide_plane(source, rows_ref, u.at[p], wide, wide)

    def tap(a, b):
        return kernel[(9 * a + 3 * b) * chans : (9 * a + 3 * b) * chans + span, :]

    for b in range(3):
        pairs[b, 0:span, 0:outs] = tap(1, b)
        pairs[b, 0:span, outs:] = tap(0, b)
        pairs[b, span:, 0:outs] = tap(2, b)
        pairs[b, span:, outs:] = tap(1, b)
    first_taps = jnp.concatenate([tap(0, b) for b in range(3)], axis=0)
    last_taps = jnp.concatenate([tap(2, b) for b in range(3)], axis=0)

    def one_pair(t, carry):
        def window(q, b):
            return u[2 * t + q, b * wide : b * wide + cells, :]

        left = jnp.concatenate([window(0, b) for b in range(3)], axis=1)
        acc[:, 0:outs] = jnp.dot(left, first_taps, preferred_element_type=f32)
        right = jnp.concatenate([window(3, b) for b in range(3)], axis=1)
        acc[:, outs:] = jnp.dot(right, last_taps, preferred_element_type=f32)
        for b in range(3):
            both = jnp.concatenate([window(1, b), window(2, b)], axis=1)
            acc[...] += jnp.dot(both, pairs[b], preferred_element_type=f32)
        for h in range(rows // 2):
            part = acc[h * 2 * wide : (h + 1) * 2 * wide, :]
            slopes, values = slope_and_activation(part)
            slope[2 * t, h * 2 * wide : (h + 1) * 2 * wide, :] = slopes[:, 0:outs]
            slope[2 * t + 1, h * 2 * wide : (h + 1) * 2 * wide, :] = slopes[:, outs:]
            values = values[:, 0:outs] + values[:, outs:]
            half[h * wide : (h + 1) * wide, :] = values[0:wide] + values[wide:]
        for h in range(rows // 2):
            even = half[pl.ds(h * wide, cols // 2, stride=2), :]
            odd = half[pl.ds(h * wide + 1, cols // 2, stride=2), :]
            dense[t, h * (cols // 2) : (h + 1) * (cols // 2), :] = (even + odd) * 0.125
        return carry

    lax.fori_loop(0, depth // 2, one_pair, 0)
    pooled[...] = dense[...].astype(bf16)


def run_first_forward(vol, before, after, kernel):
    depth, rows, cols, chans = vol.shape
    wide, outs = 32, kernel.shape[1]
    cells = rows * wide
    return call(
        first_forward,
        (
            jax.ShapeDtypeStruct((depth // 2, rows * cols // 4, outs), bf16),
            jax.ShapeDtypeStruct((depth, cells, outs), f32),
        ),
        [
            pltpu.VMEM((depth + 2, cells + 2 * wide, 3 * chans), bf16),
            pltpu.VMEM((cells + 2 * front, chans), f32),
            pltpu.VMEM((3, 6 * chans, 2 * outs), bf16),
            pltpu.VMEM((cells, 2 * outs), f32),
            pltpu.VMEM((cells // 2, outs), f32),
            pltpu.VMEM((depth // 2, rows * cols // 4, outs), f32),
        ],
        vol, before, after, kernel, work=heavy * 8,
    )


def first_backward(vol, before, after, spread, slope, which, keep, send, u, rows_ref, g, acc, twice):
    depth, rows, cols, chans = vol.shape
    wide = 32
    cells = rows * wide
    outs = slope.shape[2]
    rows_ref[...] = jnp.zeros_like(rows_ref)
    for p in range(depth + 2):
        if p == 0:
            source = before[0]
        elif p == depth + 1:
            source = after[0]
        else:
            source = vol[p - 1]
        wide_plane(source, rows_ref, u.at[p], 0, wide)
    edge = jnp.zeros((depth, wide, outs), bf16)
    g[:, 0:wide, :] = edge
    g[:, wide + cells :, :] = edge
    for d in range(depth):
        if d % 2 == 0:
            values = spread[d // 2] * 0.125
            twice[pl.ds(0, cells // 4, stride=2), :] = values
            twice[pl.ds(1, cells // 4, stride=2), :] = values
        for h in range(rows):
            some = twice[(h // 2) * wide : (h // 2 + 1) * wide, :] * slope[d, h * wide : (h + 1) * wide, :]
            g[d, (h + 1) * wide : (h + 2) * wide, :] = some.astype(bf16)
    started = set()
    for p in range(depth + 2):
        taps = [a for a in range(3) if 0 <= p - a < depth]
        rhs = jnp.concatenate(
            [g[p - a, (2 - b) * wide : (2 - b) * wide + cells, :] for a in taps for b in range(3)], axis=1
        )
        part = lax.dot_general(u[p], rhs, (((0,), (0,)), ((), ())), preferred_element_type=f32)
        for place, a in enumerate(taps):
            block = part[:, place * 3 * outs : (place + 1) * 3 * outs]
            lanes = slice(a * 3 * outs, (a + 1) * 3 * outs)
            if a in started:
                acc[:, lanes] += block
            else:
                acc[:, lanes] = block
                started.add(a)
    length = keep.shape[0]

    def write(first, second):
        for a in range(3):
            for b in range(3):
                for e in range(3):
                    top = (9 * a + 3 * b + e) * chans
                    lanes = slice((3 * a + b) * outs, (3 * a + b + 1) * outs)
                    cut = min(max(length - top, 0), chans)
                    if cut > 0:
                        first[top : top + cut, :] = acc[e * chans : e * chans + cut, lanes]
                    if cut < chans:
                        low = top + cut - length
                        second[low : low + chans - cut, :] = acc[e * chans + cut : (e + 1) * chans, lanes]

    @pl.when(which[0] == 0)
    def _():
        write(keep, send)

    @pl.when(which[0] != 0)
    def _():
        write(send, keep)


def run_first_backward(vol, before, after, spread, slope, which):
    depth, rows, cols, chans = vol.shape
    wide, outs = 32, slope.shape[2]
    cells = rows * wide
    return call(
        first_backward,
        (jax.ShapeDtypeStruct((27 * chans // 2, outs), f32),) * 2,
        [
            pltpu.VMEM((depth + 2, cells, 3 * chans), bf16),
            pltpu.VMEM((cells + 2 * front, chans), f32),
            pltpu.VMEM((depth, cells + 2 * wide, outs), bf16),
            pltpu.VMEM((3 * chans, 9 * outs), f32),
            pltpu.VMEM((cells // 2, outs), f32),
        ],
        vol, before, after, spread, slope, which, work=heavy * 7, smem=(5,),
    )


def lay_pooled(parts, places, flat, rows_ref, target, top, side, wide):
    chans = target.shape[2] // 3
    cells = side * wide
    for part, place in zip(parts, places):
        for d in range(part.shape[0]):
            flat[...] = part[d].astype(f32)
            for h in range(side):
                rows_ref[front + h * wide : front + h * wide + side, :] = flat[h * side : (h + 1) * side, :]
            for e in range(3):
                target[place + d, top : top + cells, e * chans : (e + 1) * chans] = shifted(
                    rows_ref, cells, e - 1
                ).astype(bf16)


def second_layer(
    where, p0, p1, p2, p3, w0, w1, w2, w3, w4, head, wanted,
    pooled_grad, own, result, p, flat, rows_ref, w, acc, slopes, shift_ref, g,
):
    parts, pieces = (p0, p1, p2, p3), (w1, w2, w3, w4)
    planes, area, chans = p0.shape
    side, wide = 12, 16
    cells = side * wide
    depth = planes * len(parts)
    outs = w.shape[0]
    rows_ref[...] = jnp.zeros_like(rows_ref)
    p[0] = jnp.zeros(p.shape[1:], bf16)
    p[depth + 1] = jnp.zeros(p.shape[1:], bf16)
    edge = jnp.zeros((depth + 2, wide, 3 * chans), bf16)
    p[:, 0:wide, :] = edge
    p[:, wide + cells :, :] = edge
    lay_pooled(parts, [1 + planes * where[k] for k in range(4)], flat, rows_ref, p, wide, side, wide)
    share = w0.shape[0]
    quarter = share // 4
    w[0:share, :] = w0[...]
    for k in range(1, 4):
        for j in range(4):
            at = pl.multiple_of(k * share + where[4 + j] * quarter, quarter)
            w[pl.ds(at, quarter), :] = pieces[j][(k - 1) * quarter : k * quarter, :]
    column = lax.broadcasted_iota(jnp.int32, (cells, outs), 0) % wide
    inside = column < side
    step = depth // 2
    slopes[0] = jnp.zeros((cells, outs), f32)
    slopes[depth + 1] = jnp.zeros((cells, outs), f32)

    def half(t, total):
        for a in range(3):
            lhs = jnp.concatenate(
                [
                    p[pl.ds(t * step + a, step), b * wide : b * wide + cells, :].reshape(step * cells, 3 * chans)
                    for b in range(3)
                ],
                axis=1,
            )
            part = lax.dot_general(
                lhs, w[:, 9 * a * chans : 9 * (a + 1) * chans], (((1,), (1,)), ((), ())), preferred_element_type=f32
            )
            if a == 0:
                acc[...] = part
            else:
                acc[...] += part
        for d in range(step):
            slope, value = slope_and_activation(acc[d * cells : (d + 1) * cells, :])
            slopes[t * step + d + 1] = jnp.where(inside, slope, 0.0)
            value = jnp.where(inside, value, 0.0)
            total = total + value.reshape(cells // 8, 8, outs).sum(axis=0)
        return total

    total = lax.fori_loop(0, 2, half, jnp.zeros((8, outs), f32))
    feature = total.sum(axis=0, keepdims=True) / float(depth * area)
    predicted = jnp.sum(feature * head[...], axis=1, keepdims=True)
    error = predicted - wanted[:, 0:1]
    result[...] = error * feature
    scale = jnp.sum(head[...] * error, axis=0, keepdims=True)
    for d in range(depth):
        own[d] = (slopes[d + 1, :, 0:share] * scale[:, 0:share]).astype(bf16)
    shift_ref[...] = jnp.zeros_like(shift_ref)
    rim = jnp.zeros((planes + 2, wide, outs), bf16)
    for e in range(3):
        g[e, :, 0:wide, :] = rim
        g[e, :, wide + cells :, :] = rim
    for k in range(planes + 2):
        shift_ref[front : front + cells, :] = (slopes[where[0] * planes + k] * scale).astype(bf16).astype(f32)
        for e in range(3):
            g[e, k, wide : wide + cells, :] = shifted(shift_ref, cells, 1 - e).astype(bf16)
    out = jnp.zeros((planes * cells, chans), f32)
    for a in range(3):
        for b in range(3):
            for e in range(3):
                lhs = g[e, 2 - a : 2 - a + planes, (2 - b) * wide : (2 - b) * wide + cells, :].reshape(planes * cells, outs)
                t = 9 * a + 3 * b + e
                out = out + jnp.dot(lhs, w[:, t * chans : (t + 1) * chans], preferred_element_type=f32)
    keep = lax.broadcasted_iota(jnp.int32, (planes * cells, chans), 0) % wide < side
    pooled_grad[...] = jnp.where(keep, out, 0.0).reshape(planes, cells, chans)


def run_second_layer(where, parts, part_kernel, pieces, head, wanted):
    planes, area, chans = parts[0].shape
    side, wide = 12, 16
    cells = side * wide
    depth = planes * 4
    share, taps = part_kernel.shape
    outs = 4 * share
    return call(
        second_layer,
        (
            jax.ShapeDtypeStruct((planes, cells, chans), f32),
            jax.ShapeDtypeStruct((depth, cells, share), bf16),
            jax.ShapeDtypeStruct((8, outs), f32),
        ),
        [
            pltpu.VMEM((depth + 2, cells + 2 * wide, 3 * chans), bf16),
            pltpu.VMEM((area, chans), f32),
            pltpu.VMEM((cells + 2 * front, chans), f32),
            pltpu.VMEM((outs, taps), bf16),
            pltpu.VMEM((depth // 2 * cells, outs), f32),
            pltpu.VMEM((depth + 2, cells, outs), f32),
            pltpu.VMEM((cells + 2 * front, outs), f32),
            pltpu.VMEM((3, planes + 2, cells + 2 * wide, outs), bf16),
        ],
        where, *parts, part_kernel, *pieces, head, wanted, smem=(0,), work=heavy * 8,
    )


def second_backward(where, p0, p1, p2, p3, own, result, which, keep, send, p, flat, rows_ref, g, grad):
    parts = (p0, p1, p2, p3)
    planes, area, chans = p0.shape
    side, wide = 12, 16
    cells = side * wide
    depth = planes * len(parts)
    share = own.shape[2]
    rows_ref[...] = jnp.zeros_like(rows_ref)
    p[0] = jnp.zeros(p.shape[1:], bf16)
    p[depth + 1] = jnp.zeros(p.shape[1:], bf16)
    lay_pooled(parts, [1 + planes * where[k] for k in range(4)], flat, rows_ref, p, 0, side, wide)
    none = jnp.zeros((depth, wide, share), bf16)
    for b in range(3):
        lanes = slice(b * share, (b + 1) * share)
        if b == 0:
            g[:, 0 : cells - wide, lanes] = own[:, wide:cells, :]
            g[:, cells - wide :, lanes] = none
        elif b == 1:
            g[:, :, lanes] = own[...]
        else:
            g[:, wide:, lanes] = own[:, 0 : cells - wide, :]
            g[:, 0:wide, lanes] = none
    rhs = g[...].reshape(depth * cells, 3 * share)
    for a in range(3):
        lhs = p[a : a + depth].reshape(depth * cells, 3 * chans)
        part = lax.dot_general(rhs, lhs, (((0,), (0,)), ((), ())), preferred_element_type=f32)
        for b in range(3):
            for e in range(3):
                t = 9 * a + 3 * b + e
                block = part[b * share : (b + 1) * share, e * chans : (e + 1) * chans]
                grad[t * share : (t + 1) * share, :] = block
    grad[27 * share : 27 * share + 8, :] = result[:, 0:chans]
    grad[27 * share + 8 :, :] = jnp.zeros((8, chans), f32)
    half = keep.shape[0]
    low = pl.multiple_of(which[0] * half, 8)
    keep[...] = grad[pl.ds(low, half), :]
    send[...] = grad[pl.ds(pl.multiple_of(half - low, 8), half), :]


def run_second_backward(where, parts, own, result, which):
    planes, area, chans = parts[0].shape
    depth, cells, share = own.shape
    return call(
        second_backward,
        (jax.ShapeDtypeStruct((27 * share // 2 + 8, chans), f32),) * 2,
        [
            pltpu.VMEM((depth + 2, cells, 3 * chans), bf16),
            pltpu.VMEM((area, chans), f32),
            pltpu.VMEM((cells + 2 * front, chans), f32),
            pltpu.VMEM((depth, cells, 3 * share), bf16),
            pltpu.VMEM((27 * share + 16, chans), f32),
        ],
        where, *parts, own, result, which, smem=(0, 7), work=heavy * 4,
    )


def join(r0, r1, r2, out):
    rows = r0.shape[0]
    for k, r in enumerate((r0, r1, r2)):
        out[k * rows : (k + 1) * rows, :] = r[...]


def run_join(parts):
    rows, cols = parts[0].shape
    return call(join, jax.ShapeDtypeStruct((3 * rows, cols), bf16), [], *parts)


def merge_half(which, kept, came, keep, send):
    half = keep.shape[0]
    low = pl.multiple_of(which[0] * half, 8)
    high = pl.multiple_of(half - low, 8)
    keep[...] = kept[pl.ds(low, half), :] + came[pl.ds(low, half), :]
    send[...] = (kept[pl.ds(high, half), :] + came[pl.ds(high, half), :]).astype(bf16)


def run_merge_half(which, kept, came):
    rows, cols = kept.shape
    outs = tuple(jax.ShapeDtypeStruct((rows // 2, cols), kind) for kind in (f32, bf16))
    return call(merge_half, outs, [], which, kept, came, smem=(0,))


def merge_blocks(which, kept, came, keep, s1, s2, s3):
    size = keep.shape[0]

    def block(step):
        low = pl.multiple_of((which[0] + step) % 4 * size, 8)
        return kept[pl.ds(low, size), :] + came[pl.ds(low, size), :].astype(f32)

    keep[...] = block(0)
    for step, send in ((1, s1), (2, s2), (3, s3)):
        send[...] = block(step).astype(bf16)


def run_merge_blocks(which, kept, came):
    rows, cols = kept.shape
    outs = tuple(jax.ShapeDtypeStruct((rows // 4, cols), kind) for kind in (f32, bf16, bf16, bf16))
    return call(merge_blocks, outs, [], which, kept, came, smem=(0,))


def spread_second(packed, out, head):
    chans = packed.shape[1]
    share = out.shape[0]
    for t in range(27):
        out[:, t * chans : (t + 1) * chans] = packed[t * share : (t + 1) * share, :]
    head[...] = packed[27 * share : 27 * share + head.shape[0], 0:share]


def run_spread_second(packed, share, outs):
    rows, chans = packed.shape
    return call(
        spread_second,
        (jax.ShapeDtypeStruct((share, 27 * chans), f32), jax.ShapeDtypeStruct((outs, share), f32)),
        [],
        packed,
        work=heavy * 2,
    )


def turn(x, axis, step):
    size = lax.axis_size(axis)
    return lax.ppermute(x, axis, [(i, (i + step) % size) for i in range(size)])


def paired(x, axis, bits):
    return lax.ppermute(x, axis, [(i, i ^ bits) for i in range(lax.axis_size(axis))])


def direct(axis):
    return lax.axis_size(axis) <= direct_most


def gathered(x, axis):
    if not direct(axis):
        return lax.all_gather(x, axis)
    size, place = lax.axis_size(axis), lax.axis_index(axis)
    parts = [x] + [turn(x, axis, step) for step in range(1, size)]
    out = jnp.zeros((size,) + x.shape, x.dtype)
    for step, part in enumerate(parts):
        out = lax.dynamic_update_index_in_dim(out, part, (place - step) % size, 0)
    return out


def scattered_sum(x, axis, wire):
    size, place = lax.axis_size(axis), lax.axis_index(axis)
    blocks = x.reshape((size, x.shape[0] // size) + x.shape[1:])
    if not direct(axis):
        return lax.psum_scatter(blocks, axis)
    total = lax.dynamic_index_in_dim(blocks, place, 0, False)
    for step in range(1, size):
        sent = lax.dynamic_index_in_dim(blocks, (place + step) % size, 0, False).astype(wire)
        total = total + turn(sent, axis, step).astype(jnp.float32)
    return total


def total_first(x):
    columns = x.shape[1]
    x = scattered_sum(x, "rep", jnp.float32)
    x = scattered_sum(x, "dp", jnp.bfloat16)
    if direct("space"):
        x = scattered_sum(x, "space", jnp.bfloat16).astype(jnp.bfloat16)
        x = gathered(x, "space").reshape(-1, columns)
    else:
        x = lax.psum(x, "space").astype(jnp.bfloat16)
    x = gathered(x, "dp").reshape(-1, columns)
    x = gathered(x, "rep").reshape(-1, columns)
    return x.astype(jnp.float32)


def total_second(x):
    columns = x.shape[1]
    x = scattered_sum(x, "rep", jnp.float32)
    if direct("dp"):
        x = gathered(x, "dp").sum(0)
    else:
        x = lax.psum(x, "dp")
    return gathered(x, "rep").reshape(-1, columns)


def whole_kernel(part):
    rows, share = part.shape
    copies = [axis for axis in ("dp", "rep")]
    pieces, place = (1, 0)
    for axis in copies:
        place = place * lax.axis_size(axis) + lax.axis_index(axis)
        pieces = pieces * lax.axis_size(axis)
    length = rows // pieces
    piece = lax.dynamic_slice_in_dim(part, place * length, length, 0)
    packed = jnp.concatenate([piece[: length // 2], piece[length // 2 :]], axis=1)
    packs = gathered(packed, "space")
    upper = jnp.moveaxis(packs[:, :, :share], 0, 1).reshape(length // 2, -1)
    lower = jnp.moveaxis(packs[:, :, share:], 0, 1).reshape(length // 2, -1)
    wide = jnp.concatenate([upper, lower], axis=0)
    wide = gathered(wide, "dp")
    wide = jnp.moveaxis(gathered(wide, "rep"), 0, 1)
    return wide.reshape(rows, -1)


def extended_2(x, sides, width):
    for axis, dim in sides:
        devices, length = (lax.axis_size(axis), x.shape[dim])
        up = [(i, (i + 1) % devices) for i in range(devices - 1)]
        down = [(j, i) for i, j in up]
        last = lax.slice_in_dim(x, length - width, length, axis=dim)
        leading = lax.slice_in_dim(x, 0, width, axis=dim)
        before = lax.ppermute(last, axis, up)
        after = lax.ppermute(leading, axis, down)
        x = jnp.concatenate([before, x, after], axis=dim)
    return x


def activate(value):
    return leak_slope * value + (1.0 - leak_slope) * (jax.nn.softplus(value) - log_two)


def activate_slope(value):
    return leak_slope + (1.0 - leak_slope) * jax.nn.sigmoid(value)


def convolve(extended, kernel):
    result = lax.conv_general_dilated(
        extended[None],
        kernel,
        (1, 1, 1),
        [(0, 0), (1, 1), (1, 1)],
        dimension_numbers=("NDHWC", "DHWIO", "NDHWC"),
        preferred_element_type=jnp.float32,
    )
    return result[0]


def pooling(grid):
    depth, rows, cols, chans = grid.shape
    return grid.reshape(depth // 2, 2, rows // 2, 2, cols // 2, 2, chans).mean(axis=(1, 3, 5))


def expand(grid):
    depth, rows, cols, chans = grid.shape
    spread = jnp.broadcast_to(
        grid[:, None, :, None, :, None, :], (depth, 2, rows, 2, cols, 2, chans)
    )
    return spread.reshape(depth * 2, rows * 2, cols * 2, chans) / 8.0


def kernel_grad(extended, grad):
    widened = jnp.pad(extended, ((0, 0), (1, 1), (1, 1), (0, 0)))
    result = lax.conv_general_dilated(
        widened[..., None],
        grad[:, :, :, None, :],
        (1, 1, 1),
        "VALID",
        dimension_numbers=("DHWNC", "DHWIO", "NDHWC"),
        preferred_element_type=jnp.float32,
    )
    return jnp.transpose(result, (1, 2, 3, 0, 4)).reshape(-1, grad.shape[-1])


def general_shards(volumes, targets, first_kernel, second_kernel, head_weights):
    grid_in = volumes[0]
    target_row = targets[0]
    channels = grid_in.shape[-1]
    kernel_one = first_kernel.reshape(3, 3, 3, channels, first_kernel.shape[1])
    extended = extended_2(grid_in, (("space", 0),), 1)
    share = second_kernel.shape[1]
    place = lax.axis_index("space")
    kernel_two = whole_kernel(second_kernel).reshape(3, 3, 3, channels, -1)
    before_one = convolve(extended, kernel_one)
    pooled = pooling(activate(before_one)).astype(jnp.bfloat16)
    whole = gathered(pooled, "space").reshape((-1,) + pooled.shape[1:])
    padded_whole = jnp.pad(whole, ((1, 1), (0, 0), (0, 0), (0, 0)))
    before_two = convolve(padded_whole, kernel_two)
    feature = jnp.mean(activate(before_two), axis=(0, 1, 2))
    predicted = jnp.dot(feature, head_weights, precision=lax.Precision.HIGHEST)
    error = predicted - target_row
    feature_part = lax.dynamic_slice_in_dim(feature, place * share, share, 0)
    head_grad = feature_part[:, None] * error[None, :]
    feature_grad = jnp.dot(head_weights, error, precision=lax.Precision.HIGHEST)
    grad_two = (feature_grad * activate_slope(before_two)).astype(jnp.bfloat16)
    padded_grad = jnp.pad(grad_two, ((1, 1), (0, 0), (0, 0), (0, 0)))
    flipped = jnp.swapaxes(kernel_two[::-1, ::-1, ::-1], 3, 4)
    planes = pooled.shape[0]
    window = lax.dynamic_slice_in_dim(padded_grad, place * planes, planes + 2, 0)
    pooled_grad = convolve(window, flipped)
    grad_one = (expand(pooled_grad) * activate_slope(before_one)).astype(jnp.bfloat16)
    first_total = total_first(kernel_grad(extended, grad_one))
    grad_part = lax.dynamic_slice_in_dim(grad_two, place * share, share, 3)
    second_part = kernel_grad(padded_whole, grad_part)
    rows = second_part.shape[0]
    packed = jnp.concatenate([second_part[: rows // 2], second_part[rows // 2 :]], axis=1)
    packed = total_second(packed)
    second_total = jnp.concatenate([packed[:, :share], packed[:, share:]], axis=0)
    head_total = gathered(gathered(head_grad, "rep").sum(0), "dp").sum(0)
    return (first_total, second_total, head_total)


def neighbours(first, last):
    devices = lax.axis_size("space")
    up = [(i, i + 1) for i in range(devices - 1)]
    down = [(j, i) for i, j in up]
    before = lax.ppermute(last, "space", up)
    after = lax.ppermute(first, "space", down)
    return before, after


def shards(volumes, targets, first_kernel, second_kernel, head_weights):
    sizes = tuple(lax.axis_size(axis) for axis in ("space", "dp", "rep"))
    if sizes != (4, 2, 2):
        return general_shards(volumes, targets, first_kernel, second_kernel, head_weights)
    grid = volumes[0]
    share = second_kernel.shape[1]
    outs = head_weights.shape[1]
    place = lax.axis_index("space")
    rep = lax.axis_index("rep")
    copy = 2 * lax.axis_index("dp") + rep
    where = jnp.stack([(place - k) % 4 for k in range(4)] + [copy ^ k for k in range(4)])
    turned = second_kernel.T
    before, after = neighbours(grid[:1], grid[-1:])
    piece = lax.dynamic_slice_in_dim(turned, copy * (share // 4), share // 4, 0)
    others = [turn(piece, "space", k) for k in range(1, 4)]
    blocks = head_weights.T.reshape(outs, 4, share)
    head = jnp.concatenate([lax.dynamic_index_in_dim(blocks, (place - k) % 4, 1, False) for k in range(4)], axis=1)
    head = jnp.pad(head, ((0, 8 - outs), (0, 0)))
    wanted = jnp.pad(jnp.broadcast_to(targets[0][:, None], (outs, 128)), ((0, 8 - outs), (0, 0)))
    pooled, slope = run_first_forward(grid, before, after, first_kernel)
    pooled, *others = lax.optimization_barrier([pooled] + others)
    others = run_join(others)
    across = turn(others, "dp", 1)
    parts = [pooled] + [turn(pooled, "space", k) for k in range(1, 4)]
    across, *parts = lax.optimization_barrier([across] + parts)
    pieces = [others, turn(others, "rep", 1), across, turn(across, "rep", 1)]
    pooled_grad, own, result = run_second_layer(where, parts, turned, pieces, head, wanted)
    keep, send = run_first_backward(grid, before, after, pooled_grad, slope, rep[None])
    keep, send = run_merge_half(lax.axis_index("dp")[None], keep, turn(send, "rep", 1))
    arrived = turn(send, "dp", 1)
    keep, own = lax.optimization_barrier((keep, own))
    kept, sent = run_second_backward(where, parts, own, result, rep[None])
    x, *sends = run_merge_blocks(place[None], keep, arrived)
    sends[0], sends[1], sends[2], kept, sent = lax.optimization_barrier((*sends, kept, sent))
    second = kept + turn(sent, "rep", 1)
    for k in (1, 3, 2):
        x = x + turn(sends[k - 1], "space", k).astype(f32)
    x = x.astype(bf16)
    second = second + turn(second, "dp", 1)
    whole = jnp.zeros((4,) + x.shape, bf16)
    for k in (0, 1, 3, 2):
        part = turn(x, "space", k) if k else x
        if k == 1:
            part, second = lax.optimization_barrier((part, second))
        whole = lax.dynamic_update_index_in_dim(whole, part, (place - k) % 4, 0)
    x = whole.reshape(-1, x.shape[1])
    second = gathered(second, "rep").reshape(-1, second.shape[1])
    second_total, head_total = run_spread_second(second, share, outs)
    for axis in ("dp", "rep"):
        x = gathered(x, axis).reshape(-1, x.shape[1])
    first_total = x.astype(f32)
    return (first_total, second_total.T, head_total.T)


def solution(mesh):
    in_specs = (
        P(("groups", "dp", "rep"), "space", None, None, None),
        P(("groups", "dp", "rep"), None),
        P(),
        P(None, "space"),
        P(),
    )
    out_specs = (P("groups", None), P("groups", "space"), P(("groups", "space"), None))
    return jax.shard_map(shards, mesh=mesh, in_specs=in_specs, out_specs=out_specs, check_vma=False)
```

```python
import jax
import jax.numpy as jnp
from jax import lax
from jax.experimental import pallas as pl
from jax.experimental.pallas import tpu as pltpu
from jax.sharding import PartitionSpec as P

leak_slope = 0.3
log_two = 0.6931471805599453
direct_most = 4
f32, bf16 = jnp.float32, jnp.bfloat16
front = 8
heavy = 10**9


def call(body, outs, scratch, *args, smem=(), away=(), work=0, room=16, far_outs=()):
    spaces = [pltpu.SMEM if k in smem else pltpu.HBM if k in away else pltpu.VMEM for k in range(len(args))]
    specs = [pl.BlockSpec(memory_space=space) for space in spaces]
    one = not isinstance(outs, tuple)
    out_specs = [
        pl.BlockSpec(memory_space=pltpu.HBM if k in far_outs else pltpu.VMEM) for k in range(1 if one else len(outs))
    ]
    out_specs = out_specs[0] if one else tuple(out_specs)
    return pl.pallas_call(
        body,
        out_shape=outs,
        in_specs=specs,
        out_specs=out_specs,
        scratch_shapes=scratch,
        compiler_params=pltpu.CompilerParams(vmem_limit_bytes=room * 2**20),
        cost_estimate=pl.CostEstimate(flops=work, bytes_accessed=0, transcendentals=0),
    )(*args)


def slope_and_activation(value):
    shrunk = jnp.exp(-jnp.abs(value))
    inverse = 1.0 / (1.0 + shrunk)
    slope = leak_slope + (1.0 - leak_slope) * jnp.where(value >= 0, inverse, shrunk * inverse)
    soft = jnp.maximum(value, 0.0) + jnp.log(1.0 + shrunk)
    return slope, leak_slope * value + (1.0 - leak_slope) * (soft - log_two)


def shifted(rows_ref, length, step):
    return rows_ref[front + step : front + step + length, :]


def lay_plane(plane, rows_ref, wide):
    rows, cols, chans = plane.shape
    for h in range(rows):
        rows_ref[front + h * wide : front + h * wide + cols, :] = plane[h].astype(f32)


def wide_plane(source, rows_ref, target, top, wide):
    rows, chans = source.shape[0], source.shape[2]
    lay_plane(source, rows_ref, wide)
    for e in range(3):
        target[top : top + rows * wide, e * chans : (e + 1) * chans] = shifted(
            rows_ref, rows * wide, e - 1
        ).astype(bf16)


def first_forward(vol, before, after, kernel, pooled, slope, u, rows_ref, pairs, acc, half, dense):
    depth, rows, cols, chans = vol.shape
    wide = 32
    cells = rows * wide
    outs = kernel.shape[1]
    span = 3 * chans
    rows_ref[...] = jnp.zeros_like(rows_ref)
    edge = jnp.zeros((u.shape[0], wide, span), bf16)
    u[:, 0:wide, :] = edge
    u[:, wide + cells :, :] = edge
    for p in range(depth + 2):
        if p == 0:
            source = before[0]
        elif p == depth + 1:
            source = after[0]
        else:
            source = vol[p - 1]
        wide_plane(source, rows_ref, u.at[p], wide, wide)

    def tap(a, b):
        return kernel[(9 * a + 3 * b) * chans : (9 * a + 3 * b) * chans + span, :]

    for b in range(3):
        pairs[b, 0:span, 0:outs] = tap(1, b)
        pairs[b, 0:span, outs:] = tap(0, b)
        pairs[b, span:, 0:outs] = tap(2, b)
        pairs[b, span:, outs:] = tap(1, b)
    first_taps = jnp.concatenate([tap(0, b) for b in range(3)], axis=0)
    last_taps = jnp.concatenate([tap(2, b) for b in range(3)], axis=0)

    def one_pair(t, carry):
        def window(q, b):
            return u[2 * t + q, b * wide : b * wide + cells, :]

        left = jnp.concatenate([window(0, b) for b in range(3)], axis=1)
        acc[:, 0:outs] = jnp.dot(left, first_taps, preferred_element_type=f32)
        right = jnp.concatenate([window(3, b) for b in range(3)], axis=1)
        acc[:, outs:] = jnp.dot(right, last_taps, preferred_element_type=f32)
        for b in range(3):
            both = jnp.concatenate([window(1, b), window(2, b)], axis=1)
            acc[...] += jnp.dot(both, pairs[b], preferred_element_type=f32)
        for h in range(rows // 2):
            part = acc[h * 2 * wide : (h + 1) * 2 * wide, :]
            slopes, values = slope_and_activation(part)
            slope[2 * t, h * 2 * wide : (h + 1) * 2 * wide, :] = slopes[:, 0:outs]
            slope[2 * t + 1, h * 2 * wide : (h + 1) * 2 * wide, :] = slopes[:, outs:]
            values = values[:, 0:outs] + values[:, outs:]
            half[h * wide : (h + 1) * wide, :] = values[0:wide] + values[wide:]
        for h in range(rows // 2):
            even = half[pl.ds(h * wide, cols // 2, stride=2), :]
            odd = half[pl.ds(h * wide + 1, cols // 2, stride=2), :]
            dense[t, h * (cols // 2) : (h + 1) * (cols // 2), :] = (even + odd) * 0.125
        return carry

    lax.fori_loop(0, depth // 2, one_pair, 0)
    pooled[...] = dense[...].astype(bf16)


def run_first_forward(vol, before, after, kernel):
    depth, rows, cols, chans = vol.shape
    wide, outs = 32, kernel.shape[1]
    cells = rows * wide
    return call(
        first_forward,
        (
            jax.ShapeDtypeStruct((depth // 2, rows * cols // 4, outs), bf16),
            jax.ShapeDtypeStruct((depth, cells, outs), f32),
        ),
        [
            pltpu.VMEM((depth + 2, cells + 2 * wide, 3 * chans), bf16),
            pltpu.VMEM((cells + 2 * front, chans), f32),
            pltpu.VMEM((3, 6 * chans, 2 * outs), bf16),
            pltpu.VMEM((cells, 2 * outs), f32),
            pltpu.VMEM((cells // 2, outs), f32),
            pltpu.VMEM((depth // 2, rows * cols // 4, outs), f32),
        ],
        vol, before, after, kernel, work=heavy * 8,
    )


def first_backward(vol, before, after, spread, slope, keep, send, u, rows_ref, g, acc, twice):
    depth, rows, cols, chans = vol.shape
    wide = 32
    cells = rows * wide
    outs = slope.shape[2]
    rows_ref[...] = jnp.zeros_like(rows_ref)
    for p in range(depth + 2):
        if p == 0:
            source = before[0]
        elif p == depth + 1:
            source = after[0]
        else:
            source = vol[p - 1]
        wide_plane(source, rows_ref, u.at[p], 0, wide)
    edge = jnp.zeros((depth, wide, outs), bf16)
    g[:, 0:wide, :] = edge
    g[:, wide + cells :, :] = edge
    for d in range(depth):
        if d % 2 == 0:
            values = spread[d // 2] * 0.125
            twice[pl.ds(0, cells // 4, stride=2), :] = values
            twice[pl.ds(1, cells // 4, stride=2), :] = values
        for h in range(rows):
            some = twice[(h // 2) * wide : (h // 2 + 1) * wide, :] * slope[d, h * wide : (h + 1) * wide, :]
            g[d, (h + 1) * wide : (h + 2) * wide, :] = some.astype(bf16)
    started = set()
    for p in range(depth + 2):
        taps = [a for a in range(3) if 0 <= p - a < depth]
        rhs = jnp.concatenate(
            [g[p - a, (2 - b) * wide : (2 - b) * wide + cells, :] for a in taps for b in range(3)], axis=1
        )
        part = lax.dot_general(u[p], rhs, (((0,), (0,)), ((), ())), preferred_element_type=f32)
        for place, a in enumerate(taps):
            block = part[:, place * 3 * outs : (place + 1) * 3 * outs]
            lanes = slice(a * 3 * outs, (a + 1) * 3 * outs)
            if a in started:
                acc[:, lanes] += block
            else:
                acc[:, lanes] = block
                started.add(a)
    length = keep.shape[0]

    def write(first, second):
        for a in range(3):
            for b in range(3):
                for e in range(3):
                    top = (9 * a + 3 * b + e) * chans
                    lanes = slice((3 * a + b) * outs, (3 * a + b + 1) * outs)
                    cut = min(max(length - top, 0), chans)
                    if cut > 0:
                        first[top : top + cut, :] = acc[e * chans : e * chans + cut, lanes]
                    if cut < chans:
                        low = top + cut - length
                        second[low : low + chans - cut, :] = acc[e * chans + cut : (e + 1) * chans, lanes]

    @pl.when(lax.axis_index("rep") == 0)
    def _():
        write(keep, send)

    @pl.when(lax.axis_index("rep") != 0)
    def _():
        write(send, keep)


def run_first_backward(vol, before, after, spread, slope):
    depth, rows, cols, chans = vol.shape
    wide, outs = 32, slope.shape[2]
    cells = rows * wide
    return call(
        first_backward,
        (jax.ShapeDtypeStruct((27 * chans // 2, outs), f32),) * 2,
        [
            pltpu.VMEM((depth + 2, cells, 3 * chans), bf16),
            pltpu.VMEM((cells + 2 * front, chans), f32),
            pltpu.VMEM((depth, cells + 2 * wide, outs), bf16),
            pltpu.VMEM((3 * chans, 9 * outs), f32),
            pltpu.VMEM((cells // 2, outs), f32),
        ],
        vol, before, after, spread, slope, work=heavy * 7,
    )


def positions():
    place = lax.axis_index("space")
    copy = 2 * lax.axis_index("dp") + lax.axis_index("rep")
    return [(place + 4 - k) % 4 for k in range(4)] + [copy ^ k for k in range(4)]


def lay_pooled(parts, places, flat, rows_ref, target, top, side, wide):
    chans = target.shape[2] // 3
    cells = side * wide
    for part, place in zip(parts, places):
        for d in range(part.shape[0]):
            flat[...] = part[d].astype(f32)
            for h in range(side):
                rows_ref[front + h * wide : front + h * wide + side, :] = flat[h * side : (h + 1) * side, :]
            for e in range(3):
                target[place + d, top : top + cells, e * chans : (e + 1) * chans] = shifted(
                    rows_ref, cells, e - 1
                ).astype(bf16)


def second_layer(
    p0, p1, p2, p3, w0, w1, w2, w3, w4, head, wanted,
    pooled_grad, own, result, p, flat, rows_ref, w, acc, slopes, shift_ref, g,
):
    parts, pieces = (p0, p1, p2, p3), (w1, w2, w3, w4)
    where = positions()
    planes, area, chans = p0.shape
    side, wide = 12, 16
    cells = side * wide
    depth = planes * len(parts)
    outs = w.shape[0]
    rows_ref[...] = jnp.zeros_like(rows_ref)
    p[0] = jnp.zeros(p.shape[1:], bf16)
    p[depth + 1] = jnp.zeros(p.shape[1:], bf16)
    edge = jnp.zeros((depth + 2, wide, 3 * chans), bf16)
    p[:, 0:wide, :] = edge
    p[:, wide + cells :, :] = edge
    lay_pooled(parts, [1 + planes * where[k] for k in range(4)], flat, rows_ref, p, wide, side, wide)
    share = w0.shape[0]
    quarter = share // 4
    w[0:share, :] = w0[...]
    for k in range(1, 4):
        for j in range(4):
            at = pl.multiple_of(k * share + where[4 + j] * quarter, quarter)
            w[pl.ds(at, quarter), :] = pieces[j][(k - 1) * quarter : k * quarter, :]
    column = lax.broadcasted_iota(jnp.int32, (cells, outs), 0) % wide
    inside = column < side
    step = depth // 2
    slopes[0] = jnp.zeros((cells, outs), f32)
    slopes[depth + 1] = jnp.zeros((cells, outs), f32)

    def half(t, total):
        for a in range(3):
            lhs = jnp.concatenate(
                [
                    p[pl.ds(t * step + a, step), b * wide : b * wide + cells, :].reshape(step * cells, 3 * chans)
                    for b in range(3)
                ],
                axis=1,
            )
            part = lax.dot_general(
                lhs, w[:, 9 * a * chans : 9 * (a + 1) * chans], (((1,), (1,)), ((), ())), preferred_element_type=f32
            )
            if a == 0:
                acc[...] = part
            else:
                acc[...] += part
        for d in range(step):
            slope, value = slope_and_activation(acc[d * cells : (d + 1) * cells, :])
            slopes[t * step + d + 1] = jnp.where(inside, slope, 0.0)
            value = jnp.where(inside, value, 0.0)
            total = total + value.reshape(cells // 8, 8, outs).sum(axis=0)
        return total

    total = lax.fori_loop(0, 2, half, jnp.zeros((8, outs), f32))
    feature = total.sum(axis=0, keepdims=True) / float(depth * area)
    natural = [head[:, k * share : (k + 1) * share] for k in range(4)]
    turned = []
    for k in range(4):
        block = natural[0]
        for j in range(1, 4):
            block = jnp.where(where[k] == j, natural[j], block)
        turned.append(block)
    head = jnp.concatenate(turned, axis=1)
    count = head.shape[0]
    predicted = jnp.sum(feature * head, axis=1, keepdims=True)
    row = lax.broadcasted_iota(jnp.int32, (count, 1), 0)
    target = jnp.zeros((count, 1), f32)
    for k in range(count):
        target = jnp.where(row == k, wanted[0, k], target)
    error = predicted - target
    result[...] = error * feature
    scale = jnp.sum(head * error, axis=0, keepdims=True)
    for d in range(depth):
        own[d] = (slopes[d + 1, :, 0:share] * scale[:, 0:share]).astype(bf16)
    shift_ref[...] = jnp.zeros_like(shift_ref)
    rim = jnp.zeros((planes + 2, wide, outs), bf16)
    for e in range(3):
        g[e, :, 0:wide, :] = rim
        g[e, :, wide + cells :, :] = rim
    for k in range(planes + 2):
        shift_ref[front : front + cells, :] = (slopes[where[0] * planes + k] * scale).astype(bf16).astype(f32)
        for e in range(3):
            g[e, k, wide : wide + cells, :] = shifted(shift_ref, cells, 1 - e).astype(bf16)
    out = jnp.zeros((planes * cells, chans), f32)
    for a in range(3):
        for b in range(3):
            for e in range(3):
                lhs = g[e, 2 - a : 2 - a + planes, (2 - b) * wide : (2 - b) * wide + cells, :].reshape(planes * cells, outs)
                t = 9 * a + 3 * b + e
                out = out + jnp.dot(lhs, w[:, t * chans : (t + 1) * chans], preferred_element_type=f32)
    keep = lax.broadcasted_iota(jnp.int32, (planes * cells, chans), 0) % wide < side
    pooled_grad[...] = jnp.where(keep, out, 0.0).reshape(planes, cells, chans)


def run_second_layer(parts, part_kernel, pieces, head, wanted):
    planes, area, chans = parts[0].shape
    side, wide = 12, 16
    cells = side * wide
    depth = planes * 4
    share, taps = part_kernel.shape
    outs = 4 * share
    return call(
        second_layer,
        (
            jax.ShapeDtypeStruct((planes, cells, chans), f32),
            jax.ShapeDtypeStruct((depth, cells, share), bf16),
            jax.ShapeDtypeStruct((head.shape[0], outs), f32),
        ),
        [
            pltpu.VMEM((depth + 2, cells + 2 * wide, 3 * chans), bf16),
            pltpu.VMEM((area, chans), f32),
            pltpu.VMEM((cells + 2 * front, chans), f32),
            pltpu.VMEM((outs, taps), bf16),
            pltpu.VMEM((depth // 2 * cells, outs), f32),
            pltpu.VMEM((depth + 2, cells, outs), f32),
            pltpu.VMEM((cells + 2 * front, outs), f32),
            pltpu.VMEM((3, planes + 2, cells + 2 * wide, outs), bf16),
        ],
        *parts, part_kernel, *pieces, head, wanted, smem=(10,), work=heavy * 8,
    )


def second_backward(p0, p1, p2, p3, own, result, keep, send, p, flat, rows_ref, g, grad):
    parts = (p0, p1, p2, p3)
    where = positions()
    planes, area, chans = p0.shape
    side, wide = 12, 16
    cells = side * wide
    depth = planes * len(parts)
    share = own.shape[2]
    rows_ref[...] = jnp.zeros_like(rows_ref)
    p[0] = jnp.zeros(p.shape[1:], bf16)
    p[depth + 1] = jnp.zeros(p.shape[1:], bf16)
    lay_pooled(parts, [1 + planes * where[k] for k in range(4)], flat, rows_ref, p, 0, side, wide)
    none = jnp.zeros((depth, wide, share), bf16)
    for b in range(3):
        lanes = slice(b * share, (b + 1) * share)
        if b == 0:
            g[:, 0 : cells - wide, lanes] = own[:, wide:cells, :]
            g[:, cells - wide :, lanes] = none
        elif b == 1:
            g[:, :, lanes] = own[...]
        else:
            g[:, wide:, lanes] = own[:, 0 : cells - wide, :]
            g[:, 0:wide, lanes] = none
    rhs = g[...].reshape(depth * cells, 3 * share)
    for a in range(3):
        lhs = p[a : a + depth].reshape(depth * cells, 3 * chans)
        part = lax.dot_general(rhs, lhs, (((0,), (0,)), ((), ())), preferred_element_type=f32)
        for b in range(3):
            for e in range(3):
                t = 9 * a + 3 * b + e
                block = part[b * share : (b + 1) * share, e * chans : (e + 1) * chans]
                grad[t * share : (t + 1) * share, :] = block
    grad[27 * share :, :] = jnp.zeros((16, chans), f32)
    grad[27 * share : 27 * share + result.shape[0], :] = result[:, 0:chans]
    half = keep.shape[0]
    low = pl.multiple_of(lax.axis_index("rep") * half, 8)
    keep[...] = grad[pl.ds(low, half), :]
    send[...] = grad[pl.ds(pl.multiple_of(half - low, 8), half), :]


def run_second_backward(parts, own, result):
    planes, area, chans = parts[0].shape
    depth, cells, share = own.shape
    return call(
        second_backward,
        (jax.ShapeDtypeStruct((27 * share // 2 + 8, chans), f32),) * 2,
        [
            pltpu.VMEM((depth + 2, cells, 3 * chans), bf16),
            pltpu.VMEM((area, chans), f32),
            pltpu.VMEM((cells + 2 * front, chans), f32),
            pltpu.VMEM((depth, cells, 3 * share), bf16),
            pltpu.VMEM((27 * share + 16, chans), f32),
        ],
        *parts, own, result, work=heavy * 4,
    )


def entry(vol, kernel, other, first, last, piece):
    rows = piece.shape[0]
    copy = 2 * lax.axis_index("dp") + lax.axis_index("rep")
    piece[...] = kernel[pl.ds(pl.multiple_of(copy * rows, rows), rows), :]
    first[0] = vol[0]
    last[0] = vol[vol.shape[0] - 1]


def run_entry(vol, kernel, other):
    plane = jax.ShapeDtypeStruct((1,) + vol.shape[1:], bf16)
    piece = jax.ShapeDtypeStruct((kernel.shape[0] // 4, kernel.shape[1]), bf16)
    return call(entry, (plane, plane, piece), [], vol, kernel, other)


def join(r0, r1, r2, out):
    rows = r0.shape[0]
    for k, r in enumerate((r0, r1, r2)):
        out[k * rows : (k + 1) * rows, :] = r[...]


def run_join(parts):
    rows, cols = parts[0].shape
    return call(join, jax.ShapeDtypeStruct((3 * rows, cols), bf16), [], *parts)


def merge_half(kept, came, keep, send):
    half = keep.shape[0]
    low = pl.multiple_of(lax.axis_index("dp") * half, 8)
    high = pl.multiple_of(half - low, 8)
    keep[...] = kept[pl.ds(low, half), :] + came[pl.ds(low, half), :]
    send[...] = (kept[pl.ds(high, half), :] + came[pl.ds(high, half), :]).astype(bf16)


def run_merge_half(kept, came):
    rows, cols = kept.shape
    outs = tuple(jax.ShapeDtypeStruct((rows // 2, cols), kind) for kind in (f32, bf16))
    return call(merge_half, outs, [], kept, came)


def merge_blocks(kept, came, keep, s1, s2, s3):
    size = keep.shape[0]

    def block(step):
        low = pl.multiple_of((lax.axis_index("space") + step) % 4 * size, 8)
        return kept[pl.ds(low, size), :] + came[pl.ds(low, size), :].astype(f32)

    keep[...] = block(0)
    for step, send in ((1, s1), (2, s2), (3, s3)):
        send[...] = block(step).astype(bf16)


def run_merge_blocks(kept, came):
    rows, cols = kept.shape
    outs = tuple(jax.ShapeDtypeStruct((rows // 4, cols), kind) for kind in (f32, bf16, bf16, bf16))
    return call(merge_blocks, outs, [], kept, came)


def spread_second(packed, out, head):
    chans = packed.shape[1]
    share = out.shape[0]
    for t in range(27):
        out[:, t * chans : (t + 1) * chans] = packed[t * share : (t + 1) * share, :]
    head[...] = packed[27 * share : 27 * share + head.shape[0], 0:share]


def run_spread_second(packed, share, outs):
    rows, chans = packed.shape
    return call(
        spread_second,
        (jax.ShapeDtypeStruct((share, 27 * chans), f32), jax.ShapeDtypeStruct((outs, share), f32)),
        [],
        packed,
        work=heavy * 2,
    )


def turn(x, axis, step):
    size = lax.axis_size(axis)
    return lax.ppermute(x, axis, [(i, (i + step) % size) for i in range(size)])


def paired(x, axis, bits):
    return lax.ppermute(x, axis, [(i, i ^ bits) for i in range(lax.axis_size(axis))])


def direct(axis):
    return lax.axis_size(axis) <= direct_most


def gathered(x, axis):
    if not direct(axis):
        return lax.all_gather(x, axis)
    size, place = lax.axis_size(axis), lax.axis_index(axis)
    parts = [x] + [turn(x, axis, step) for step in range(1, size)]
    out = jnp.zeros((size,) + x.shape, x.dtype)
    for step, part in enumerate(parts):
        out = lax.dynamic_update_index_in_dim(out, part, (place - step) % size, 0)
    return out


def scattered_sum(x, axis, wire):
    size, place = lax.axis_size(axis), lax.axis_index(axis)
    blocks = x.reshape((size, x.shape[0] // size) + x.shape[1:])
    if not direct(axis):
        return lax.psum_scatter(blocks, axis)
    total = lax.dynamic_index_in_dim(blocks, place, 0, False)
    for step in range(1, size):
        sent = lax.dynamic_index_in_dim(blocks, (place + step) % size, 0, False).astype(wire)
        total = total + turn(sent, axis, step).astype(jnp.float32)
    return total


def total_first(x):
    columns = x.shape[1]
    x = scattered_sum(x, "rep", jnp.float32)
    x = scattered_sum(x, "dp", jnp.bfloat16)
    if direct("space"):
        x = scattered_sum(x, "space", jnp.bfloat16).astype(jnp.bfloat16)
        x = gathered(x, "space").reshape(-1, columns)
    else:
        x = lax.psum(x, "space").astype(jnp.bfloat16)
    x = gathered(x, "dp").reshape(-1, columns)
    x = gathered(x, "rep").reshape(-1, columns)
    return x.astype(jnp.float32)


def total_second(x):
    columns = x.shape[1]
    x = scattered_sum(x, "rep", jnp.float32)
    if direct("dp"):
        x = gathered(x, "dp").sum(0)
    else:
        x = lax.psum(x, "dp")
    return gathered(x, "rep").reshape(-1, columns)


def whole_kernel(part):
    rows, share = part.shape
    copies = [axis for axis in ("dp", "rep")]
    pieces, place = (1, 0)
    for axis in copies:
        place = place * lax.axis_size(axis) + lax.axis_index(axis)
        pieces = pieces * lax.axis_size(axis)
    length = rows // pieces
    piece = lax.dynamic_slice_in_dim(part, place * length, length, 0)
    packed = jnp.concatenate([piece[: length // 2], piece[length // 2 :]], axis=1)
    packs = gathered(packed, "space")
    upper = jnp.moveaxis(packs[:, :, :share], 0, 1).reshape(length // 2, -1)
    lower = jnp.moveaxis(packs[:, :, share:], 0, 1).reshape(length // 2, -1)
    wide = jnp.concatenate([upper, lower], axis=0)
    wide = gathered(wide, "dp")
    wide = jnp.moveaxis(gathered(wide, "rep"), 0, 1)
    return wide.reshape(rows, -1)


def extended_2(x, sides, width):
    for axis, dim in sides:
        devices, length = (lax.axis_size(axis), x.shape[dim])
        up = [(i, (i + 1) % devices) for i in range(devices - 1)]
        down = [(j, i) for i, j in up]
        last = lax.slice_in_dim(x, length - width, length, axis=dim)
        leading = lax.slice_in_dim(x, 0, width, axis=dim)
        before = lax.ppermute(last, axis, up)
        after = lax.ppermute(leading, axis, down)
        x = jnp.concatenate([before, x, after], axis=dim)
    return x


def activate(value):
    return leak_slope * value + (1.0 - leak_slope) * (jax.nn.softplus(value) - log_two)


def activate_slope(value):
    return leak_slope + (1.0 - leak_slope) * jax.nn.sigmoid(value)


def convolve(extended, kernel):
    result = lax.conv_general_dilated(
        extended[None],
        kernel,
        (1, 1, 1),
        [(0, 0), (1, 1), (1, 1)],
        dimension_numbers=("NDHWC", "DHWIO", "NDHWC"),
        preferred_element_type=jnp.float32,
    )
    return result[0]


def pooling(grid):
    depth, rows, cols, chans = grid.shape
    return grid.reshape(depth // 2, 2, rows // 2, 2, cols // 2, 2, chans).mean(axis=(1, 3, 5))


def expand(grid):
    depth, rows, cols, chans = grid.shape
    spread = jnp.broadcast_to(
        grid[:, None, :, None, :, None, :], (depth, 2, rows, 2, cols, 2, chans)
    )
    return spread.reshape(depth * 2, rows * 2, cols * 2, chans) / 8.0


def kernel_grad(extended, grad):
    widened = jnp.pad(extended, ((0, 0), (1, 1), (1, 1), (0, 0)))
    result = lax.conv_general_dilated(
        widened[..., None],
        grad[:, :, :, None, :],
        (1, 1, 1),
        "VALID",
        dimension_numbers=("DHWNC", "DHWIO", "NDHWC"),
        preferred_element_type=jnp.float32,
    )
    return jnp.transpose(result, (1, 2, 3, 0, 4)).reshape(-1, grad.shape[-1])


def general_shards(volumes, targets, first_kernel, second_kernel, head_weights):
    grid_in = volumes[0]
    target_row = targets[0]
    channels = grid_in.shape[-1]
    kernel_one = first_kernel.reshape(3, 3, 3, channels, first_kernel.shape[1])
    extended = extended_2(grid_in, (("space", 0),), 1)
    share = second_kernel.shape[1]
    place = lax.axis_index("space")
    kernel_two = whole_kernel(second_kernel).reshape(3, 3, 3, channels, -1)
    before_one = convolve(extended, kernel_one)
    pooled = pooling(activate(before_one)).astype(jnp.bfloat16)
    whole = gathered(pooled, "space").reshape((-1,) + pooled.shape[1:])
    padded_whole = jnp.pad(whole, ((1, 1), (0, 0), (0, 0), (0, 0)))
    before_two = convolve(padded_whole, kernel_two)
    feature = jnp.mean(activate(before_two), axis=(0, 1, 2))
    predicted = jnp.dot(feature, head_weights, precision=lax.Precision.HIGHEST)
    error = predicted - target_row
    feature_part = lax.dynamic_slice_in_dim(feature, place * share, share, 0)
    head_grad = feature_part[:, None] * error[None, :]
    feature_grad = jnp.dot(head_weights, error, precision=lax.Precision.HIGHEST)
    grad_two = (feature_grad * activate_slope(before_two)).astype(jnp.bfloat16)
    padded_grad = jnp.pad(grad_two, ((1, 1), (0, 0), (0, 0), (0, 0)))
    flipped = jnp.swapaxes(kernel_two[::-1, ::-1, ::-1], 3, 4)
    planes = pooled.shape[0]
    window = lax.dynamic_slice_in_dim(padded_grad, place * planes, planes + 2, 0)
    pooled_grad = convolve(window, flipped)
    grad_one = (expand(pooled_grad) * activate_slope(before_one)).astype(jnp.bfloat16)
    first_total = total_first(kernel_grad(extended, grad_one))
    grad_part = lax.dynamic_slice_in_dim(grad_two, place * share, share, 3)
    second_part = kernel_grad(padded_whole, grad_part)
    rows = second_part.shape[0]
    packed = jnp.concatenate([second_part[: rows // 2], second_part[rows // 2 :]], axis=1)
    packed = total_second(packed)
    second_total = jnp.concatenate([packed[:, :share], packed[:, share:]], axis=0)
    head_total = gathered(gathered(head_grad, "rep").sum(0), "dp").sum(0)
    return (first_total, second_total, head_total)


def neighbours(first, last):
    devices = lax.axis_size("space")
    up = [(i, i + 1) for i in range(devices - 1)]
    down = [(j, i) for i, j in up]
    before = lax.ppermute(last, "space", up)
    after = lax.ppermute(first, "space", down)
    return before, after


def shards(volumes, targets, first_kernel, second_kernel, head_weights):
    sizes = tuple(lax.axis_size(axis) for axis in ("space", "dp", "rep"))
    if sizes != (4, 2, 2):
        return general_shards(volumes, targets, first_kernel, second_kernel, head_weights)
    grid = volumes[0]
    share = second_kernel.shape[1]
    outs = head_weights.shape[1]
    place = lax.axis_index("space")
    turned = second_kernel.T
    before, after = neighbours(grid[:1], grid[-1:])
    copy = 2 * lax.axis_index("dp") + lax.axis_index("rep")
    piece = lax.dynamic_slice_in_dim(turned, copy * (share // 4), share // 4, 0)
    others = [turn(piece, "space", k) for k in range(1, 4)]
    pooled, slope = run_first_forward(grid, before, after, first_kernel)
    pooled, *others = lax.optimization_barrier([pooled] + others)
    others = run_join(others)
    across = turn(others, "dp", 1)
    parts = [pooled] + [turn(pooled, "space", k) for k in range(1, 4)]
    across, *parts = lax.optimization_barrier([across] + parts)
    pieces = [others, turn(others, "rep", 1), across, turn(across, "rep", 1)]
    pooled_grad, own, result = run_second_layer(parts, turned, pieces, head_weights.T, targets)
    keep, send = run_first_backward(grid, before, after, pooled_grad, slope)
    keep, send = run_merge_half(keep, turn(send, "rep", 1))
    arrived = turn(send, "dp", 1)
    kept, sent = run_second_backward(parts, own, result)
    x, *sends = run_merge_blocks(keep, arrived)
    second = kept + turn(sent, "rep", 1)
    *sends, second = lax.optimization_barrier((*sends, second))
    for k in (1, 3, 2):
        x = x + turn(sends[k - 1], "space", k).astype(f32)
    x = x.astype(bf16)
    second = second + turn(second, "dp", 1)
    whole = jnp.zeros((4,) + x.shape, bf16)
    for k in (0, 1, 3, 2):
        part = turn(x, "space", k) if k else x
        if k == 1:
            part, second = lax.optimization_barrier((part, second))
        whole = lax.dynamic_update_index_in_dim(whole, part, (place - k) % 4, 0)
    x = whole.reshape(-1, x.shape[1])
    second = gathered(second, "rep").reshape(-1, second.shape[1])
    second_total, head_total = run_spread_second(second, share, outs)
    for axis in ("dp", "rep"):
        x = gathered(x, axis).reshape(-1, x.shape[1])
    first_total = x.astype(f32)
    return (first_total, second_total.T, head_total.T)


def solution(mesh):
    in_specs = (
        P(("groups", "dp", "rep"), "space", None, None, None),
        P(("groups", "dp", "rep"), None),
        P(),
        P(None, "space"),
        P(),
    )
    out_specs = (P("groups", None), P("groups", "space"), P(("groups", "space"), None))
    return jax.shard_map(shards, mesh=mesh, in_specs=in_specs, out_specs=out_specs, check_vma=False)
```

```python
import jax
import jax.numpy as jnp
from jax import lax
from jax.experimental import pallas as pl
from jax.experimental.pallas import tpu as pltpu
from jax.sharding import PartitionSpec as P

leak_slope = 0.3
log_two = 0.6931471805599453
direct_most = 4
f32, bf16 = jnp.float32, jnp.bfloat16
front = 8
heavy = 10**9


def call(body, outs, scratch, *args, smem=(), away=(), work=0, room=16, far_outs=()):
    spaces = [pltpu.SMEM if k in smem else pltpu.HBM if k in away else pltpu.VMEM for k in range(len(args))]
    specs = [pl.BlockSpec(memory_space=space) for space in spaces]
    one = not isinstance(outs, tuple)
    out_specs = [
        pl.BlockSpec(memory_space=pltpu.HBM if k in far_outs else pltpu.VMEM) for k in range(1 if one else len(outs))
    ]
    out_specs = out_specs[0] if one else tuple(out_specs)
    return pl.pallas_call(
        body,
        out_shape=outs,
        in_specs=specs,
        out_specs=out_specs,
        scratch_shapes=scratch,
        compiler_params=pltpu.CompilerParams(vmem_limit_bytes=room * 2**20),
        cost_estimate=pl.CostEstimate(flops=work, bytes_accessed=0, transcendentals=0),
    )(*args)


def slope_and_activation(value):
    shrunk = jnp.exp(-jnp.abs(value))
    inverse = 1.0 / (1.0 + shrunk)
    slope = leak_slope + (1.0 - leak_slope) * jnp.where(value >= 0, inverse, shrunk * inverse)
    soft = jnp.maximum(value, 0.0) + jnp.log(1.0 + shrunk)
    return slope, leak_slope * value + (1.0 - leak_slope) * (soft - log_two)


def shifted(rows_ref, length, step):
    return rows_ref[front + step : front + step + length, :]


def lay_plane(plane, rows_ref, wide):
    rows, cols, chans = plane.shape
    for h in range(rows):
        rows_ref[front + h * wide : front + h * wide + cols, :] = plane[h].astype(f32)


def wide_plane(source, rows_ref, target, top, wide):
    rows, chans = source.shape[0], source.shape[2]
    lay_plane(source, rows_ref, wide)
    for e in range(3):
        target[top : top + rows * wide, e * chans : (e + 1) * chans] = shifted(
            rows_ref, rows * wide, e - 1
        ).astype(bf16)


def first_forward(vol, before, after, kernel, pooled, slope, u, rows_ref, pairs, acc, half, dense):
    depth, rows, cols, chans = vol.shape
    wide = 32
    cells = rows * wide
    outs = kernel.shape[1]
    span = 3 * chans
    rows_ref[...] = jnp.zeros_like(rows_ref)
    edge = jnp.zeros((u.shape[0], wide, span), bf16)
    u[:, 0:wide, :] = edge
    u[:, wide + cells :, :] = edge
    for p in range(depth + 2):
        if p == 0:
            source = before[0]
        elif p == depth + 1:
            source = after[0]
        else:
            source = vol[p - 1]
        wide_plane(source, rows_ref, u.at[p], wide, wide)

    def tap(a, b):
        return kernel[(9 * a + 3 * b) * chans : (9 * a + 3 * b) * chans + span, :]

    for b in range(3):
        pairs[b, 0:span, 0:outs] = tap(1, b)
        pairs[b, 0:span, outs:] = tap(0, b)
        pairs[b, span:, 0:outs] = tap(2, b)
        pairs[b, span:, outs:] = tap(1, b)
    first_taps = jnp.concatenate([tap(0, b) for b in range(3)], axis=0)
    last_taps = jnp.concatenate([tap(2, b) for b in range(3)], axis=0)

    def one_pair(t, carry):
        def window(q, b):
            return u[2 * t + q, b * wide : b * wide + cells, :]

        left = jnp.concatenate([window(0, b) for b in range(3)], axis=1)
        acc[:, 0:outs] = jnp.dot(left, first_taps, preferred_element_type=f32)
        right = jnp.concatenate([window(3, b) for b in range(3)], axis=1)
        acc[:, outs:] = jnp.dot(right, last_taps, preferred_element_type=f32)
        for b in range(3):
            both = jnp.concatenate([window(1, b), window(2, b)], axis=1)
            acc[...] += jnp.dot(both, pairs[b], preferred_element_type=f32)
        for h in range(rows // 2):
            part = acc[h * 2 * wide : (h + 1) * 2 * wide, :]
            slopes, values = slope_and_activation(part)
            slope[2 * t, h * 2 * wide : (h + 1) * 2 * wide, :] = slopes[:, 0:outs]
            slope[2 * t + 1, h * 2 * wide : (h + 1) * 2 * wide, :] = slopes[:, outs:]
            values = values[:, 0:outs] + values[:, outs:]
            half[h * wide : (h + 1) * wide, :] = values[0:wide] + values[wide:]
        for h in range(rows // 2):
            even = half[pl.ds(h * wide, cols // 2, stride=2), :]
            odd = half[pl.ds(h * wide + 1, cols // 2, stride=2), :]
            dense[t, h * (cols // 2) : (h + 1) * (cols // 2), :] = (even + odd) * 0.125
        return carry

    lax.fori_loop(0, depth // 2, one_pair, 0)
    pooled[...] = dense[...].astype(bf16)


def run_first_forward(vol, before, after, kernel):
    depth, rows, cols, chans = vol.shape
    wide, outs = 32, kernel.shape[1]
    cells = rows * wide
    return call(
        first_forward,
        (
            jax.ShapeDtypeStruct((depth // 2, rows * cols // 4, outs), bf16),
            jax.ShapeDtypeStruct((depth, cells, outs), f32),
        ),
        [
            pltpu.VMEM((depth + 2, cells + 2 * wide, 3 * chans), bf16),
            pltpu.VMEM((cells + 2 * front, chans), f32),
            pltpu.VMEM((3, 6 * chans, 2 * outs), bf16),
            pltpu.VMEM((cells, 2 * outs), f32),
            pltpu.VMEM((cells // 2, outs), f32),
            pltpu.VMEM((depth // 2, rows * cols // 4, outs), f32),
        ],
        vol, before, after, kernel, work=heavy * 8,
    )


def first_backward(vol, before, after, spread, slope, keep, send, u, rows_ref, g, acc, twice):
    depth, rows, cols, chans = vol.shape
    wide = 32
    cells = rows * wide
    outs = slope.shape[2]
    rows_ref[...] = jnp.zeros_like(rows_ref)
    for p in range(depth + 2):
        if p == 0:
            source = before[0]
        elif p == depth + 1:
            source = after[0]
        else:
            source = vol[p - 1]
        wide_plane(source, rows_ref, u.at[p], 0, wide)
    edge = jnp.zeros((depth, wide, outs), bf16)
    g[:, 0:wide, :] = edge
    g[:, wide + cells :, :] = edge
    for d in range(depth):
        if d % 2 == 0:
            values = spread[d // 2] * 0.125
            twice[pl.ds(0, cells // 4, stride=2), :] = values
            twice[pl.ds(1, cells // 4, stride=2), :] = values
        for h in range(rows):
            some = twice[(h // 2) * wide : (h // 2 + 1) * wide, :] * slope[d, h * wide : (h + 1) * wide, :]
            g[d, (h + 1) * wide : (h + 2) * wide, :] = some.astype(bf16)
    started = set()
    for p in range(depth + 2):
        taps = [a for a in range(3) if 0 <= p - a < depth]
        rhs = jnp.concatenate(
            [g[p - a, (2 - b) * wide : (2 - b) * wide + cells, :] for a in taps for b in range(3)], axis=1
        )
        part = lax.dot_general(u[p], rhs, (((0,), (0,)), ((), ())), preferred_element_type=f32)
        for place, a in enumerate(taps):
            block = part[:, place * 3 * outs : (place + 1) * 3 * outs]
            lanes = slice(a * 3 * outs, (a + 1) * 3 * outs)
            if a in started:
                acc[:, lanes] += block
            else:
                acc[:, lanes] = block
                started.add(a)
    length = keep.shape[0]

    def write(first, second):
        for a in range(3):
            for b in range(3):
                for e in range(3):
                    top = (9 * a + 3 * b + e) * chans
                    lanes = slice((3 * a + b) * outs, (3 * a + b + 1) * outs)
                    cut = min(max(length - top, 0), chans)
                    if cut > 0:
                        first[top : top + cut, :] = acc[e * chans : e * chans + cut, lanes]
                    if cut < chans:
                        low = top + cut - length
                        second[low : low + chans - cut, :] = acc[e * chans + cut : (e + 1) * chans, lanes]

    @pl.when(lax.axis_index("rep") == 0)
    def _():
        write(keep, send)

    @pl.when(lax.axis_index("rep") != 0)
    def _():
        write(send, keep)


def run_first_backward(vol, before, after, spread, slope):
    depth, rows, cols, chans = vol.shape
    wide, outs = 32, slope.shape[2]
    cells = rows * wide
    return call(
        first_backward,
        (jax.ShapeDtypeStruct((27 * chans // 2, outs), f32),) * 2,
        [
            pltpu.VMEM((depth + 2, cells, 3 * chans), bf16),
            pltpu.VMEM((cells + 2 * front, chans), f32),
            pltpu.VMEM((depth, cells + 2 * wide, outs), bf16),
            pltpu.VMEM((3 * chans, 9 * outs), f32),
            pltpu.VMEM((cells // 2, outs), f32),
        ],
        vol, before, after, spread, slope, work=heavy * 7,
    )


def positions():
    place = lax.axis_index("space")
    copy = 2 * lax.axis_index("dp") + lax.axis_index("rep")
    return [(place + 4 - k) % 4 for k in range(4)] + [copy ^ k for k in range(4)]


def lay_pooled(parts, places, flat, rows_ref, target, top, side, wide):
    chans = target.shape[2] // 3
    cells = side * wide
    for part, place in zip(parts, places):
        for d in range(part.shape[0]):
            flat[...] = part[d].astype(f32)
            for h in range(side):
                rows_ref[front + h * wide : front + h * wide + side, :] = flat[h * side : (h + 1) * side, :]
            for e in range(3):
                target[place + d, top : top + cells, e * chans : (e + 1) * chans] = shifted(
                    rows_ref, cells, e - 1
                ).astype(bf16)


def second_layer(
    p0, p1, p2, p3, w0, w1, w2, w3, w4, head, wanted,
    pooled_grad, own, result, p, flat, rows_ref, w, acc, slopes, shift_ref, g,
):
    parts, pieces = (p0, p1, p2, p3), (w1, w2, w3, w4)
    where = positions()
    planes, area, chans = p0.shape
    side, wide = 12, 16
    cells = side * wide
    depth = planes * len(parts)
    outs = w.shape[0]
    rows_ref[...] = jnp.zeros_like(rows_ref)
    p[0] = jnp.zeros(p.shape[1:], bf16)
    p[depth + 1] = jnp.zeros(p.shape[1:], bf16)
    edge = jnp.zeros((depth + 2, wide, 3 * chans), bf16)
    p[:, 0:wide, :] = edge
    p[:, wide + cells :, :] = edge
    lay_pooled(parts, [1 + planes * where[k] for k in range(4)], flat, rows_ref, p, wide, side, wide)
    share = w0.shape[0]
    quarter = share // 4
    w[0:share, :] = w0[...]
    for k in range(1, 4):
        for j in range(4):
            at = pl.multiple_of(k * share + where[4 + j] * quarter, quarter)
            w[pl.ds(at, quarter), :] = pieces[j][(k - 1) * quarter : k * quarter, :]
    column = lax.broadcasted_iota(jnp.int32, (cells, outs), 0) % wide
    inside = column < side
    step = depth // 2
    slopes[0] = jnp.zeros((cells, outs), f32)
    slopes[depth + 1] = jnp.zeros((cells, outs), f32)

    def half(t, total):
        for a in range(3):
            lhs = jnp.concatenate(
                [
                    p[pl.ds(t * step + a, step), b * wide : b * wide + cells, :].reshape(step * cells, 3 * chans)
                    for b in range(3)
                ],
                axis=1,
            )
            part = lax.dot_general(
                lhs, w[:, 9 * a * chans : 9 * (a + 1) * chans], (((1,), (1,)), ((), ())), preferred_element_type=f32
            )
            if a == 0:
                acc[...] = part
            else:
                acc[...] += part
        for d in range(step):
            slope, value = slope_and_activation(acc[d * cells : (d + 1) * cells, :])
            slopes[t * step + d + 1] = jnp.where(inside, slope, 0.0)
            value = jnp.where(inside, value, 0.0)
            total = total + value.reshape(cells // 8, 8, outs).sum(axis=0)
        return total

    total = lax.fori_loop(0, 2, half, jnp.zeros((8, outs), f32))
    feature = total.sum(axis=0, keepdims=True) / float(depth * area)
    natural = [head[:, k * share : (k + 1) * share] for k in range(4)]
    turned = []
    for k in range(4):
        block = natural[0]
        for j in range(1, 4):
            block = jnp.where(where[k] == j, natural[j], block)
        turned.append(block)
    head = jnp.concatenate(turned, axis=1)
    count = head.shape[0]
    predicted = jnp.sum(feature * head, axis=1, keepdims=True)
    row = lax.broadcasted_iota(jnp.int32, (count, 1), 0)
    target = jnp.zeros((count, 1), f32)
    for k in range(count):
        target = jnp.where(row == k, wanted[0, k], target)
    error = predicted - target
    result[...] = error * feature
    scale = jnp.sum(head * error, axis=0, keepdims=True)
    for d in range(depth):
        own[d] = (slopes[d + 1, :, 0:share] * scale[:, 0:share]).astype(bf16)
    shift_ref[...] = jnp.zeros_like(shift_ref)
    rim = jnp.zeros((planes + 2, wide, outs), bf16)
    for e in range(3):
        g[e, :, 0:wide, :] = rim
        g[e, :, wide + cells :, :] = rim
    for k in range(planes + 2):
        shift_ref[front : front + cells, :] = (slopes[where[0] * planes + k] * scale).astype(bf16).astype(f32)
        for e in range(3):
            g[e, k, wide : wide + cells, :] = shifted(shift_ref, cells, 1 - e).astype(bf16)
    out = None
    for a in range(3):
        taps = [(b, e) for b in range(3) for e in range(3)]
        lhs = jnp.concatenate(
            [
                g[e, 2 - a : 2 - a + planes, (2 - b) * wide : (2 - b) * wide + cells, :].reshape(planes * cells, outs)
                for b, e in taps
            ],
            axis=1,
        )
        rhs = jnp.concatenate(
            [w[:, (9 * a + 3 * b + e) * chans : (9 * a + 3 * b + e + 1) * chans] for b, e in taps], axis=0
        )
        part = jnp.dot(lhs, rhs, preferred_element_type=f32)
        out = part if out is None else out + part
    keep = lax.broadcasted_iota(jnp.int32, (planes * cells, chans), 0) % wide < side
    pooled_grad[...] = jnp.where(keep, out, 0.0).reshape(planes, cells, chans)


def run_second_layer(parts, part_kernel, pieces, head, wanted):
    planes, area, chans = parts[0].shape
    side, wide = 12, 16
    cells = side * wide
    depth = planes * 4
    share, taps = part_kernel.shape
    outs = 4 * share
    return call(
        second_layer,
        (
            jax.ShapeDtypeStruct((planes, cells, chans), f32),
            jax.ShapeDtypeStruct((depth, cells, share), bf16),
            jax.ShapeDtypeStruct((head.shape[0], outs), f32),
        ),
        [
            pltpu.VMEM((depth + 2, cells + 2 * wide, 3 * chans), bf16),
            pltpu.VMEM((area, chans), f32),
            pltpu.VMEM((cells + 2 * front, chans), f32),
            pltpu.VMEM((outs, taps), bf16),
            pltpu.VMEM((depth // 2 * cells, outs), f32),
            pltpu.VMEM((depth + 2, cells, outs), f32),
            pltpu.VMEM((cells + 2 * front, outs), f32),
            pltpu.VMEM((3, planes + 2, cells + 2 * wide, outs), bf16),
        ],
        *parts, part_kernel, *pieces, head, wanted, smem=(10,), work=heavy * 8,
    )


def second_backward(p0, p1, p2, p3, own, result, keep, send, p, flat, rows_ref, g, grad):
    parts = (p0, p1, p2, p3)
    where = positions()
    planes, area, chans = p0.shape
    side, wide = 12, 16
    cells = side * wide
    depth = planes * len(parts)
    share = own.shape[2]
    rows_ref[...] = jnp.zeros_like(rows_ref)
    p[0] = jnp.zeros(p.shape[1:], bf16)
    p[depth + 1] = jnp.zeros(p.shape[1:], bf16)
    lay_pooled(parts, [1 + planes * where[k] for k in range(4)], flat, rows_ref, p, 0, side, wide)
    none = jnp.zeros((depth, wide, share), bf16)
    for b in range(3):
        lanes = slice(b * share, (b + 1) * share)
        if b == 0:
            g[:, 0 : cells - wide, lanes] = own[:, wide:cells, :]
            g[:, cells - wide :, lanes] = none
        elif b == 1:
            g[:, :, lanes] = own[...]
        else:
            g[:, wide:, lanes] = own[:, 0 : cells - wide, :]
            g[:, 0:wide, lanes] = none
    rhs = g[...].reshape(depth * cells, 3 * share)
    for a in range(3):
        lhs = p[a : a + depth].reshape(depth * cells, 3 * chans)
        part = lax.dot_general(rhs, lhs, (((0,), (0,)), ((), ())), preferred_element_type=f32)
        for b in range(3):
            for e in range(3):
                t = 9 * a + 3 * b + e
                block = part[b * share : (b + 1) * share, e * chans : (e + 1) * chans]
                grad[t * share : (t + 1) * share, :] = block
    grad[27 * share :, :] = jnp.zeros((16, chans), f32)
    grad[27 * share : 27 * share + result.shape[0], :] = result[:, 0:chans]
    half = keep.shape[0]
    low = pl.multiple_of(lax.axis_index("rep") * half, 8)
    keep[...] = grad[pl.ds(low, half), :]
    send[...] = grad[pl.ds(pl.multiple_of(half - low, 8), half), :]


def run_second_backward(parts, own, result):
    planes, area, chans = parts[0].shape
    depth, cells, share = own.shape
    return call(
        second_backward,
        (jax.ShapeDtypeStruct((27 * share // 2 + 8, chans), f32),) * 2,
        [
            pltpu.VMEM((depth + 2, cells, 3 * chans), bf16),
            pltpu.VMEM((area, chans), f32),
            pltpu.VMEM((cells + 2 * front, chans), f32),
            pltpu.VMEM((depth, cells, 3 * share), bf16),
            pltpu.VMEM((27 * share + 16, chans), f32),
        ],
        *parts, own, result, work=heavy * 4,
    )


def entry(vol, first, last):
    first[0] = vol[0]
    last[0] = vol[vol.shape[0] - 1]


def run_entry(vol):
    plane = jax.ShapeDtypeStruct((1,) + vol.shape[1:], bf16)
    return call(entry, (plane, plane), [], vol)


def widen(x, across, near, far, out, room, done):
    rows = x.shape[0]
    own = 2 * lax.axis_index("rep") + lax.axis_index("dp")
    copies = []
    for k, part in enumerate((x, across, near, far)):
        room[k] = part[...].astype(f32)
        to = out.at[pl.ds(pl.multiple_of((own ^ k) * rows, 8), rows)]
        copies.append(pltpu.make_async_copy(room.at[k], to, done.at[k]))
        copies[-1].start()
    for copy in copies:
        copy.wait()


def run_widen(x, across, near, far):
    rows, cols = x.shape
    return call(
        widen,
        jax.ShapeDtypeStruct((4 * rows, cols), f32),
        [pltpu.VMEM((4, rows, cols), f32), pltpu.SemaphoreType.DMA((4,))],
        x, across, near, far, far_outs=(0,),
    )


def join(r0, r1, r2, out):
    rows = r0.shape[0]
    for k, r in enumerate((r0, r1, r2)):
        out[k * rows : (k + 1) * rows, :] = r[...]


def run_join(parts):
    rows, cols = parts[0].shape
    return call(join, jax.ShapeDtypeStruct((3 * rows, cols), bf16), [], *parts)


def merge_half(kept, came, keep, send):
    half = keep.shape[0]
    low = pl.multiple_of(lax.axis_index("dp") * half, 8)
    high = pl.multiple_of(half - low, 8)
    keep[...] = kept[pl.ds(low, half), :] + came[pl.ds(low, half), :]
    send[...] = (kept[pl.ds(high, half), :] + came[pl.ds(high, half), :]).astype(bf16)


def run_merge_half(kept, came):
    rows, cols = kept.shape
    outs = tuple(jax.ShapeDtypeStruct((rows // 2, cols), kind) for kind in (f32, bf16))
    return call(merge_half, outs, [], kept, came)


def merge_blocks(kept, came, keep, s1, s2, s3):
    size = keep.shape[0]

    def block(step):
        low = pl.multiple_of((lax.axis_index("space") + step) % 4 * size, 8)
        return kept[pl.ds(low, size), :] + came[pl.ds(low, size), :].astype(f32)

    keep[...] = block(0)
    for step, send in ((1, s1), (2, s2), (3, s3)):
        send[...] = block(step).astype(bf16)


def run_merge_blocks(kept, came):
    rows, cols = kept.shape
    outs = tuple(jax.ShapeDtypeStruct((rows // 4, cols), kind) for kind in (f32, bf16, bf16, bf16))
    return call(merge_blocks, outs, [], kept, came)


def spread_second(packed, out, head):
    chans = packed.shape[1]
    share = out.shape[0]
    for t in range(27):
        out[:, t * chans : (t + 1) * chans] = packed[t * share : (t + 1) * share, :]
    head[...] = packed[27 * share : 27 * share + head.shape[0], 0:share]


def run_spread_second(packed, share, outs):
    rows, chans = packed.shape
    return call(
        spread_second,
        (jax.ShapeDtypeStruct((share, 27 * chans), f32), jax.ShapeDtypeStruct((outs, share), f32)),
        [],
        packed,
        work=heavy * 2,
    )


def turn(x, axis, step):
    size = lax.axis_size(axis)
    return lax.ppermute(x, axis, [(i, (i + step) % size) for i in range(size)])


def paired(x, axis, bits):
    return lax.ppermute(x, axis, [(i, i ^ bits) for i in range(lax.axis_size(axis))])


def direct(axis):
    return lax.axis_size(axis) <= direct_most


def gathered(x, axis):
    if not direct(axis):
        return lax.all_gather(x, axis)
    size, place = lax.axis_size(axis), lax.axis_index(axis)
    parts = [x] + [turn(x, axis, step) for step in range(1, size)]
    out = jnp.zeros((size,) + x.shape, x.dtype)
    for step, part in enumerate(parts):
        out = lax.dynamic_update_index_in_dim(out, part, (place - step) % size, 0)
    return out


def scattered_sum(x, axis, wire):
    size, place = lax.axis_size(axis), lax.axis_index(axis)
    blocks = x.reshape((size, x.shape[0] // size) + x.shape[1:])
    if not direct(axis):
        return lax.psum_scatter(blocks, axis)
    total = lax.dynamic_index_in_dim(blocks, place, 0, False)
    for step in range(1, size):
        sent = lax.dynamic_index_in_dim(blocks, (place + step) % size, 0, False).astype(wire)
        total = total + turn(sent, axis, step).astype(jnp.float32)
    return total


def total_first(x):
    columns = x.shape[1]
    x = scattered_sum(x, "rep", jnp.float32)
    x = scattered_sum(x, "dp", jnp.bfloat16)
    if direct("space"):
        x = scattered_sum(x, "space", jnp.bfloat16).astype(jnp.bfloat16)
        x = gathered(x, "space").reshape(-1, columns)
    else:
        x = lax.psum(x, "space").astype(jnp.bfloat16)
    x = gathered(x, "dp").reshape(-1, columns)
    x = gathered(x, "rep").reshape(-1, columns)
    return x.astype(jnp.float32)


def total_second(x):
    columns = x.shape[1]
    x = scattered_sum(x, "rep", jnp.float32)
    if direct("dp"):
        x = gathered(x, "dp").sum(0)
    else:
        x = lax.psum(x, "dp")
    return gathered(x, "rep").reshape(-1, columns)


def whole_kernel(part):
    rows, share = part.shape
    copies = [axis for axis in ("dp", "rep")]
    pieces, place = (1, 0)
    for axis in copies:
        place = place * lax.axis_size(axis) + lax.axis_index(axis)
        pieces = pieces * lax.axis_size(axis)
    length = rows // pieces
    piece = lax.dynamic_slice_in_dim(part, place * length, length, 0)
    packed = jnp.concatenate([piece[: length // 2], piece[length // 2 :]], axis=1)
    packs = gathered(packed, "space")
    upper = jnp.moveaxis(packs[:, :, :share], 0, 1).reshape(length // 2, -1)
    lower = jnp.moveaxis(packs[:, :, share:], 0, 1).reshape(length // 2, -1)
    wide = jnp.concatenate([upper, lower], axis=0)
    wide = gathered(wide, "dp")
    wide = jnp.moveaxis(gathered(wide, "rep"), 0, 1)
    return wide.reshape(rows, -1)


def extended_2(x, sides, width):
    for axis, dim in sides:
        devices, length = (lax.axis_size(axis), x.shape[dim])
        up = [(i, (i + 1) % devices) for i in range(devices - 1)]
        down = [(j, i) for i, j in up]
        last = lax.slice_in_dim(x, length - width, length, axis=dim)
        leading = lax.slice_in_dim(x, 0, width, axis=dim)
        before = lax.ppermute(last, axis, up)
        after = lax.ppermute(leading, axis, down)
        x = jnp.concatenate([before, x, after], axis=dim)
    return x


def activate(value):
    return leak_slope * value + (1.0 - leak_slope) * (jax.nn.softplus(value) - log_two)


def activate_slope(value):
    return leak_slope + (1.0 - leak_slope) * jax.nn.sigmoid(value)


def convolve(extended, kernel):
    result = lax.conv_general_dilated(
        extended[None],
        kernel,
        (1, 1, 1),
        [(0, 0), (1, 1), (1, 1)],
        dimension_numbers=("NDHWC", "DHWIO", "NDHWC"),
        preferred_element_type=jnp.float32,
    )
    return result[0]


def pooling(grid):
    depth, rows, cols, chans = grid.shape
    return grid.reshape(depth // 2, 2, rows // 2, 2, cols // 2, 2, chans).mean(axis=(1, 3, 5))


def expand(grid):
    depth, rows, cols, chans = grid.shape
    spread = jnp.broadcast_to(
        grid[:, None, :, None, :, None, :], (depth, 2, rows, 2, cols, 2, chans)
    )
    return spread.reshape(depth * 2, rows * 2, cols * 2, chans) / 8.0


def kernel_grad(extended, grad):
    widened = jnp.pad(extended, ((0, 0), (1, 1), (1, 1), (0, 0)))
    result = lax.conv_general_dilated(
        widened[..., None],
        grad[:, :, :, None, :],
        (1, 1, 1),
        "VALID",
        dimension_numbers=("DHWNC", "DHWIO", "NDHWC"),
        preferred_element_type=jnp.float32,
    )
    return jnp.transpose(result, (1, 2, 3, 0, 4)).reshape(-1, grad.shape[-1])


def general_shards(volumes, targets, first_kernel, second_kernel, head_weights):
    grid_in = volumes[0]
    target_row = targets[0]
    channels = grid_in.shape[-1]
    kernel_one = first_kernel.reshape(3, 3, 3, channels, first_kernel.shape[1])
    extended = extended_2(grid_in, (("space", 0),), 1)
    share = second_kernel.shape[1]
    place = lax.axis_index("space")
    kernel_two = whole_kernel(second_kernel).reshape(3, 3, 3, channels, -1)
    before_one = convolve(extended, kernel_one)
    pooled = pooling(activate(before_one)).astype(jnp.bfloat16)
    whole = gathered(pooled, "space").reshape((-1,) + pooled.shape[1:])
    padded_whole = jnp.pad(whole, ((1, 1), (0, 0), (0, 0), (0, 0)))
    before_two = convolve(padded_whole, kernel_two)
    feature = jnp.mean(activate(before_two), axis=(0, 1, 2))
    predicted = jnp.dot(feature, head_weights, precision=lax.Precision.HIGHEST)
    error = predicted - target_row
    feature_part = lax.dynamic_slice_in_dim(feature, place * share, share, 0)
    head_grad = feature_part[:, None] * error[None, :]
    feature_grad = jnp.dot(head_weights, error, precision=lax.Precision.HIGHEST)
    grad_two = (feature_grad * activate_slope(before_two)).astype(jnp.bfloat16)
    padded_grad = jnp.pad(grad_two, ((1, 1), (0, 0), (0, 0), (0, 0)))
    flipped = jnp.swapaxes(kernel_two[::-1, ::-1, ::-1], 3, 4)
    planes = pooled.shape[0]
    window = lax.dynamic_slice_in_dim(padded_grad, place * planes, planes + 2, 0)
    pooled_grad = convolve(window, flipped)
    grad_one = (expand(pooled_grad) * activate_slope(before_one)).astype(jnp.bfloat16)
    first_total = total_first(kernel_grad(extended, grad_one))
    grad_part = lax.dynamic_slice_in_dim(grad_two, place * share, share, 3)
    second_part = kernel_grad(padded_whole, grad_part)
    rows = second_part.shape[0]
    packed = jnp.concatenate([second_part[: rows // 2], second_part[rows // 2 :]], axis=1)
    packed = total_second(packed)
    second_total = jnp.concatenate([packed[:, :share], packed[:, share:]], axis=0)
    head_total = gathered(gathered(head_grad, "rep").sum(0), "dp").sum(0)
    return (first_total, second_total, head_total)


def neighbours(first, last):
    devices = lax.axis_size("space")
    up = [(i, i + 1) for i in range(devices - 1)]
    down = [(j, i) for i, j in up]
    before = lax.ppermute(last, "space", up)
    after = lax.ppermute(first, "space", down)
    return before, after


def shards(volumes, targets, first_kernel, second_kernel, head_weights):
    sizes = tuple(lax.axis_size(axis) for axis in ("space", "dp", "rep"))
    if sizes != (4, 2, 2):
        return general_shards(volumes, targets, first_kernel, second_kernel, head_weights)
    grid = volumes[0]
    share = second_kernel.shape[1]
    outs = head_weights.shape[1]
    place = lax.axis_index("space")
    turned = second_kernel.T
    before, after = neighbours(grid[:1], grid[-1:])
    copy = 2 * lax.axis_index("dp") + lax.axis_index("rep")
    piece = lax.dynamic_slice_in_dim(turned, copy * (share // 4), share // 4, 0)
    others = [turn(piece, "space", k) for k in range(1, 4)]
    pooled, slope = run_first_forward(grid, before, after, first_kernel)
    pooled, *others = lax.optimization_barrier([pooled] + others)
    others = run_join(others)
    across = turn(others, "dp", 1)
    parts = [pooled] + [turn(pooled, "space", k) for k in range(1, 4)]
    across, *parts = lax.optimization_barrier([across] + parts)
    pieces = [others, turn(others, "rep", 1), across, turn(across, "rep", 1)]
    pooled_grad, own, result = run_second_layer(parts, turned, pieces, head_weights.T, targets)
    keep, send = run_first_backward(grid, before, after, pooled_grad, slope)
    keep, send = run_merge_half(keep, turn(send, "rep", 1))
    arrived = turn(send, "dp", 1)
    kept, sent = run_second_backward(parts, own, result)
    x, *sends = run_merge_blocks(keep, arrived)
    second = kept + turn(sent, "rep", 1)
    *sends, second = lax.optimization_barrier((*sends, second))
    for k in (1, 3, 2):
        x = x + turn(sends[k - 1], "space", k).astype(f32)
    x = x.astype(bf16)
    second = second + turn(second, "dp", 1)
    whole = jnp.zeros((4,) + x.shape, bf16)
    for k in (0, 1, 3, 2):
        part = turn(x, "space", k) if k else x
        if k == 1:
            part, second = lax.optimization_barrier((part, second))
        whole = lax.dynamic_update_index_in_dim(whole, part, (place - k) % 4, 0)
    x = whole.reshape(-1, x.shape[1])
    second = gathered(second, "rep").reshape(-1, second.shape[1])
    second_total, head_total = run_spread_second(second, share, outs)
    across_x = turn(x, "dp", 1)
    near = turn(x, "rep", 1)
    across_x, near, second_total, head_total = lax.optimization_barrier((across_x, near, second_total, head_total))
    far = turn(across_x, "rep", 1)
    first_total = run_widen(x, across_x, near, far)
    return (first_total, second_total.T, head_total.T)


def solution(mesh):
    in_specs = (
        P(("groups", "dp", "rep"), "space", None, None, None),
        P(("groups", "dp", "rep"), None),
        P(),
        P(None, "space"),
        P(),
    )
    out_specs = (P("groups", None), P("groups", "space"), P(("groups", "space"), None))
    return jax.shard_map(shards, mesh=mesh, in_specs=in_specs, out_specs=out_specs, check_vma=False)
```

```python
import jax
import jax.numpy as jnp
from jax import lax
from jax.experimental import pallas as pl
from jax.experimental.pallas import tpu as pltpu
from jax.sharding import PartitionSpec as P

leak_slope = 0.3
log_two = 0.6931471805599453
direct_most = 4
f32, bf16 = jnp.float32, jnp.bfloat16
front = 8
heavy = 10**9


def call(body, outs, scratch, *args, smem=(), away=(), work=0, room=16, far_outs=()):
    spaces = [pltpu.SMEM if k in smem else pltpu.HBM if k in away else pltpu.VMEM for k in range(len(args))]
    specs = [pl.BlockSpec(memory_space=space) for space in spaces]
    one = not isinstance(outs, tuple)
    out_specs = [
        pl.BlockSpec(memory_space=pltpu.HBM if k in far_outs else pltpu.VMEM) for k in range(1 if one else len(outs))
    ]
    out_specs = out_specs[0] if one else tuple(out_specs)
    return pl.pallas_call(
        body,
        out_shape=outs,
        in_specs=specs,
        out_specs=out_specs,
        scratch_shapes=scratch,
        compiler_params=pltpu.CompilerParams(vmem_limit_bytes=room * 2**20),
        cost_estimate=pl.CostEstimate(flops=work, bytes_accessed=0, transcendentals=0),
    )(*args)


def slope_and_activation(value):
    shrunk = jnp.exp(-jnp.abs(value))
    inverse = 1.0 / (1.0 + shrunk)
    slope = leak_slope + (1.0 - leak_slope) * jnp.where(value >= 0, inverse, shrunk * inverse)
    soft = jnp.maximum(value, 0.0) + jnp.log(1.0 + shrunk)
    return slope, leak_slope * value + (1.0 - leak_slope) * (soft - log_two)


def shifted(rows_ref, length, step):
    return rows_ref[front + step : front + step + length, :]


def lay_plane(plane, rows_ref, wide):
    rows, cols, chans = plane.shape
    for h in range(rows):
        rows_ref[front + h * wide : front + h * wide + cols, :] = plane[h].astype(f32)


def wide_plane(source, rows_ref, target, top, wide):
    rows, chans = source.shape[0], source.shape[2]
    lay_plane(source, rows_ref, wide)
    for e in range(3):
        target[top : top + rows * wide, e * chans : (e + 1) * chans] = shifted(
            rows_ref, rows * wide, e - 1
        ).astype(bf16)


def first_forward(vol, before, after, kernel, pooled, slope, u, rows_ref, pairs, accs, halves, dense):
    depth, rows, cols, chans = vol.shape
    wide = 32
    cells = rows * wide
    outs = kernel.shape[1]
    span = 3 * chans
    rows_ref[...] = jnp.zeros_like(rows_ref)
    edge = jnp.zeros((u.shape[0], wide, span), bf16)
    u[:, 0:wide, :] = edge
    u[:, wide + cells :, :] = edge
    for p in range(depth + 2):
        if p == 0:
            source = before[0]
        elif p == depth + 1:
            source = after[0]
        else:
            source = vol[p - 1]
        wide_plane(source, rows_ref, u.at[p], wide, wide)

    def tap(a, b):
        return kernel[(9 * a + 3 * b) * chans : (9 * a + 3 * b) * chans + span, :]

    for b in range(3):
        pairs[b, 0:span, 0:outs] = tap(1, b)
        pairs[b, 0:span, outs:] = tap(0, b)
        pairs[b, span:, 0:outs] = tap(2, b)
        pairs[b, span:, outs:] = tap(1, b)
    first_taps = jnp.concatenate([tap(0, b) for b in range(3)], axis=0)
    last_taps = jnp.concatenate([tap(2, b) for b in range(3)], axis=0)

    def one_pair(t):
        acc, half = accs.at[t], halves.at[t]

        def window(q, b):
            return u[2 * t + q, b * wide : b * wide + cells, :]

        left = jnp.concatenate([window(0, b) for b in range(3)], axis=1)
        acc[:, 0:outs] = jnp.dot(left, first_taps, preferred_element_type=f32)
        right = jnp.concatenate([window(3, b) for b in range(3)], axis=1)
        acc[:, outs:] = jnp.dot(right, last_taps, preferred_element_type=f32)
        for b in range(3):
            both = jnp.concatenate([window(1, b), window(2, b)], axis=1)
            acc[...] += jnp.dot(both, pairs[b], preferred_element_type=f32)
        for h in range(rows // 2):
            part = acc[h * 2 * wide : (h + 1) * 2 * wide, :]
            slopes, values = slope_and_activation(part)
            slope[2 * t, h * 2 * wide : (h + 1) * 2 * wide, :] = slopes[:, 0:outs]
            slope[2 * t + 1, h * 2 * wide : (h + 1) * 2 * wide, :] = slopes[:, outs:]
            values = values[:, 0:outs] + values[:, outs:]
            half[h * wide : (h + 1) * wide, :] = values[0:wide] + values[wide:]
        for h in range(rows // 2):
            even = half[pl.ds(h * wide, cols // 2, stride=2), :]
            odd = half[pl.ds(h * wide + 1, cols // 2, stride=2), :]
            dense[t, h * (cols // 2) : (h + 1) * (cols // 2), :] = (even + odd) * 0.125

    for t in range(depth // 2):
        one_pair(t)
    pooled[...] = dense[...].astype(bf16)


def run_first_forward(vol, before, after, kernel):
    depth, rows, cols, chans = vol.shape
    wide, outs = 32, kernel.shape[1]
    cells = rows * wide
    return call(
        first_forward,
        (
            jax.ShapeDtypeStruct((depth // 2, rows * cols // 4, outs), bf16),
            jax.ShapeDtypeStruct((depth, cells, outs), f32),
        ),
        [
            pltpu.VMEM((depth + 2, cells + 2 * wide, 3 * chans), bf16),
            pltpu.VMEM((cells + 2 * front, chans), f32),
            pltpu.VMEM((3, 6 * chans, 2 * outs), bf16),
            pltpu.VMEM((depth // 2, cells, 2 * outs), f32),
            pltpu.VMEM((depth // 2, cells // 2, outs), f32),
            pltpu.VMEM((depth // 2, rows * cols // 4, outs), f32),
        ],
        vol, before, after, kernel, work=heavy * 8,
    )


def first_backward(vol, before, after, spread, slope, keep, send, u, rows_ref, g, acc, twice):
    depth, rows, cols, chans = vol.shape
    wide = 32
    cells = rows * wide
    outs = slope.shape[2]
    rows_ref[...] = jnp.zeros_like(rows_ref)
    for p in range(depth + 2):
        if p == 0:
            source = before[0]
        elif p == depth + 1:
            source = after[0]
        else:
            source = vol[p - 1]
        wide_plane(source, rows_ref, u.at[p], 0, wide)
    edge = jnp.zeros((depth, wide, outs), bf16)
    g[:, 0:wide, :] = edge
    g[:, wide + cells :, :] = edge
    for d in range(depth):
        if d % 2 == 0:
            values = spread[d // 2] * 0.125
            twice[pl.ds(0, cells // 4, stride=2), :] = values
            twice[pl.ds(1, cells // 4, stride=2), :] = values
        for h in range(rows):
            some = twice[(h // 2) * wide : (h // 2 + 1) * wide, :] * slope[d, h * wide : (h + 1) * wide, :]
            g[d, (h + 1) * wide : (h + 2) * wide, :] = some.astype(bf16)
    started = set()
    for p in range(depth + 2):
        taps = [a for a in range(3) if 0 <= p - a < depth]
        rhs = jnp.concatenate(
            [g[p - a, (2 - b) * wide : (2 - b) * wide + cells, :] for a in taps for b in range(3)], axis=1
        )
        part = lax.dot_general(u[p], rhs, (((0,), (0,)), ((), ())), preferred_element_type=f32)
        for place, a in enumerate(taps):
            block = part[:, place * 3 * outs : (place + 1) * 3 * outs]
            lanes = slice(a * 3 * outs, (a + 1) * 3 * outs)
            if a in started:
                acc[:, lanes] += block
            else:
                acc[:, lanes] = block
                started.add(a)
    length = keep.shape[0]

    def write(first, second):
        for a in range(3):
            for b in range(3):
                for e in range(3):
                    top = (9 * a + 3 * b + e) * chans
                    lanes = slice((3 * a + b) * outs, (3 * a + b + 1) * outs)
                    cut = min(max(length - top, 0), chans)
                    if cut > 0:
                        first[top : top + cut, :] = acc[e * chans : e * chans + cut, lanes]
                    if cut < chans:
                        low = top + cut - length
                        second[low : low + chans - cut, :] = acc[e * chans + cut : (e + 1) * chans, lanes]

    @pl.when(lax.axis_index("rep") == 0)
    def _():
        write(keep, send)

    @pl.when(lax.axis_index("rep") != 0)
    def _():
        write(send, keep)


def run_first_backward(vol, before, after, spread, slope):
    depth, rows, cols, chans = vol.shape
    wide, outs = 32, slope.shape[2]
    cells = rows * wide
    return call(
        first_backward,
        (jax.ShapeDtypeStruct((27 * chans // 2, outs), f32),) * 2,
        [
            pltpu.VMEM((depth + 2, cells, 3 * chans), bf16),
            pltpu.VMEM((cells + 2 * front, chans), f32),
            pltpu.VMEM((depth, cells + 2 * wide, outs), bf16),
            pltpu.VMEM((3 * chans, 9 * outs), f32),
            pltpu.VMEM((cells // 2, outs), f32),
        ],
        vol, before, after, spread, slope, work=heavy * 7,
    )


def positions():
    place = lax.axis_index("space")
    copy = 2 * lax.axis_index("dp") + lax.axis_index("rep")
    return [(place + 4 - k) % 4 for k in range(4)] + [copy ^ k for k in range(4)]


def lay_pooled(parts, places, flat, rows_ref, target, top, side, wide):
    chans = target.shape[2] // 3
    cells = side * wide
    for part, place in zip(parts, places):
        for d in range(part.shape[0]):
            flat[...] = part[d].astype(f32)
            for h in range(side):
                rows_ref[front + h * wide : front + h * wide + side, :] = flat[h * side : (h + 1) * side, :]
            for e in range(3):
                target[place + d, top : top + cells, e * chans : (e + 1) * chans] = shifted(
                    rows_ref, cells, e - 1
                ).astype(bf16)


def second_layer(
    p0, p1, p2, p3, w0, w1, w2, w3, w4, head, wanted,
    pooled_grad, own, result, p, flat, rows_ref, w, acc, slopes, shift_ref, g,
):
    parts, pieces = (p0, p1, p2, p3), (w1, w2, w3, w4)
    where = positions()
    planes, area, chans = p0.shape
    side, wide = 12, 16
    cells = side * wide
    depth = planes * len(parts)
    outs = w.shape[0]
    rows_ref[...] = jnp.zeros_like(rows_ref)
    p[0] = jnp.zeros(p.shape[1:], bf16)
    p[depth + 1] = jnp.zeros(p.shape[1:], bf16)
    edge = jnp.zeros((depth + 2, wide, 3 * chans), bf16)
    p[:, 0:wide, :] = edge
    p[:, wide + cells :, :] = edge
    lay_pooled(parts, [1 + planes * where[k] for k in range(4)], flat, rows_ref, p, wide, side, wide)
    share = w0.shape[0]
    quarter = share // 4
    w[0:share, :] = w0[...]
    for k in range(1, 4):
        for j in range(4):
            at = pl.multiple_of(k * share + where[4 + j] * quarter, quarter)
            w[pl.ds(at, quarter), :] = pieces[j][(k - 1) * quarter : k * quarter, :]
    column = lax.broadcasted_iota(jnp.int32, (cells, outs), 0) % wide
    inside = column < side
    step = depth // 2
    slopes[0] = jnp.zeros((cells, outs), f32)
    slopes[depth + 1] = jnp.zeros((cells, outs), f32)

    def half(t, total):
        for a in range(3):
            lhs = jnp.concatenate(
                [
                    p[pl.ds(t * step + a, step), b * wide : b * wide + cells, :].reshape(step * cells, 3 * chans)
                    for b in range(3)
                ],
                axis=1,
            )
            part = lax.dot_general(
                lhs, w[:, 9 * a * chans : 9 * (a + 1) * chans], (((1,), (1,)), ((), ())), preferred_element_type=f32
            )
            if a == 0:
                acc[...] = part
            else:
                acc[...] += part
        for d in range(step):
            slope, value = slope_and_activation(acc[d * cells : (d + 1) * cells, :])
            slopes[t * step + d + 1] = jnp.where(inside, slope, 0.0)
            value = jnp.where(inside, value, 0.0)
            total = total + value.reshape(cells // 8, 8, outs).sum(axis=0)
        return total

    total = lax.fori_loop(0, 2, half, jnp.zeros((8, outs), f32))
    feature = total.sum(axis=0, keepdims=True) / float(depth * area)
    natural = [head[:, k * share : (k + 1) * share] for k in range(4)]
    turned = []
    for k in range(4):
        block = natural[0]
        for j in range(1, 4):
            block = jnp.where(where[k] == j, natural[j], block)
        turned.append(block)
    head = jnp.concatenate(turned, axis=1)
    count = head.shape[0]
    predicted = jnp.sum(feature * head, axis=1, keepdims=True)
    row = lax.broadcasted_iota(jnp.int32, (count, 1), 0)
    target = jnp.zeros((count, 1), f32)
    for k in range(count):
        target = jnp.where(row == k, wanted[0, k], target)
    error = predicted - target
    result[...] = error * feature
    scale = jnp.sum(head * error, axis=0, keepdims=True)
    for d in range(depth):
        own[d] = (slopes[d + 1, :, 0:share] * scale[:, 0:share]).astype(bf16)
    shift_ref[...] = jnp.zeros_like(shift_ref)
    rim = jnp.zeros((planes + 2, wide, outs), bf16)
    for e in range(3):
        g[e, :, 0:wide, :] = rim
        g[e, :, wide + cells :, :] = rim
    for k in range(planes + 2):
        shift_ref[front : front + cells, :] = (slopes[where[0] * planes + k] * scale).astype(bf16).astype(f32)
        for e in range(3):
            g[e, k, wide : wide + cells, :] = shifted(shift_ref, cells, 1 - e).astype(bf16)
    out = None
    for a in range(3):
        taps = [(b, e) for b in range(3) for e in range(3)]
        lhs = jnp.concatenate(
            [
                g[e, 2 - a : 2 - a + planes, (2 - b) * wide : (2 - b) * wide + cells, :].reshape(planes * cells, outs)
                for b, e in taps
            ],
            axis=1,
        )
        rhs = jnp.concatenate(
            [w[:, (9 * a + 3 * b + e) * chans : (9 * a + 3 * b + e + 1) * chans] for b, e in taps], axis=0
        )
        part = jnp.dot(lhs, rhs, preferred_element_type=f32)
        out = part if out is None else out + part
    keep = lax.broadcasted_iota(jnp.int32, (planes * cells, chans), 0) % wide < side
    pooled_grad[...] = jnp.where(keep, out, 0.0).reshape(planes, cells, chans)


def run_second_layer(parts, part_kernel, pieces, head, wanted):
    planes, area, chans = parts[0].shape
    side, wide = 12, 16
    cells = side * wide
    depth = planes * 4
    share, taps = part_kernel.shape
    outs = 4 * share
    return call(
        second_layer,
        (
            jax.ShapeDtypeStruct((planes, cells, chans), f32),
            jax.ShapeDtypeStruct((depth, cells, share), bf16),
            jax.ShapeDtypeStruct((head.shape[0], outs), f32),
        ),
        [
            pltpu.VMEM((depth + 2, cells + 2 * wide, 3 * chans), bf16),
            pltpu.VMEM((area, chans), f32),
            pltpu.VMEM((cells + 2 * front, chans), f32),
            pltpu.VMEM((outs, taps), bf16),
            pltpu.VMEM((depth // 2 * cells, outs), f32),
            pltpu.VMEM((depth + 2, cells, outs), f32),
            pltpu.VMEM((cells + 2 * front, outs), f32),
            pltpu.VMEM((3, planes + 2, cells + 2 * wide, outs), bf16),
        ],
        *parts, part_kernel, *pieces, head, wanted, smem=(10,), work=heavy * 8,
    )


def second_backward(p0, p1, p2, p3, own, result, keep, send, p, flat, rows_ref, g, grad):
    parts = (p0, p1, p2, p3)
    where = positions()
    planes, area, chans = p0.shape
    side, wide = 12, 16
    cells = side * wide
    depth = planes * len(parts)
    share = own.shape[2]
    rows_ref[...] = jnp.zeros_like(rows_ref)
    p[0] = jnp.zeros(p.shape[1:], bf16)
    p[depth + 1] = jnp.zeros(p.shape[1:], bf16)
    lay_pooled(parts, [1 + planes * where[k] for k in range(4)], flat, rows_ref, p, 0, side, wide)
    none = jnp.zeros((depth, wide, share), bf16)
    for b in range(3):
        lanes = slice(b * share, (b + 1) * share)
        if b == 0:
            g[:, 0 : cells - wide, lanes] = own[:, wide:cells, :]
            g[:, cells - wide :, lanes] = none
        elif b == 1:
            g[:, :, lanes] = own[...]
        else:
            g[:, wide:, lanes] = own[:, 0 : cells - wide, :]
            g[:, 0:wide, lanes] = none
    rhs = g[...].reshape(depth * cells, 3 * share)
    for a in range(3):
        lhs = p[a : a + depth].reshape(depth * cells, 3 * chans)
        part = lax.dot_general(rhs, lhs, (((0,), (0,)), ((), ())), preferred_element_type=f32)
        for b in range(3):
            for e in range(3):
                t = 9 * a + 3 * b + e
                block = part[b * share : (b + 1) * share, e * chans : (e + 1) * chans]
                grad[t * share : (t + 1) * share, :] = block
    grad[27 * share :, :] = jnp.zeros((16, chans), f32)
    grad[27 * share : 27 * share + result.shape[0], :] = result[:, 0:chans]
    half = keep.shape[0]
    low = pl.multiple_of(lax.axis_index("rep") * half, 8)
    keep[...] = grad[pl.ds(low, half), :]
    send[...] = grad[pl.ds(pl.multiple_of(half - low, 8), half), :]


def run_second_backward(parts, own, result):
    planes, area, chans = parts[0].shape
    depth, cells, share = own.shape
    return call(
        second_backward,
        (jax.ShapeDtypeStruct((27 * share // 2 + 8, chans), f32),) * 2,
        [
            pltpu.VMEM((depth + 2, cells, 3 * chans), bf16),
            pltpu.VMEM((area, chans), f32),
            pltpu.VMEM((cells + 2 * front, chans), f32),
            pltpu.VMEM((depth, cells, 3 * share), bf16),
            pltpu.VMEM((27 * share + 16, chans), f32),
        ],
        *parts, own, result, work=heavy * 4,
    )


def entry(vol, first, last):
    first[0] = vol[0]
    last[0] = vol[vol.shape[0] - 1]


def run_entry(vol):
    plane = jax.ShapeDtypeStruct((1,) + vol.shape[1:], bf16)
    return call(entry, (plane, plane), [], vol)


def widen(x, across, near, far, out, room, done):
    rows = x.shape[0]
    own = 2 * lax.axis_index("rep") + lax.axis_index("dp")
    copies = []
    for k, part in enumerate((x, across, near, far)):
        room[k] = part[...].astype(f32)
        to = out.at[pl.ds(pl.multiple_of((own ^ k) * rows, 8), rows)]
        copies.append(pltpu.make_async_copy(room.at[k], to, done.at[k]))
        copies[-1].start()
    for copy in copies:
        copy.wait()


def run_widen(x, across, near, far):
    rows, cols = x.shape
    return call(
        widen,
        jax.ShapeDtypeStruct((4 * rows, cols), f32),
        [pltpu.VMEM((4, rows, cols), f32), pltpu.SemaphoreType.DMA((4,))],
        x, across, near, far, far_outs=(0,),
    )


def join(r0, r1, r2, out):
    rows = r0.shape[0]
    for k, r in enumerate((r0, r1, r2)):
        out[k * rows : (k + 1) * rows, :] = r[...]


def run_join(parts):
    rows, cols = parts[0].shape
    return call(join, jax.ShapeDtypeStruct((3 * rows, cols), bf16), [], *parts)


def merge_half(kept, came, keep, send):
    half = keep.shape[0]
    low = pl.multiple_of(lax.axis_index("dp") * half, 8)
    high = pl.multiple_of(half - low, 8)
    keep[...] = kept[pl.ds(low, half), :] + came[pl.ds(low, half), :]
    send[...] = (kept[pl.ds(high, half), :] + came[pl.ds(high, half), :]).astype(bf16)


def run_merge_half(kept, came):
    rows, cols = kept.shape
    outs = tuple(jax.ShapeDtypeStruct((rows // 2, cols), kind) for kind in (f32, bf16))
    return call(merge_half, outs, [], kept, came)


def merge_blocks(kept, came, keep, s1, s2, s3):
    size = keep.shape[0]

    def block(step):
        low = pl.multiple_of((lax.axis_index("space") + step) % 4 * size, 8)
        return kept[pl.ds(low, size), :] + came[pl.ds(low, size), :].astype(f32)

    keep[...] = block(0)
    for step, send in ((1, s1), (2, s2), (3, s3)):
        send[...] = block(step).astype(bf16)


def run_merge_blocks(kept, came):
    rows, cols = kept.shape
    outs = tuple(jax.ShapeDtypeStruct((rows // 4, cols), kind) for kind in (f32, bf16, bf16, bf16))
    return call(merge_blocks, outs, [], kept, came)


def spread_second(packed, out, head):
    chans = packed.shape[1]
    share = out.shape[0]
    for t in range(27):
        out[:, t * chans : (t + 1) * chans] = packed[t * share : (t + 1) * share, :]
    head[...] = packed[27 * share : 27 * share + head.shape[0], 0:share]


def run_spread_second(packed, share, outs):
    rows, chans = packed.shape
    return call(
        spread_second,
        (jax.ShapeDtypeStruct((share, 27 * chans), f32), jax.ShapeDtypeStruct((outs, share), f32)),
        [],
        packed,
        work=heavy * 2,
    )


def turn(x, axis, step):
    size = lax.axis_size(axis)
    return lax.ppermute(x, axis, [(i, (i + step) % size) for i in range(size)])


def paired(x, axis, bits):
    return lax.ppermute(x, axis, [(i, i ^ bits) for i in range(lax.axis_size(axis))])


def direct(axis):
    return lax.axis_size(axis) <= direct_most


def gathered(x, axis):
    if not direct(axis):
        return lax.all_gather(x, axis)
    size, place = lax.axis_size(axis), lax.axis_index(axis)
    parts = [x] + [turn(x, axis, step) for step in range(1, size)]
    out = jnp.zeros((size,) + x.shape, x.dtype)
    for step, part in enumerate(parts):
        out = lax.dynamic_update_index_in_dim(out, part, (place - step) % size, 0)
    return out


def scattered_sum(x, axis, wire):
    size, place = lax.axis_size(axis), lax.axis_index(axis)
    blocks = x.reshape((size, x.shape[0] // size) + x.shape[1:])
    if not direct(axis):
        return lax.psum_scatter(blocks, axis)
    total = lax.dynamic_index_in_dim(blocks, place, 0, False)
    for step in range(1, size):
        sent = lax.dynamic_index_in_dim(blocks, (place + step) % size, 0, False).astype(wire)
        total = total + turn(sent, axis, step).astype(jnp.float32)
    return total


def total_first(x):
    columns = x.shape[1]
    x = scattered_sum(x, "rep", jnp.float32)
    x = scattered_sum(x, "dp", jnp.bfloat16)
    if direct("space"):
        x = scattered_sum(x, "space", jnp.bfloat16).astype(jnp.bfloat16)
        x = gathered(x, "space").reshape(-1, columns)
    else:
        x = lax.psum(x, "space").astype(jnp.bfloat16)
    x = gathered(x, "dp").reshape(-1, columns)
    x = gathered(x, "rep").reshape(-1, columns)
    return x.astype(jnp.float32)


def total_second(x):
    columns = x.shape[1]
    x = scattered_sum(x, "rep", jnp.float32)
    if direct("dp"):
        x = gathered(x, "dp").sum(0)
    else:
        x = lax.psum(x, "dp")
    return gathered(x, "rep").reshape(-1, columns)


def whole_kernel(part):
    rows, share = part.shape
    copies = [axis for axis in ("dp", "rep")]
    pieces, place = (1, 0)
    for axis in copies:
        place = place * lax.axis_size(axis) + lax.axis_index(axis)
        pieces = pieces * lax.axis_size(axis)
    length = rows // pieces
    piece = lax.dynamic_slice_in_dim(part, place * length, length, 0)
    packed = jnp.concatenate([piece[: length // 2], piece[length // 2 :]], axis=1)
    packs = gathered(packed, "space")
    upper = jnp.moveaxis(packs[:, :, :share], 0, 1).reshape(length // 2, -1)
    lower = jnp.moveaxis(packs[:, :, share:], 0, 1).reshape(length // 2, -1)
    wide = jnp.concatenate([upper, lower], axis=0)
    wide = gathered(wide, "dp")
    wide = jnp.moveaxis(gathered(wide, "rep"), 0, 1)
    return wide.reshape(rows, -1)


def extended_2(x, sides, width):
    for axis, dim in sides:
        devices, length = (lax.axis_size(axis), x.shape[dim])
        up = [(i, (i + 1) % devices) for i in range(devices - 1)]
        down = [(j, i) for i, j in up]
        last = lax.slice_in_dim(x, length - width, length, axis=dim)
        leading = lax.slice_in_dim(x, 0, width, axis=dim)
        before = lax.ppermute(last, axis, up)
        after = lax.ppermute(leading, axis, down)
        x = jnp.concatenate([before, x, after], axis=dim)
    return x


def activate(value):
    return leak_slope * value + (1.0 - leak_slope) * (jax.nn.softplus(value) - log_two)


def activate_slope(value):
    return leak_slope + (1.0 - leak_slope) * jax.nn.sigmoid(value)


def convolve(extended, kernel):
    result = lax.conv_general_dilated(
        extended[None],
        kernel,
        (1, 1, 1),
        [(0, 0), (1, 1), (1, 1)],
        dimension_numbers=("NDHWC", "DHWIO", "NDHWC"),
        preferred_element_type=jnp.float32,
    )
    return result[0]


def pooling(grid):
    depth, rows, cols, chans = grid.shape
    return grid.reshape(depth // 2, 2, rows // 2, 2, cols // 2, 2, chans).mean(axis=(1, 3, 5))


def expand(grid):
    depth, rows, cols, chans = grid.shape
    spread = jnp.broadcast_to(
        grid[:, None, :, None, :, None, :], (depth, 2, rows, 2, cols, 2, chans)
    )
    return spread.reshape(depth * 2, rows * 2, cols * 2, chans) / 8.0


def kernel_grad(extended, grad):
    widened = jnp.pad(extended, ((0, 0), (1, 1), (1, 1), (0, 0)))
    result = lax.conv_general_dilated(
        widened[..., None],
        grad[:, :, :, None, :],
        (1, 1, 1),
        "VALID",
        dimension_numbers=("DHWNC", "DHWIO", "NDHWC"),
        preferred_element_type=jnp.float32,
    )
    return jnp.transpose(result, (1, 2, 3, 0, 4)).reshape(-1, grad.shape[-1])


def general_shards(volumes, targets, first_kernel, second_kernel, head_weights):
    grid_in = volumes[0]
    target_row = targets[0]
    channels = grid_in.shape[-1]
    kernel_one = first_kernel.reshape(3, 3, 3, channels, first_kernel.shape[1])
    extended = extended_2(grid_in, (("space", 0),), 1)
    share = second_kernel.shape[1]
    place = lax.axis_index("space")
    kernel_two = whole_kernel(second_kernel).reshape(3, 3, 3, channels, -1)
    before_one = convolve(extended, kernel_one)
    pooled = pooling(activate(before_one)).astype(jnp.bfloat16)
    whole = gathered(pooled, "space").reshape((-1,) + pooled.shape[1:])
    padded_whole = jnp.pad(whole, ((1, 1), (0, 0), (0, 0), (0, 0)))
    before_two = convolve(padded_whole, kernel_two)
    feature = jnp.mean(activate(before_two), axis=(0, 1, 2))
    predicted = jnp.dot(feature, head_weights, precision=lax.Precision.HIGHEST)
    error = predicted - target_row
    feature_part = lax.dynamic_slice_in_dim(feature, place * share, share, 0)
    head_grad = feature_part[:, None] * error[None, :]
    feature_grad = jnp.dot(head_weights, error, precision=lax.Precision.HIGHEST)
    grad_two = (feature_grad * activate_slope(before_two)).astype(jnp.bfloat16)
    padded_grad = jnp.pad(grad_two, ((1, 1), (0, 0), (0, 0), (0, 0)))
    flipped = jnp.swapaxes(kernel_two[::-1, ::-1, ::-1], 3, 4)
    planes = pooled.shape[0]
    window = lax.dynamic_slice_in_dim(padded_grad, place * planes, planes + 2, 0)
    pooled_grad = convolve(window, flipped)
    grad_one = (expand(pooled_grad) * activate_slope(before_one)).astype(jnp.bfloat16)
    first_total = total_first(kernel_grad(extended, grad_one))
    grad_part = lax.dynamic_slice_in_dim(grad_two, place * share, share, 3)
    second_part = kernel_grad(padded_whole, grad_part)
    rows = second_part.shape[0]
    packed = jnp.concatenate([second_part[: rows // 2], second_part[rows // 2 :]], axis=1)
    packed = total_second(packed)
    second_total = jnp.concatenate([packed[:, :share], packed[:, share:]], axis=0)
    head_total = gathered(gathered(head_grad, "rep").sum(0), "dp").sum(0)
    return (first_total, second_total, head_total)


def neighbours(first, last):
    devices = lax.axis_size("space")
    up = [(i, i + 1) for i in range(devices - 1)]
    down = [(j, i) for i, j in up]
    before = lax.ppermute(last, "space", up)
    after = lax.ppermute(first, "space", down)
    return before, after


def shards(volumes, targets, first_kernel, second_kernel, head_weights):
    sizes = tuple(lax.axis_size(axis) for axis in ("space", "dp", "rep"))
    if sizes != (4, 2, 2):
        return general_shards(volumes, targets, first_kernel, second_kernel, head_weights)
    grid = volumes[0]
    share = second_kernel.shape[1]
    outs = head_weights.shape[1]
    place = lax.axis_index("space")
    turned = second_kernel.T
    before, after = neighbours(grid[:1], grid[-1:])
    copy = 2 * lax.axis_index("dp") + lax.axis_index("rep")
    piece = lax.dynamic_slice_in_dim(turned, copy * (share // 4), share // 4, 0)
    others = [turn(piece, "space", k) for k in range(1, 4)]
    pooled, slope = run_first_forward(grid, before, after, first_kernel)
    pooled, *others = lax.optimization_barrier([pooled] + others)
    others = run_join(others)
    across = turn(others, "dp", 1)
    parts = [pooled] + [turn(pooled, "space", k) for k in range(1, 4)]
    across, *parts = lax.optimization_barrier([across] + parts)
    pieces = [others, turn(others, "rep", 1), across, turn(across, "rep", 1)]
    pooled_grad, own, result = run_second_layer(parts, turned, pieces, head_weights.T, targets)
    keep, send = run_first_backward(grid, before, after, pooled_grad, slope)
    keep, send = run_merge_half(keep, turn(send, "rep", 1))
    arrived = turn(send, "dp", 1)
    kept, sent = run_second_backward(parts, own, result)
    x, *sends = run_merge_blocks(keep, arrived)
    second = kept + turn(sent, "rep", 1)
    *sends, second = lax.optimization_barrier((*sends, second))
    for k in (1, 3, 2):
        x = x + turn(sends[k - 1], "space", k).astype(f32)
    x = x.astype(bf16)
    second = second + turn(second, "dp", 1)
    whole = jnp.zeros((4,) + x.shape, bf16)
    for k in (0, 1, 3, 2):
        part = turn(x, "space", k) if k else x
        if k == 1:
            part, second = lax.optimization_barrier((part, second))
        whole = lax.dynamic_update_index_in_dim(whole, part, (place - k) % 4, 0)
    x = whole.reshape(-1, x.shape[1])
    second = gathered(second, "rep").reshape(-1, second.shape[1])
    second_total, head_total = run_spread_second(second, share, outs)
    across_x = turn(x, "dp", 1)
    near = turn(x, "rep", 1)
    across_x, near, second_total, head_total = lax.optimization_barrier((across_x, near, second_total, head_total))
    far = turn(across_x, "rep", 1)
    first_total = run_widen(x, across_x, near, far)
    return (first_total, second_total.T, head_total.T)


def solution(mesh):
    in_specs = (
        P(("groups", "dp", "rep"), "space", None, None, None),
        P(("groups", "dp", "rep"), None),
        P(),
        P(None, "space"),
        P(),
    )
    out_specs = (P("groups", None), P("groups", "space"), P(("groups", "space"), None))
    return jax.shard_map(shards, mesh=mesh, in_specs=in_specs, out_specs=out_specs, check_vma=False)
```

```python
import jax
import jax.numpy as jnp
from jax import lax
from jax.experimental import pallas as pl
from jax.experimental.pallas import tpu as pltpu
from jax.sharding import PartitionSpec as P

leak_slope = 0.3
log_two = 0.6931471805599453
direct_most = 4
f32, bf16 = jnp.float32, jnp.bfloat16
front = 8
heavy = 10**9


def call(body, outs, scratch, *args, smem=(), away=(), work=0, room=16, far_outs=()):
    spaces = [pltpu.SMEM if k in smem else pltpu.HBM if k in away else pltpu.VMEM for k in range(len(args))]
    specs = [pl.BlockSpec(memory_space=space) for space in spaces]
    one = not isinstance(outs, tuple)
    out_specs = [
        pl.BlockSpec(memory_space=pltpu.HBM if k in far_outs else pltpu.VMEM) for k in range(1 if one else len(outs))
    ]
    out_specs = out_specs[0] if one else tuple(out_specs)
    return pl.pallas_call(
        body,
        out_shape=outs,
        in_specs=specs,
        out_specs=out_specs,
        scratch_shapes=scratch,
        compiler_params=pltpu.CompilerParams(vmem_limit_bytes=room * 2**20),
        cost_estimate=pl.CostEstimate(flops=work, bytes_accessed=0, transcendentals=0),
    )(*args)


def slope_and_activation(value):
    shrunk = jnp.exp(-jnp.abs(value))
    inverse = 1.0 / (1.0 + shrunk)
    slope = leak_slope + (1.0 - leak_slope) * jnp.where(value >= 0, inverse, shrunk * inverse)
    soft = jnp.maximum(value, 0.0) + jnp.log(1.0 + shrunk)
    return slope, leak_slope * value + (1.0 - leak_slope) * (soft - log_two)


def shifted(rows_ref, length, step):
    return rows_ref[front + step : front + step + length, :]


def lay_plane(plane, rows_ref, wide):
    rows, cols, chans = plane.shape
    for h in range(rows):
        rows_ref[front + h * wide : front + h * wide + cols, :] = plane[h].astype(f32)


def wide_plane(source, rows_ref, target, top, wide):
    rows, chans = source.shape[0], source.shape[2]
    lay_plane(source, rows_ref, wide)
    for e in range(3):
        target[top : top + rows * wide, e * chans : (e + 1) * chans] = shifted(
            rows_ref, rows * wide, e - 1
        ).astype(bf16)


def first_forward(vol, before, after, kernel, pooled, slope, u, rows_ref, pairs, accs, halves, dense):
    depth, rows, cols, chans = vol.shape
    wide = 32
    cells = rows * wide
    outs = kernel.shape[1]
    span = 3 * chans
    rows_ref[...] = jnp.zeros_like(rows_ref)
    edge = jnp.zeros((u.shape[0], wide, span), bf16)
    u[:, 0:wide, :] = edge
    u[:, wide + cells :, :] = edge
    for p in range(depth + 2):
        if p == 0:
            source = before[0]
        elif p == depth + 1:
            source = after[0]
        else:
            source = vol[p - 1]
        wide_plane(source, rows_ref, u.at[p], wide, wide)

    def tap(a, b):
        return kernel[(9 * a + 3 * b) * chans : (9 * a + 3 * b) * chans + span, :]

    for b in range(3):
        pairs[b, 0:span, 0:outs] = tap(1, b)
        pairs[b, 0:span, outs:] = tap(0, b)
        pairs[b, span:, 0:outs] = tap(2, b)
        pairs[b, span:, outs:] = tap(1, b)
    first_taps = jnp.concatenate([tap(0, b) for b in range(3)], axis=0)
    last_taps = jnp.concatenate([tap(2, b) for b in range(3)], axis=0)

    def one_pair(t):
        acc, half = accs.at[t], halves.at[t]

        def window(q, b):
            return u[2 * t + q, b * wide : b * wide + cells, :]

        left = jnp.concatenate([window(0, b) for b in range(3)], axis=1)
        acc[:, 0:outs] = jnp.dot(left, first_taps, preferred_element_type=f32)
        right = jnp.concatenate([window(3, b) for b in range(3)], axis=1)
        acc[:, outs:] = jnp.dot(right, last_taps, preferred_element_type=f32)
        both = jnp.concatenate([window(q, b) for b in range(3) for q in (1, 2)], axis=1)
        acc[...] += jnp.dot(both, pairs[...].reshape(18 * chans, 2 * outs), preferred_element_type=f32)
        for h in range(rows // 2):
            part = acc[h * 2 * wide : (h + 1) * 2 * wide, :]
            slopes, values = slope_and_activation(part)
            slope[2 * t, h * 2 * wide : (h + 1) * 2 * wide, :] = slopes[:, 0:outs]
            slope[2 * t + 1, h * 2 * wide : (h + 1) * 2 * wide, :] = slopes[:, outs:]
            values = values[:, 0:outs] + values[:, outs:]
            half[h * wide : (h + 1) * wide, :] = values[0:wide] + values[wide:]
        for h in range(rows // 2):
            even = half[pl.ds(h * wide, cols // 2, stride=2), :]
            odd = half[pl.ds(h * wide + 1, cols // 2, stride=2), :]
            dense[t, h * (cols // 2) : (h + 1) * (cols // 2), :] = (even + odd) * 0.125

    for t in range(depth // 2):
        one_pair(t)
    pooled[...] = dense[...].astype(bf16)


def run_first_forward(vol, before, after, kernel):
    depth, rows, cols, chans = vol.shape
    wide, outs = 32, kernel.shape[1]
    cells = rows * wide
    return call(
        first_forward,
        (
            jax.ShapeDtypeStruct((depth // 2, rows * cols // 4, outs), bf16),
            jax.ShapeDtypeStruct((depth, cells, outs), f32),
        ),
        [
            pltpu.VMEM((depth + 2, cells + 2 * wide, 3 * chans), bf16),
            pltpu.VMEM((cells + 2 * front, chans), f32),
            pltpu.VMEM((3, 6 * chans, 2 * outs), bf16),
            pltpu.VMEM((depth // 2, cells, 2 * outs), f32),
            pltpu.VMEM((depth // 2, cells // 2, outs), f32),
            pltpu.VMEM((depth // 2, rows * cols // 4, outs), f32),
        ],
        vol, before, after, kernel, work=heavy * 8,
    )


def first_backward(vol, before, after, spread, slope, keep, send, u, rows_ref, g, acc, twice):
    depth, rows, cols, chans = vol.shape
    wide = 32
    cells = rows * wide
    outs = slope.shape[2]
    rows_ref[...] = jnp.zeros_like(rows_ref)
    for p in range(depth + 2):
        if p == 0:
            source = before[0]
        elif p == depth + 1:
            source = after[0]
        else:
            source = vol[p - 1]
        wide_plane(source, rows_ref, u.at[p], 0, wide)
    edge = jnp.zeros((depth, wide, outs), bf16)
    g[:, 0:wide, :] = edge
    g[:, wide + cells :, :] = edge
    for d in range(depth):
        if d % 2 == 0:
            values = spread[d // 2] * 0.125
            twice[pl.ds(0, cells // 4, stride=2), :] = values
            twice[pl.ds(1, cells // 4, stride=2), :] = values
        for h in range(rows):
            some = twice[(h // 2) * wide : (h // 2 + 1) * wide, :] * slope[d, h * wide : (h + 1) * wide, :]
            g[d, (h + 1) * wide : (h + 2) * wide, :] = some.astype(bf16)
    started = set()
    for p in range(depth + 2):
        taps = [a for a in range(3) if 0 <= p - a < depth]
        rhs = jnp.concatenate(
            [g[p - a, (2 - b) * wide : (2 - b) * wide + cells, :] for a in taps for b in range(3)], axis=1
        )
        part = lax.dot_general(u[p], rhs, (((0,), (0,)), ((), ())), preferred_element_type=f32)
        for place, a in enumerate(taps):
            block = part[:, place * 3 * outs : (place + 1) * 3 * outs]
            lanes = slice(a * 3 * outs, (a + 1) * 3 * outs)
            if a in started:
                acc[:, lanes] += block
            else:
                acc[:, lanes] = block
                started.add(a)
    length = keep.shape[0]

    def write(first, second):
        for a in range(3):
            for b in range(3):
                for e in range(3):
                    top = (9 * a + 3 * b + e) * chans
                    lanes = slice((3 * a + b) * outs, (3 * a + b + 1) * outs)
                    cut = min(max(length - top, 0), chans)
                    if cut > 0:
                        first[top : top + cut, :] = acc[e * chans : e * chans + cut, lanes]
                    if cut < chans:
                        low = top + cut - length
                        second[low : low + chans - cut, :] = acc[e * chans + cut : (e + 1) * chans, lanes]

    @pl.when(lax.axis_index("rep") == 0)
    def _():
        write(keep, send)

    @pl.when(lax.axis_index("rep") != 0)
    def _():
        write(send, keep)


def run_first_backward(vol, before, after, spread, slope):
    depth, rows, cols, chans = vol.shape
    wide, outs = 32, slope.shape[2]
    cells = rows * wide
    return call(
        first_backward,
        (jax.ShapeDtypeStruct((27 * chans // 2, outs), f32),) * 2,
        [
            pltpu.VMEM((depth + 2, cells, 3 * chans), bf16),
            pltpu.VMEM((cells + 2 * front, chans), f32),
            pltpu.VMEM((depth, cells + 2 * wide, outs), bf16),
            pltpu.VMEM((3 * chans, 9 * outs), f32),
            pltpu.VMEM((cells // 2, outs), f32),
        ],
        vol, before, after, spread, slope, work=heavy * 7,
    )


def positions():
    place = lax.axis_index("space")
    copy = 2 * lax.axis_index("dp") + lax.axis_index("rep")
    return [(place + 4 - k) % 4 for k in range(4)] + [copy ^ k for k in range(4)]


def lay_pooled(parts, places, flat, rows_ref, target, top, side, wide):
    chans = target.shape[2] // 3
    cells = side * wide
    for part, place in zip(parts, places):
        for d in range(part.shape[0]):
            flat[...] = part[d].astype(f32)
            for h in range(side):
                rows_ref[front + h * wide : front + h * wide + side, :] = flat[h * side : (h + 1) * side, :]
            for e in range(3):
                target[place + d, top : top + cells, e * chans : (e + 1) * chans] = shifted(
                    rows_ref, cells, e - 1
                ).astype(bf16)


def second_layer(
    p0, p1, p2, p3, w0, w1, w2, w3, w4, head, wanted,
    pooled_grad, own, result, p, flat, rows_ref, w, acc, slopes, shift_ref, g,
):
    parts, pieces = (p0, p1, p2, p3), (w1, w2, w3, w4)
    where = positions()
    planes, area, chans = p0.shape
    side, wide = 12, 16
    cells = side * wide
    depth = planes * len(parts)
    outs = w.shape[0]
    rows_ref[...] = jnp.zeros_like(rows_ref)
    p[0] = jnp.zeros(p.shape[1:], bf16)
    p[depth + 1] = jnp.zeros(p.shape[1:], bf16)
    edge = jnp.zeros((depth + 2, wide, 3 * chans), bf16)
    p[:, 0:wide, :] = edge
    p[:, wide + cells :, :] = edge
    lay_pooled(parts, [1 + planes * where[k] for k in range(4)], flat, rows_ref, p, wide, side, wide)
    share = w0.shape[0]
    quarter = share // 4
    w[0:share, :] = w0[...]
    for k in range(1, 4):
        for j in range(4):
            at = pl.multiple_of(k * share + where[4 + j] * quarter, quarter)
            w[pl.ds(at, quarter), :] = pieces[j][(k - 1) * quarter : k * quarter, :]
    column = lax.broadcasted_iota(jnp.int32, (cells, outs), 0) % wide
    inside = column < side
    step = depth // 2
    slopes[0] = jnp.zeros((cells, outs), f32)
    slopes[depth + 1] = jnp.zeros((cells, outs), f32)

    def half(t, total):
        for a in range(3):
            lhs = jnp.concatenate(
                [
                    p[pl.ds(t * step + a, step), b * wide : b * wide + cells, :].reshape(step * cells, 3 * chans)
                    for b in range(3)
                ],
                axis=1,
            )
            part = lax.dot_general(
                lhs, w[:, 9 * a * chans : 9 * (a + 1) * chans], (((1,), (1,)), ((), ())), preferred_element_type=f32
            )
            if a == 0:
                acc[...] = part
            else:
                acc[...] += part
        for d in range(step):
            slope, value = slope_and_activation(acc[d * cells : (d + 1) * cells, :])
            slopes[t * step + d + 1] = jnp.where(inside, slope, 0.0)
            value = jnp.where(inside, value, 0.0)
            total = total + value.reshape(cells // 8, 8, outs).sum(axis=0)
        return total

    total = lax.fori_loop(0, 2, half, jnp.zeros((8, outs), f32))
    feature = total.sum(axis=0, keepdims=True) / float(depth * area)
    natural = [head[:, k * share : (k + 1) * share] for k in range(4)]
    turned = []
    for k in range(4):
        block = natural[0]
        for j in range(1, 4):
            block = jnp.where(where[k] == j, natural[j], block)
        turned.append(block)
    head = jnp.concatenate(turned, axis=1)
    count = head.shape[0]
    predicted = jnp.sum(feature * head, axis=1, keepdims=True)
    row = lax.broadcasted_iota(jnp.int32, (count, 1), 0)
    target = jnp.zeros((count, 1), f32)
    for k in range(count):
        target = jnp.where(row == k, wanted[0, k], target)
    error = predicted - target
    result[...] = error * feature
    scale = jnp.sum(head * error, axis=0, keepdims=True)
    shift_ref[...] = jnp.zeros_like(shift_ref)
    rim = jnp.zeros((planes + 2, wide, outs), bf16)
    for e in range(3):
        g[e, :, 0:wide, :] = rim
        g[e, :, wide + cells :, :] = rim
    for k in range(planes + 2):
        shift_ref[front : front + cells, :] = (slopes[where[0] * planes + k] * scale).astype(bf16).astype(f32)
        for e in range(3):
            g[e, k, wide : wide + cells, :] = shifted(shift_ref, cells, 1 - e).astype(bf16)
    out = None
    for a in range(3):
        taps = [(b, e) for b in range(3) for e in range(3)]
        lhs = jnp.concatenate(
            [
                g[e, 2 - a : 2 - a + planes, (2 - b) * wide : (2 - b) * wide + cells, :].reshape(planes * cells, outs)
                for b, e in taps
            ],
            axis=1,
        )
        rhs = jnp.concatenate(
            [w[:, (9 * a + 3 * b + e) * chans : (9 * a + 3 * b + e + 1) * chans] for b, e in taps], axis=0
        )
        part = jnp.dot(lhs, rhs, preferred_element_type=f32)
        out = part if out is None else out + part
    keep = lax.broadcasted_iota(jnp.int32, (planes * cells, chans), 0) % wide < side
    pooled_grad[...] = jnp.where(keep, out, 0.0).reshape(planes, cells, chans)
    for d in range(depth):
        own[d] = (slopes[d + 1, :, 0:share] * scale[:, 0:share]).astype(bf16)


def run_second_layer(parts, part_kernel, pieces, head, wanted):
    planes, area, chans = parts[0].shape
    side, wide = 12, 16
    cells = side * wide
    depth = planes * 4
    share, taps = part_kernel.shape
    outs = 4 * share
    return call(
        second_layer,
        (
            jax.ShapeDtypeStruct((planes, cells, chans), f32),
            jax.ShapeDtypeStruct((depth, cells, share), bf16),
            jax.ShapeDtypeStruct((head.shape[0], outs), f32),
        ),
        [
            pltpu.VMEM((depth + 2, cells + 2 * wide, 3 * chans), bf16),
            pltpu.VMEM((area, chans), f32),
            pltpu.VMEM((cells + 2 * front, chans), f32),
            pltpu.VMEM((outs, taps), bf16),
            pltpu.VMEM((depth // 2 * cells, outs), f32),
            pltpu.VMEM((depth + 2, cells, outs), f32),
            pltpu.VMEM((cells + 2 * front, outs), f32),
            pltpu.VMEM((3, planes + 2, cells + 2 * wide, outs), bf16),
        ],
        *parts, part_kernel, *pieces, head, wanted, smem=(10,), work=heavy * 8,
    )


def second_backward(p0, p1, p2, p3, own, result, keep, send, p, flat, rows_ref, g, grad):
    parts = (p0, p1, p2, p3)
    where = positions()
    planes, area, chans = p0.shape
    side, wide = 12, 16
    cells = side * wide
    depth = planes * len(parts)
    share = own.shape[2]
    rows_ref[...] = jnp.zeros_like(rows_ref)
    p[0] = jnp.zeros(p.shape[1:], bf16)
    p[depth + 1] = jnp.zeros(p.shape[1:], bf16)
    lay_pooled(parts, [1 + planes * where[k] for k in range(4)], flat, rows_ref, p, 0, side, wide)
    none = jnp.zeros((depth, wide, share), bf16)
    for b in range(3):
        lanes = slice(b * share, (b + 1) * share)
        if b == 0:
            g[:, 0 : cells - wide, lanes] = own[:, wide:cells, :]
            g[:, cells - wide :, lanes] = none
        elif b == 1:
            g[:, :, lanes] = own[...]
        else:
            g[:, wide:, lanes] = own[:, 0 : cells - wide, :]
            g[:, 0:wide, lanes] = none
    rhs = g[...].reshape(depth * cells, 3 * share)
    for a in range(3):
        lhs = p[a : a + depth].reshape(depth * cells, 3 * chans)
        part = lax.dot_general(rhs, lhs, (((0,), (0,)), ((), ())), preferred_element_type=f32)
        for b in range(3):
            for e in range(3):
                t = 9 * a + 3 * b + e
                block = part[b * share : (b + 1) * share, e * chans : (e + 1) * chans]
                grad[t * share : (t + 1) * share, :] = block
    grad[27 * share :, :] = jnp.zeros((16, chans), f32)
    grad[27 * share : 27 * share + result.shape[0], :] = result[:, 0:chans]
    half = keep.shape[0]
    low = pl.multiple_of(lax.axis_index("rep") * half, 8)
    keep[...] = grad[pl.ds(low, half), :]
    send[...] = grad[pl.ds(pl.multiple_of(half - low, 8), half), :]


def run_second_backward(parts, own, result):
    planes, area, chans = parts[0].shape
    depth, cells, share = own.shape
    return call(
        second_backward,
        (jax.ShapeDtypeStruct((27 * share // 2 + 8, chans), f32),) * 2,
        [
            pltpu.VMEM((depth + 2, cells, 3 * chans), bf16),
            pltpu.VMEM((area, chans), f32),
            pltpu.VMEM((cells + 2 * front, chans), f32),
            pltpu.VMEM((depth, cells, 3 * share), bf16),
            pltpu.VMEM((27 * share + 16, chans), f32),
        ],
        *parts, own, result, work=heavy * 4,
    )


def entry(vol, first, last):
    first[0] = vol[0]
    last[0] = vol[vol.shape[0] - 1]


def run_entry(vol):
    plane = jax.ShapeDtypeStruct((1,) + vol.shape[1:], bf16)
    return call(entry, (plane, plane), [], vol)


def widen(x, across, near, far, out, room, done):
    rows = x.shape[0]
    own = 2 * lax.axis_index("rep") + lax.axis_index("dp")
    copies = []
    for k, part in enumerate((x, across, near, far)):
        room[k] = part[...].astype(f32)
        to = out.at[pl.ds(pl.multiple_of((own ^ k) * rows, 8), rows)]
        copies.append(pltpu.make_async_copy(room.at[k], to, done.at[k]))
        copies[-1].start()
    for copy in copies:
        copy.wait()


def run_widen(x, across, near, far):
    rows, cols = x.shape
    return call(
        widen,
        jax.ShapeDtypeStruct((4 * rows, cols), f32),
        [pltpu.VMEM((4, rows, cols), f32), pltpu.SemaphoreType.DMA((4,))],
        x, across, near, far, far_outs=(0,),
    )


def join(r0, r1, r2, out):
    rows = r0.shape[0]
    for k, r in enumerate((r0, r1, r2)):
        out[k * rows : (k + 1) * rows, :] = r[...]


def run_join(parts):
    rows, cols = parts[0].shape
    return call(join, jax.ShapeDtypeStruct((3 * rows, cols), bf16), [], *parts)


def merge_half(kept, came, keep, send):
    half = keep.shape[0]
    low = pl.multiple_of(lax.axis_index("dp") * half, 8)
    high = pl.multiple_of(half - low, 8)
    keep[...] = kept[pl.ds(low, half), :] + came[pl.ds(low, half), :]
    send[...] = (kept[pl.ds(high, half), :] + came[pl.ds(high, half), :]).astype(bf16)


def run_merge_half(kept, came):
    rows, cols = kept.shape
    outs = tuple(jax.ShapeDtypeStruct((rows // 2, cols), kind) for kind in (f32, bf16))
    return call(merge_half, outs, [], kept, came)


def merge_blocks(kept, came, keep, s1, s2, s3):
    size = keep.shape[0]

    def block(step):
        low = pl.multiple_of((lax.axis_index("space") + step) % 4 * size, 8)
        return kept[pl.ds(low, size), :] + came[pl.ds(low, size), :].astype(f32)

    keep[...] = block(0)
    for step, send in ((1, s1), (2, s2), (3, s3)):
        send[...] = block(step).astype(bf16)


def run_merge_blocks(kept, came):
    rows, cols = kept.shape
    outs = tuple(jax.ShapeDtypeStruct((rows // 4, cols), kind) for kind in (f32, bf16, bf16, bf16))
    return call(merge_blocks, outs, [], kept, came)


def spread_second(packed, out, head):
    chans = packed.shape[1]
    share = out.shape[0]
    for t in range(27):
        out[:, t * chans : (t + 1) * chans] = packed[t * share : (t + 1) * share, :]
    head[...] = packed[27 * share : 27 * share + head.shape[0], 0:share]


def run_spread_second(packed, share, outs):
    rows, chans = packed.shape
    return call(
        spread_second,
        (jax.ShapeDtypeStruct((share, 27 * chans), f32), jax.ShapeDtypeStruct((outs, share), f32)),
        [],
        packed,
        work=heavy * 2,
    )


def turn(x, axis, step):
    size = lax.axis_size(axis)
    return lax.ppermute(x, axis, [(i, (i + step) % size) for i in range(size)])


def paired(x, axis, bits):
    return lax.ppermute(x, axis, [(i, i ^ bits) for i in range(lax.axis_size(axis))])


def direct(axis):
    return lax.axis_size(axis) <= direct_most


def gathered(x, axis):
    if not direct(axis):
        return lax.all_gather(x, axis)
    size, place = lax.axis_size(axis), lax.axis_index(axis)
    parts = [x] + [turn(x, axis, step) for step in range(1, size)]
    out = jnp.zeros((size,) + x.shape, x.dtype)
    for step, part in enumerate(parts):
        out = lax.dynamic_update_index_in_dim(out, part, (place - step) % size, 0)
    return out


def scattered_sum(x, axis, wire):
    size, place = lax.axis_size(axis), lax.axis_index(axis)
    blocks = x.reshape((size, x.shape[0] // size) + x.shape[1:])
    if not direct(axis):
        return lax.psum_scatter(blocks, axis)
    total = lax.dynamic_index_in_dim(blocks, place, 0, False)
    for step in range(1, size):
        sent = lax.dynamic_index_in_dim(blocks, (place + step) % size, 0, False).astype(wire)
        total = total + turn(sent, axis, step).astype(jnp.float32)
    return total


def total_first(x):
    columns = x.shape[1]
    x = scattered_sum(x, "rep", jnp.float32)
    x = scattered_sum(x, "dp", jnp.bfloat16)
    if direct("space"):
        x = scattered_sum(x, "space", jnp.bfloat16).astype(jnp.bfloat16)
        x = gathered(x, "space").reshape(-1, columns)
    else:
        x = lax.psum(x, "space").astype(jnp.bfloat16)
    x = gathered(x, "dp").reshape(-1, columns)
    x = gathered(x, "rep").reshape(-1, columns)
    return x.astype(jnp.float32)


def total_second(x):
    columns = x.shape[1]
    x = scattered_sum(x, "rep", jnp.float32)
    if direct("dp"):
        x = gathered(x, "dp").sum(0)
    else:
        x = lax.psum(x, "dp")
    return gathered(x, "rep").reshape(-1, columns)


def whole_kernel(part):
    rows, share = part.shape
    copies = [axis for axis in ("dp", "rep")]
    pieces, place = (1, 0)
    for axis in copies:
        place = place * lax.axis_size(axis) + lax.axis_index(axis)
        pieces = pieces * lax.axis_size(axis)
    length = rows // pieces
    piece = lax.dynamic_slice_in_dim(part, place * length, length, 0)
    packed = jnp.concatenate([piece[: length // 2], piece[length // 2 :]], axis=1)
    packs = gathered(packed, "space")
    upper = jnp.moveaxis(packs[:, :, :share], 0, 1).reshape(length // 2, -1)
    lower = jnp.moveaxis(packs[:, :, share:], 0, 1).reshape(length // 2, -1)
    wide = jnp.concatenate([upper, lower], axis=0)
    wide = gathered(wide, "dp")
    wide = jnp.moveaxis(gathered(wide, "rep"), 0, 1)
    return wide.reshape(rows, -1)


def extended_2(x, sides, width):
    for axis, dim in sides:
        devices, length = (lax.axis_size(axis), x.shape[dim])
        up = [(i, (i + 1) % devices) for i in range(devices - 1)]
        down = [(j, i) for i, j in up]
        last = lax.slice_in_dim(x, length - width, length, axis=dim)
        leading = lax.slice_in_dim(x, 0, width, axis=dim)
        before = lax.ppermute(last, axis, up)
        after = lax.ppermute(leading, axis, down)
        x = jnp.concatenate([before, x, after], axis=dim)
    return x


def activate(value):
    return leak_slope * value + (1.0 - leak_slope) * (jax.nn.softplus(value) - log_two)


def activate_slope(value):
    return leak_slope + (1.0 - leak_slope) * jax.nn.sigmoid(value)


def convolve(extended, kernel):
    result = lax.conv_general_dilated(
        extended[None],
        kernel,
        (1, 1, 1),
        [(0, 0), (1, 1), (1, 1)],
        dimension_numbers=("NDHWC", "DHWIO", "NDHWC"),
        preferred_element_type=jnp.float32,
    )
    return result[0]


def pooling(grid):
    depth, rows, cols, chans = grid.shape
    return grid.reshape(depth // 2, 2, rows // 2, 2, cols // 2, 2, chans).mean(axis=(1, 3, 5))


def expand(grid):
    depth, rows, cols, chans = grid.shape
    spread = jnp.broadcast_to(
        grid[:, None, :, None, :, None, :], (depth, 2, rows, 2, cols, 2, chans)
    )
    return spread.reshape(depth * 2, rows * 2, cols * 2, chans) / 8.0


def kernel_grad(extended, grad):
    widened = jnp.pad(extended, ((0, 0), (1, 1), (1, 1), (0, 0)))
    result = lax.conv_general_dilated(
        widened[..., None],
        grad[:, :, :, None, :],
        (1, 1, 1),
        "VALID",
        dimension_numbers=("DHWNC", "DHWIO", "NDHWC"),
        preferred_element_type=jnp.float32,
    )
    return jnp.transpose(result, (1, 2, 3, 0, 4)).reshape(-1, grad.shape[-1])


def general_shards(volumes, targets, first_kernel, second_kernel, head_weights):
    grid_in = volumes[0]
    target_row = targets[0]
    channels = grid_in.shape[-1]
    kernel_one = first_kernel.reshape(3, 3, 3, channels, first_kernel.shape[1])
    extended = extended_2(grid_in, (("space", 0),), 1)
    share = second_kernel.shape[1]
    place = lax.axis_index("space")
    kernel_two = whole_kernel(second_kernel).reshape(3, 3, 3, channels, -1)
    before_one = convolve(extended, kernel_one)
    pooled = pooling(activate(before_one)).astype(jnp.bfloat16)
    whole = gathered(pooled, "space").reshape((-1,) + pooled.shape[1:])
    padded_whole = jnp.pad(whole, ((1, 1), (0, 0), (0, 0), (0, 0)))
    before_two = convolve(padded_whole, kernel_two)
    feature = jnp.mean(activate(before_two), axis=(0, 1, 2))
    predicted = jnp.dot(feature, head_weights, precision=lax.Precision.HIGHEST)
    error = predicted - target_row
    feature_part = lax.dynamic_slice_in_dim(feature, place * share, share, 0)
    head_grad = feature_part[:, None] * error[None, :]
    feature_grad = jnp.dot(head_weights, error, precision=lax.Precision.HIGHEST)
    grad_two = (feature_grad * activate_slope(before_two)).astype(jnp.bfloat16)
    padded_grad = jnp.pad(grad_two, ((1, 1), (0, 0), (0, 0), (0, 0)))
    flipped = jnp.swapaxes(kernel_two[::-1, ::-1, ::-1], 3, 4)
    planes = pooled.shape[0]
    window = lax.dynamic_slice_in_dim(padded_grad, place * planes, planes + 2, 0)
    pooled_grad = convolve(window, flipped)
    grad_one = (expand(pooled_grad) * activate_slope(before_one)).astype(jnp.bfloat16)
    first_total = total_first(kernel_grad(extended, grad_one))
    grad_part = lax.dynamic_slice_in_dim(grad_two, place * share, share, 3)
    second_part = kernel_grad(padded_whole, grad_part)
    rows = second_part.shape[0]
    packed = jnp.concatenate([second_part[: rows // 2], second_part[rows // 2 :]], axis=1)
    packed = total_second(packed)
    second_total = jnp.concatenate([packed[:, :share], packed[:, share:]], axis=0)
    head_total = gathered(gathered(head_grad, "rep").sum(0), "dp").sum(0)
    return (first_total, second_total, head_total)


def neighbours(first, last):
    devices = lax.axis_size("space")
    up = [(i, i + 1) for i in range(devices - 1)]
    down = [(j, i) for i, j in up]
    before = lax.ppermute(last, "space", up)
    after = lax.ppermute(first, "space", down)
    return before, after


def shards(volumes, targets, first_kernel, second_kernel, head_weights):
    sizes = tuple(lax.axis_size(axis) for axis in ("space", "dp", "rep"))
    if sizes != (4, 2, 2):
        return general_shards(volumes, targets, first_kernel, second_kernel, head_weights)
    grid = volumes[0]
    share = second_kernel.shape[1]
    outs = head_weights.shape[1]
    place = lax.axis_index("space")
    turned = second_kernel.T
    before, after = neighbours(grid[:1], grid[-1:])
    copy = 2 * lax.axis_index("dp") + lax.axis_index("rep")
    piece = lax.dynamic_slice_in_dim(turned, copy * (share // 4), share // 4, 0)
    others = [turn(piece, "space", k) for k in range(1, 4)]
    pooled, slope = run_first_forward(grid, before, after, first_kernel)
    pooled, *others = lax.optimization_barrier([pooled] + others)
    others = run_join(others)
    across = turn(others, "dp", 1)
    parts = [pooled] + [turn(pooled, "space", k) for k in range(1, 4)]
    across, *parts = lax.optimization_barrier([across] + parts)
    pieces = [others, turn(others, "rep", 1), across, turn(across, "rep", 1)]
    pooled_grad, own, result = run_second_layer(parts, turned, pieces, head_weights.T, targets)
    keep, send = run_first_backward(grid, before, after, pooled_grad, slope)
    keep, send = run_merge_half(keep, turn(send, "rep", 1))
    arrived = turn(send, "dp", 1)
    kept, sent = run_second_backward(parts, own, result)
    x, *sends = run_merge_blocks(keep, arrived)
    second = kept + turn(sent, "rep", 1)
    *sends, second = lax.optimization_barrier((*sends, second))
    for k in (1, 3, 2):
        x = x + turn(sends[k - 1], "space", k).astype(f32)
    x = x.astype(bf16)
    second = second + turn(second, "dp", 1)
    whole = jnp.zeros((4,) + x.shape, bf16)
    for k in (0, 1, 3, 2):
        part = turn(x, "space", k) if k else x
        if k == 1:
            part, second = lax.optimization_barrier((part, second))
        whole = lax.dynamic_update_index_in_dim(whole, part, (place - k) % 4, 0)
    x = whole.reshape(-1, x.shape[1])
    second = gathered(second, "rep").reshape(-1, second.shape[1])
    second_total, head_total = run_spread_second(second, share, outs)
    across_x = turn(x, "dp", 1)
    near = turn(x, "rep", 1)
    across_x, near, second_total, head_total = lax.optimization_barrier((across_x, near, second_total, head_total))
    far = turn(across_x, "rep", 1)
    first_total = run_widen(x, across_x, near, far)
    return (first_total, second_total.T, head_total.T)


def solution(mesh):
    in_specs = (
        P(("groups", "dp", "rep"), "space", None, None, None),
        P(("groups", "dp", "rep"), None),
        P(),
        P(None, "space"),
        P(),
    )
    out_specs = (P("groups", None), P("groups", "space"), P(("groups", "space"), None))
    return jax.shard_map(shards, mesh=mesh, in_specs=in_specs, out_specs=out_specs, check_vma=False)
```
